256 devices in a mesh: tm: 128 (over z, y, x), rhs: 2 (over core).
Axes of the slice: x: 4, y: 4, z: 8, core: 2. Of those that a mesh axis runs over, the one named last changes fastest.
Arguments:
- diag: float32 [262144, 512], P('tm', 'rhs'), as said below
- lower: float32 [262144, 512], P('tm', 'rhs'), as said below
- right_side: float32 [128, 262144], P('rhs', 'tm'), may hold values from -6 to 6
- coarse_sol: float32 [128, 65536], P('rhs', 'tm'), may hold values from -6 to 6
Outputs:
- coarse_diag: float32 [65536, 512], P('tm', 'rhs')
- coarse_lower: float32 [65536, 512], P('tm', 'rhs')
- coarse_rhs: float32 [128, 65536], P('rhs', 'tm')
- solution: float32 [128, 262144], P('rhs', 'tm')
The draws below stay inside these ranges and needn't reach their ends.
Inputs may be any that keep to these rules, and one draw needn't show every extreme that they name: diag and lower are the diagonal and coupling blocks of a symmetric positive definite periodic block tridiagonal matrix whose eigenvalues are all at least 2; every diagonal block is symmetric. lower holds the coupling blocks of the matrix described for diag.
All inputs are finite; a program needn't handle non-finite values.
Results may differ from the reference program's by a relative error of at most 0.0003.
Values sent between devices are 32-bit elements; how exact they have to be, the bound alone decides.
A program may use at most 128 MiB of HBM per device.

```python
import math
import jax
import jax.numpy as jnp
from jax import lax

BLOCK = 512
RHS = 128
SECTIONS = 512
COARSE = 128


leading_gain = 4.0


trailing_gain = 1.2


def factor_pair(key):
    first_key = jax.random.fold_in(key, 7001)
    second_key = jax.random.fold_in(key, 7002)
    scale_root = math.sqrt(BLOCK)
    leading = jax.random.normal(first_key, (SECTIONS, BLOCK, BLOCK), jnp.float32) * (leading_gain / scale_root)
    trailing = jax.random.normal(second_key, (SECTIONS, BLOCK, BLOCK), jnp.float32) * (trailing_gain / scale_root)
    return (leading, trailing)


def draw_diag(key, part):
    leading, trailing = factor_pair(key)
    shifted = jnp.roll(trailing, -1, axis=0)
    gram_matrix = jnp.einsum('kab,kac->kbc', leading, leading, precision=lax.Precision.HIGHEST)
    gram_matrix = gram_matrix + jnp.einsum('kab,kac->kbc', shifted, shifted, precision=lax.Precision.HIGHEST)
    gram_matrix = 0.5 * (gram_matrix + jnp.swapaxes(gram_matrix, 1, 2))
    gram_matrix = gram_matrix + 2.0 * jnp.eye(BLOCK, dtype=jnp.float32)
    return gram_matrix.reshape(SECTIONS * BLOCK, BLOCK)


def draw_lower(key, part):
    leading, trailing = factor_pair(key)
    coupling = jnp.einsum('kab,kac->kbc', leading, trailing, precision=lax.Precision.HIGHEST)
    return coupling.reshape(SECTIONS * BLOCK, BLOCK)


def shard_levels(own_key, dims, cuts, low, top_value):
    level, own = 1.0, jax.random.fold_in(own_key, 6)
    for position, parts in cuts:
        heights = jnp.exp(jax.random.uniform(jax.random.fold_in(own, position), (parts,), jnp.float32, low / len(cuts), top_value / len(cuts)))
        level = level * jnp.repeat(heights, dims[position] // parts).reshape([-1 if axis == position else 1 for axis in range(len(dims))])
    return level


def normal_values(rng, dims, deviation, limit, cuts=(), held_as=jnp.bfloat16):
    drawn = jax.random.normal(rng, dims, jnp.float32) * deviation
    if len(cuts) > 0:
        drawn = shard_levels(rng, dims, cuts, -0.22, 0.18) * drawn
    return jnp.clip(drawn, min=-limit, max=limit).astype(held_as)


def setup_inputs(seed: int = 0) -> dict:
    splits = jax.random.split(jax.random.key(seed), 5)
    diag = draw_diag(jax.random.fold_in(splits[4], 71), 0)
    lower = draw_lower(jax.random.fold_in(splits[4], 71), 0)
    right_side = normal_values(splits[2], (RHS, SECTIONS * BLOCK), 1.0, 6.0, ((0, 2), (1, 128)), jnp.float32)
    coarse_sol = normal_values(splits[3], (RHS, COARSE * BLOCK), 1.0, 6.0, ((0, 2), (1, 128)), jnp.float32)
    return {"diag": diag, "lower": lower, "right_side": right_side, "coarse_sol": coarse_sol}


def product(first_term, second_term):
    return jnp.matmul(first_term, second_term, precision=lax.Precision.HIGHEST)

def transposed(matrix):
    return jnp.swapaxes(matrix, 1, 2)

def eliminate(diag_blocks, link_blocks, rhs_blocks):
    kept_diag = diag_blocks[0::2]
    gone_diag = diag_blocks[1::2]
    kept_link = link_blocks[0::2]
    gone_link = link_blocks[1::2]
    kept_rhs = rhs_blocks[0::2]
    gone_rhs = rhs_blocks[1::2]
    following = jnp.roll(kept_link, -1, axis=0)
    block_order = diag_blocks.shape[1]
    solved = jnp.linalg.solve(gone_diag, jnp.concatenate([gone_link, transposed(following), gone_rhs], axis=2))
    toward_prev = solved[:, :, :block_order]
    toward_next = solved[:, :, block_order:2 * block_order]
    own_part = solved[:, :, 2 * block_order:]
    updated_diagonal = kept_diag - product(transposed(gone_link), toward_prev) - product(kept_link, jnp.roll(toward_next, 1, axis=0))
    new_rhs = kept_rhs - product(transposed(gone_link), own_part) - product(kept_link, jnp.roll(own_part, 1, axis=0))
    updated_coupling = -product(kept_link, jnp.roll(toward_prev, 1, axis=0))
    return (updated_diagonal, updated_coupling, new_rhs, (toward_prev, toward_next, own_part))

def substitute(kept_values, pieces):
    toward_prev, toward_next, own_part = pieces
    dropped = own_part - product(toward_prev, kept_values) - product(toward_next, jnp.roll(kept_values, -1, axis=0))
    return jnp.stack([kept_values, dropped], axis=1).reshape(-1, kept_values.shape[1], kept_values.shape[2])

def reference(diag, lower, right_side, coarse_sol):
    section_diag = diag.reshape(SECTIONS, BLOCK, BLOCK)
    section_link = lower.reshape(SECTIONS, BLOCK, BLOCK)
    section_rhs = jnp.transpose(right_side).reshape(SECTIONS, BLOCK, RHS)
    first_diag, first_link, first_rhs, first_pieces = eliminate(section_diag, section_link, section_rhs)
    second_diag, second_link, second_rhs, second_pieces = eliminate(first_diag, first_link, first_rhs)
    coarse_values = jnp.transpose(coarse_sol).reshape(COARSE, BLOCK, RHS)
    middle = substitute(coarse_values, second_pieces)
    finest = substitute(middle, first_pieces)
    return (second_diag.reshape(COARSE * BLOCK, BLOCK), second_link.reshape(COARSE * BLOCK, BLOCK), jnp.transpose(second_rhs.reshape(COARSE * BLOCK, RHS)), jnp.transpose(finest.reshape(SECTIONS * BLOCK, RHS)))
```

```python
import functools

import jax
import jax.numpy as jnp
from jax import lax
from jax.experimental import pallas as pl
from jax.experimental.pallas import tpu as pltpu
from jax.sharding import PartitionSpec as P

f32, bf16 = jnp.float32, jnp.bfloat16
N = 512
HALF = 256
RHS = 128
LOWEST = 2.0
TOL = 2e-6
MAX_STEPS = 40
VMEM = pl.BlockSpec(memory_space=pltpu.VMEM)
ANY = pl.BlockSpec(memory_space=pl.ANY)
NN = (((1,), (0,)), ((), ()))
NT = (((1,), (1,)), ((), ()))


def split(x):
    high = x.astype(bf16)
    return high, (x - high.astype(f32)).astype(bf16)


def mul(a, b, dims=NN):
    one = lambda p, q: lax.dot_general(p, q, dims, preferred_element_type=f32)
    return one(a[0], b[0]) + (one(a[0], b[1]) + one(a[1], b[0]))


def identity(n):
    return (
        lax.broadcasted_iota(jnp.int32, (n, n), 0) == lax.broadcasted_iota(jnp.int32, (n, n), 1)
    ).astype(f32)


def newton(block, x_ref, d_ref):
    n = block.shape[0]
    parts = split(block)
    d_ref[0], d_ref[1] = parts
    top = jnp.maximum(jnp.max(jnp.sum(jnp.abs(block), axis=0, keepdims=True)), LOWEST)
    eye = identity(n)
    gap = (top - LOWEST) / (top + LOWEST)
    lead = 2.0 / (top + LOWEST)
    gain = 2.0 / (2.0 - gap * gap)
    x_ref[...] = (gain * lead) * (2.0 * eye - lead * block)
    gap = 0.5 * gain * gap * gap

    def more(state):
        step, gap = state
        return jnp.logical_and(gap > TOL, step < MAX_STEPS)

    def body(state):
        step, gap = state
        x = x_ref[...]
        x_parts = split(x)
        rest = split(eye - mul((d_ref[0], d_ref[1]), x_parts))
        gain = 2.0 / (2.0 - gap * gap)
        x_ref[...] = gain * (x + mul(x_parts, rest))
        return step + 1, 0.5 * gain * gap * gap

    lax.while_loop(more, body, (jnp.int32(0), gap))
    return x_ref[...]


def invert(block_ref, out_ref, x_ref, d_ref):
    first = newton(block_ref[:HALF, :HALF], x_ref, d_ref)
    cross = split(block_ref[HALF:, :HALF])
    lift = split(mul(cross, split(first)))
    out_ref[:HALF, :HALF] = first
    last = newton(block_ref[HALF:, HALF:] - mul(lift, cross, NT), x_ref, d_ref)
    low = -mul(split(last), lift)
    up = low.T
    out_ref[HALF:, HALF:] = last
    out_ref[HALF:, :HALF] = low
    out_ref[:HALF, HALF:] = up
    out_ref[:HALF, :HALF] = out_ref[:HALF, :HALF] - mul(split(up), lift)


def level_one(
    d_own, d_other, a_own, a_other, b_own, b_other, f_own, f_other, y_own, y_other,
    gv_ref, c_ref, hw_own_ref, hw_other_ref, v_ref, gzw_ref, hz_ref, w_ref,
    whole, inner, outer, x_ref, d_ref,
):
    core = lax.axis_index("rhs")
    mine = pl.multiple_of(core * HALF, HALF)
    other = pl.multiple_of(HALF - core * HALF, HALF)
    rows_mine = pl.multiple_of(core * 64, 64)
    rows_other = pl.multiple_of(64 - core * 64, 64)

    def join(own, partner):
        whole[:, pl.ds(mine, HALF)] = own
        whole[:, pl.ds(other, HALF)] = partner

    @pl.when(core == 0)
    def _():
        join(a_own[...], a_other[...])
        outer[...] = whole[...].T
        join(b_own[...], b_other[...])
        inner[...] = whole[...]

    @pl.when(core == 1)
    def _():
        join(a_own[...], a_other[...])
        inner[...] = whole[...].T
        outer[:, :HALF] = b_own[...]
        outer[:, HALF:] = b_other[...]

    join(d_own[...], d_other[...])
    invert(whole, v_ref, x_ref, d_ref)
    inverse = split(v_ref[...])
    g, h = split(inner[...]), split(outer[...])
    w_ref[pl.ds(rows_mine, 64)] = f_own[...]
    w_ref[pl.ds(rows_other, 64)] = f_other[...]

    @pl.when(core == 0)
    def _():
        hz_ref[pl.ds(rows_mine, 64)] = y_own[...]
        hz_ref[pl.ds(rows_other, 64)] = y_other[...]

    @pl.when(core == 1)
    def _():
        hz_ref[:64] = y_own[...]
        hz_ref[64:] = y_other[...]

    right = w_ref[...]
    moved = right - mul(split(hz_ref[...]), h)
    both = mul(split(jnp.concatenate([right, moved], axis=0)), inverse)
    w_ref[...] = both[RHS:]
    both = split(both)
    gzw_ref[...] = mul(both, g, NT)
    hz_ref[...] = mul((both[0][:RHS], both[1][:RHS]), h, NT)
    v = mul(inverse, g, NT)
    v_ref[...] = v
    v = split(v)
    gv_ref[...] = mul(g, v)
    c_ref[...] = -mul(h, v)
    hw = mul(h, split(mul(inverse, h, NT)))

    @pl.when(core == 0)
    def _():
        hw_own_ref[...] = hw[:, :HALF]
        hw_other_ref[...] = hw[:, HALF:]

    @pl.when(core == 1)
    def _():
        hw_own_ref[...] = hw[:, HALF:]
        hw_other_ref[...] = hw[:, :HALF]


def level_two(
    d_own, d_other, gv_own, gv_other, f_own, f_other, gzw_own, gzw_other,
    inverse_ref, zx_ref, whole, x_ref, d_ref,
):
    core = lax.axis_index("rhs")
    mine = pl.multiple_of(core * HALF, HALF)
    other = pl.multiple_of(HALF - core * HALF, HALF)
    rows_mine = pl.multiple_of(core * 64, 64)
    rows_other = pl.multiple_of(64 - core * 64, 64)
    whole[:, pl.ds(mine, HALF)] = d_own[...]
    whole[:, pl.ds(other, HALF)] = d_other[...]
    whole[...] = whole[...] - (gv_own[...] + gv_other[...])
    invert(whole, inverse_ref, x_ref, d_ref)
    for first_row in (0, RHS):
        zx_ref[pl.ds(first_row + rows_mine, 64)] = f_own[...]
        zx_ref[pl.ds(first_row + rows_other, 64)] = f_other[...]
    right = zx_ref[...] - (gzw_own[...] + gzw_other[...])
    zx_ref[...] = mul(split(right), split(inverse_ref[...]))


def survivors(
    inverse_ref, zx_ref, c_own, c_other, hw_own, hw_other, hz_own, hz_other,
    d0, f0, v_ref, w_ref,
    diag_ref, rhs_ref, out_diag_ref, out_low_ref, out_rhs_ref, x_own_ref, x_other_ref, u_ref,
    c_both, hw_both, hz_both,
):
    core = lax.axis_index("rhs")
    mine = pl.multiple_of(core * HALF, HALF)
    rows_mine = pl.multiple_of(core * 64, 64)
    rows_other = pl.multiple_of(64 - core * 64, 64)
    c_both[core] = c_own[...]
    c_both[1 - core] = c_other[...]
    hw_both[core] = hw_own[...]
    hw_both[1 - core] = hw_other[...]
    hz_both[core] = hz_own[pl.ds(rows_mine, 64)]
    hz_both[1 - core] = hz_other[pl.ds(rows_mine, 64)]
    inverse = split(inverse_ref[...])
    left, right = split(c_both[0]), split(c_both[1])
    u_left = split(mul(inverse, split(c_both[0, pl.ds(mine, HALF)]), NT))
    u_right = split(mul(inverse, split(c_both[1, pl.ds(mine, HALF)]), NT))
    out_low_ref[...] = -mul(right, u_left)
    out_diag_ref[...] = hw_both[1] + mul(right, u_right)
    diag_ref[...] = d0[...] - hw_both[0] - mul(left, u_left)
    z2 = split(zx_ref[pl.ds(rows_mine, 64)])
    out_rhs_ref[...] = hz_both[1] + mul(z2, right, NT)
    rhs_ref[...] = f0[...] - hz_both[0] - mul(z2, left, NT)
    x2 = zx_ref[RHS:]
    w_ref_new = w_ref[...] - mul(split(x2), split(v_ref[...]), NT)
    x_own_ref[...] = w_ref_new
    u_ref[...] = zx_ref[pl.ds(RHS + rows_mine, 64)]
    x_other_ref[...] = x_own_ref[pl.ds(rows_other, 64)]


def shape(*dims):
    return jax.ShapeDtypeStruct(dims, f32)


def local(body, outs, scratch, flops, args):
    size = sum(a.size for a in args) + sum(o.size for o in outs)
    return pl.pallas_call(
        body,
        out_shape=outs,
        in_specs=[VMEM] * len(args),
        out_specs=[VMEM] * len(outs),
        scratch_shapes=scratch,
        compiler_params=pltpu.CompilerParams(vmem_limit_bytes=56 << 20),
        cost_estimate=pl.CostEstimate(flops=flops, bytes_accessed=4 * size, transcendentals=0),
    )(*args)


def newton_scratch():
    return [pltpu.VMEM((HALF, HALF), f32), pltpu.VMEM((2, HALF, HALF), bf16)]


def exchange_body(windows, count, *refs):
    sources, targets = refs[:count], refs[count : count + len(windows)]
    send, recv = refs[count + len(windows) :]
    core = lax.axis_index("rhs")
    partner = {"rhs": 1 - core}
    barrier = pltpu.get_barrier_semaphore()
    pl.semaphore_signal(barrier, inc=1, device_id=partner, device_id_type=pl.DeviceIdType.MESH)
    pl.semaphore_wait(barrier, 1)
    copies = []
    for index, (source, window) in enumerate(windows):
        copies.append(
            pltpu.make_async_remote_copy(
                src_ref=window(sources[source], core),
                dst_ref=targets[index],
                send_sem=send.at[index],
                recv_sem=recv.at[index],
                device_id=partner,
                device_id_type=pl.DeviceIdType.MESH,
            )
        )
        copies[-1].start()
    for copy in copies:
        copy.wait()


def exchange(arrays, windows, outs, collective_id):
    return pl.pallas_call(
        functools.partial(exchange_body, windows, len(arrays)),
        out_shape=outs,
        in_specs=[ANY] * len(arrays),
        out_specs=[ANY] * len(outs),
        scratch_shapes=[pltpu.SemaphoreType.DMA((len(windows),))] * 2,
        compiler_params=pltpu.CompilerParams(collective_id=collective_id, has_side_effects=True),
    )(*arrays)


def rows_of(first, second):
    return lambda ref, core: ref.at[pl.ds(pl.multiple_of(first + core * (second - first), N), N)]


def columns_of(first, second):
    return lambda ref, core: ref.at[:, pl.ds(pl.multiple_of(first + core * (second - first), N), N)]


def all_of(ref, core):
    return ref


def shards(diag, lower, right_side, coarse_sol):
    core = lax.axis_index("rhs")
    runs = lax.axis_size("tm")
    back = lambda source: [
        (2 * ((i + 1) % runs) + source, 2 * i + 1) for i in range(runs)
    ]
    both = ("tm", "rhs")
    next_left, next_right = (lax.ppermute(lower[:N], both, back(source)) for source in (0, 1))
    later_left, later_right = (lax.ppermute(coarse_sol, both, back(source)) for source in (0, 1))

    d_other, a_other, b_part, d2_other, f_other, f2_other, y_part = exchange(
        (diag, lower, right_side, coarse_sol),
        (
            (0, rows_of(3 * N, N)),
            (1, rows_of(3 * N, N)),
            (1, rows_of(2 * N, 2 * N)),
            (0, rows_of(2 * N, 2 * N)),
            (2, columns_of(3 * N, N)),
            (2, columns_of(2 * N, 2 * N)),
            (3, all_of),
        ),
        [shape(N, HALF)] * 4 + [shape(64, N)] * 3,
        1,
    )
    own_rows = lambda array, first, second: lax.dynamic_slice_in_dim(
        array, first + core * (second - first), N, 0
    )
    d_own, a_own = own_rows(diag, N, 3 * N), own_rows(lower, N, 3 * N)
    f_own = lax.dynamic_slice_in_dim(right_side, N + core * 2 * N, N, 1)
    b_own = jnp.where(core == 0, lower[2 * N : 3 * N], next_left)
    b_other = jnp.where(core == 0, b_part, next_right)
    y_own = jnp.where(core == 0, coarse_sol, later_left)
    y_other = jnp.where(core == 0, y_part, later_right)
    gv, c, hw_own, hw_send, v, gzw, hz, w = local(
        level_one,
        [shape(N, N), shape(N, N), shape(N, HALF), shape(N, HALF), shape(N, N),
         shape(2 * RHS, N), shape(RHS, N), shape(RHS, N)],
        [pltpu.VMEM((N, N), f32)] * 3 + newton_scratch(),
        2 * N**3 * 24,
        (d_own, d_other, a_own, a_other, b_own, b_other, f_own, f_other, y_own, y_other),
    )
    gv_other, gzw_other = exchange(
        (gv, gzw), ((0, all_of), (1, all_of)), [shape(N, N), shape(2 * RHS, N)], 2
    )
    swap = lambda x: lax.ppermute(x, "rhs", [(0, 1), (1, 0)])
    c_other, hw_other, hz_other = swap(c), swap(hw_send), swap(hz)
    inverse, zx = local(
        level_two,
        [shape(N, N), shape(2 * RHS, N)],
        [pltpu.VMEM((N, N), f32)] + newton_scratch(),
        2 * N**3 * 24,
        (diag[2 * N : 3 * N], d2_other, gv, gv_other,
         right_side[:, 2 * N : 3 * N], f2_other, gzw, gzw_other),
    )
    diag_part, rhs_part, out_diag, out_low, out_rhs, x_own, x_send, u = local(
        survivors,
        [shape(N, HALF), shape(64, N), shape(N, HALF), shape(N, HALF), shape(64, N),
         shape(RHS, N), shape(64, N), shape(64, N)],
        [pltpu.VMEM((2, N, N), f32), pltpu.VMEM((2, N, HALF), f32), pltpu.VMEM((2, 64, N), f32)],
        2 * N**3 * 9,
        (inverse, zx, c, c_other, hw_own, hw_other, hz, hz_other,
         diag[:N], right_side[:, :N], v, w),
    )
    forward = lambda x: lax.ppermute(x, "tm", [(i, (i + 1) % runs) for i in range(runs)])
    coarse_lower, came_diag, came_rhs = forward(out_low), forward(out_diag), forward(out_rhs)
    x_other = swap(x_send)
    x_mine = lax.dynamic_slice_in_dim(x_own, core * 64, 64, 0)
    first = jnp.where(core == 0, x_mine, x_other)
    third = jnp.where(core == 0, x_other, x_mine)
    solution = jnp.concatenate([coarse_sol, first, u, third], axis=1)
    return diag_part - came_diag, coarse_lower, rhs_part - came_rhs, solution


def solution(mesh):
    return jax.shard_map(
        shards,
        mesh=mesh,
        in_specs=(P("tm", "rhs"), P("tm", "rhs"), P("rhs", "tm"), P("rhs", "tm")),
        out_specs=(P("tm", "rhs"), P("tm", "rhs"), P("rhs", "tm"), P("rhs", "tm")),
        check_vma=False,
    )
```

```python
import functools

import jax
import jax.numpy as jnp
from jax import lax
from jax.experimental import pallas as pl
from jax.experimental.pallas import tpu as pltpu
from jax.sharding import PartitionSpec as P

f32, bf16 = jnp.float32, jnp.bfloat16
N = 512
HALF = 256
RHS = 128
SHARE = 64
LOWEST = 2.0
TOL = 2e-6
MAX_STEPS = 40
VMEM = pl.BlockSpec(memory_space=pltpu.VMEM)
ANY = pl.BlockSpec(memory_space=pl.ANY)
MESH = pl.DeviceIdType.MESH
NN = (((1,), (0,)), ((), ()))
NT = (((1,), (1,)), ((), ()))


def split(x):
    high = x.astype(bf16)
    return high, (x - high.astype(f32)).astype(bf16)


def mul(a, b, dims=NN):
    one = lambda p, q: lax.dot_general(p, q, dims, preferred_element_type=f32)
    return one(a[0], b[0]) + (one(a[0], b[1]) + one(a[1], b[0]))


def identity(n):
    return (
        lax.broadcasted_iota(jnp.int32, (n, n), 0) == lax.broadcasted_iota(jnp.int32, (n, n), 1)
    ).astype(f32)


def newton(block, x_ref, d_ref):
    n = block.shape[0]
    d_ref[0], d_ref[1] = split(block)
    top = jnp.maximum(jnp.max(jnp.sum(jnp.abs(block), axis=0, keepdims=True)), LOWEST)
    eye = identity(n)
    gap = (top - LOWEST) / (top + LOWEST)
    lead = 2.0 / (top + LOWEST)
    gain = 2.0 / (2.0 - gap * gap)
    x_ref[...] = (gain * lead) * (2.0 * eye - lead * block)
    gap = 0.5 * gain * gap * gap

    def more(state):
        step, gap = state
        return jnp.logical_and(gap > TOL, step < MAX_STEPS)

    def body(state):
        step, gap = state
        x = x_ref[...]
        x_parts = split(x)
        rest = split(eye - mul((d_ref[0], d_ref[1]), x_parts))
        gain = 2.0 / (2.0 - gap * gap)
        x_ref[...] = gain * (x + mul(x_parts, rest))
        return step + 1, 0.5 * gain * gap * gap

    lax.while_loop(more, body, (jnp.int32(0), gap))
    return x_ref[...]


def places():
    core = lax.axis_index("rhs")
    return (
        core,
        pl.ds(pl.multiple_of(core * HALF, HALF), HALF),
        pl.ds(pl.multiple_of(HALF - core * HALF, HALF), HALF),
        pl.ds(pl.multiple_of(core * SHARE, SHARE), SHARE),
        pl.ds(pl.multiple_of(SHARE - core * SHARE, SHARE), SHARE),
    )


def invert(first_block, cross_block, last_block, out_ref, x_ref, d_ref):
    _, mine, other, _, _ = places()
    first = newton(first_block, x_ref, d_ref)
    cross = split(cross_block)
    lift = split(mul(cross, split(first)))
    out_ref[mine, mine] = first
    last = newton(last_block() - mul(lift, cross, NT), x_ref, d_ref)
    low = -mul(split(last), lift)
    up = low.T
    out_ref[other, other] = last
    out_ref[other, mine] = low
    out_ref[mine, other] = up
    out_ref[mine, mine] = out_ref[mine, mine] - mul(split(up), lift)


def loads(sems, *pairs):
    copies = [
        pltpu.make_async_copy(source, target, sems.at[index])
        for index, (source, target) in enumerate(pairs)
    ]
    for copy in copies:
        copy.start()
    return copies


def rows(first, second, count=N):
    core = lax.axis_index("rhs")
    return pl.ds(pl.multiple_of(first + core * (second - first), HALF), count)


def level_one(
    diag, lower, right_side, d_other, g_other, f_other,
    inverse_ref, v_ref, z_ref, send_ref, keep_ref, gz_ref,
    d_own, d_last, g_whole, g_ref, f_ref, x_ref, d_ref, sems,
):
    core, mine, other, share, rest = places()
    section = rows(N, 3 * N)
    copies = loads(
        sems,
        (diag.at[section], d_own),
        (d_other, d_last),
        (lower.at[rows(2 * N, 3 * N)], g_whole.at[:, mine]),
        (g_other, g_whole.at[:, other]),
        (right_side.at[:, section], f_ref.at[share]),
        (f_other, f_ref.at[rest]),
    )
    copies[0].wait()

    def last_block():
        copies[1].wait()
        return d_last[...]

    invert(d_own[mine], d_own[other], last_block, inverse_ref, x_ref, d_ref)
    for copy in copies[2:]:
        copy.wait()

    @pl.when(core == 0)
    def _():
        g_ref[...] = g_whole[...]

    @pl.when(core == 1)
    def _():
        g_ref[...] = g_whole[...].T

    inverse, g = split(inverse_ref[...]), split(g_ref[...])
    v = mul(inverse, g, NT)
    v_ref[...] = v
    g_whole[...] = mul(g, split(v))
    z = mul(split(f_ref[...]), inverse)
    z_ref[...] = z
    gz = mul(split(z), g, NT)
    gz_ref[...] = gz
    send_ref[:N] = g_whole[:, other]
    send_ref[N : N + HALF] = g_whole[mine, mine]
    send_ref[N + HALF : N + HALF + RHS] = gz[:, :HALF]
    send_ref[N + HALF + RHS :] = gz[:, HALF:]
    keep_ref[:N] = g_whole[:, mine]
    keep_ref[N:] = g_whole[other, other]


def outward(
    inverse_ref, v_ref, z_ref, lower, h_other, next_left, next_right,
    w_ref, send_ref, hw_ref, hz_ref,
    h_whole, h_ref, sems,
):
    core, mine, other, share, rest = places()

    @pl.when(core == 0)
    def _():
        copies = loads(
            sems, (lower.at[N : 2 * N], h_whole.at[:, :HALF]), (h_other, h_whole.at[:, HALF:])
        )
        for copy in copies:
            copy.wait()
        h_ref[...] = h_whole[...].T

    @pl.when(core == 1)
    def _():
        copies = loads(sems, (next_left, h_ref.at[:, :HALF]), (next_right, h_ref.at[:, HALF:]))
        for copy in copies:
            copy.wait()

    h = split(h_ref[...])
    c = -mul(h, split(v_ref[...]))
    send_ref[:N] = c[:, :HALF]
    send_ref[N : 2 * N] = c[:, HALF:]
    w = mul(split(inverse_ref[...]), h, NT)
    w_ref[...] = w
    h_whole[...] = mul(h, split(w))
    hw_ref[...] = h_whole[:, mine]
    send_ref[2 * N : 3 * N] = h_whole[:, other]
    h_ref[:RHS] = mul(split(z_ref[...]), h, NT)
    hz_ref[...] = h_ref[share]
    send_ref[3 * N : 3 * N + SHARE] = h_ref[rest, :HALF]
    send_ref[3 * N + SHARE :] = h_ref[rest, HALF:]


def level_two(
    diag, right_side, d_other, f_other, keep_ref, came_ref, gz_ref,
    inverse_ref, z_ref,
    d_own, f_ref, x_ref, d_ref, sems,
):
    core, mine, other, share, rest = places()
    copies = loads(
        sems,
        (diag.at[2 * N : 3 * N], d_own),
        (right_side.at[:, 2 * N : 3 * N], f_ref.at[share]),
    )
    copies[0].wait()
    d_own[...] = d_own[...] - (keep_ref[:N] + came_ref[:N])
    last_block = lambda: d_other[...] - (keep_ref[N:] + came_ref[N : N + HALF])
    invert(d_own[mine], d_own[other], last_block, inverse_ref, x_ref, d_ref)
    copies[1].wait()
    f_ref[rest] = f_other[...]
    start = N + HALF
    f_ref[:, :HALF] = f_ref[:, :HALF] - (gz_ref[:, :HALF] + came_ref[start : start + RHS])
    f_ref[:, HALF:] = f_ref[:, HALF:] - (gz_ref[:, HALF:] + came_ref[start + RHS :])
    z_ref[...] = mul(split(f_ref[...]), split(inverse_ref[...]))


def survivors(
    inverse_ref, z2_ref, own_ref, came_ref, hw_ref, hz_ref,
    diag, right_side, coarse_sol, v_any, w_any, z_any,
    diag_ref, low_out, rhs_ref, solution_ref,
    c_both, hw_both, hz_both, low_send, diag_send, rhs_send, diag_came, rhs_came,
    d0, f0, y_ref, v_ref, w_ref, z_ref, y_next, y_send, ys_ref, x2_ref, x_ref, x_both,
    sems, send_sems, recv_sems,
):
    core, mine, other, share, rest = places()
    me = lax.axis_index("tm")
    runs = lax.axis_size("tm")
    after, before = {"tm": lax.rem(me + 1, runs)}, {"tm": lax.rem(me + runs - 1, runs)}
    partner = {"rhs": 1 - core}
    barrier = pltpu.get_barrier_semaphore()
    for device in (after, before, partner):
        pl.semaphore_signal(barrier, inc=1, device_id=device, device_id_type=MESH)
    copies = loads(
        sems,
        (diag.at[:N], d0),
        (right_side.at[:, :N], f0),
        (coarse_sol, y_ref),
        (v_any, v_ref),
        (w_any, w_ref),
        (z_any, z_ref),
    )
    pl.semaphore_wait(barrier, 3)
    sent = []

    def send(source, target, device):
        copy = pltpu.make_async_remote_copy(
            src_ref=source,
            dst_ref=target,
            send_sem=send_sems.at[len(sent)],
            recv_sem=recv_sems.at[len(sent)],
            device_id=device,
            device_id_type=MESH,
        )
        copy.start()
        sent.append(copy)
        return copy

    later = send(coarse_sol, y_next, before)
    for column in range(2):
        span = slice(column * HALF, (column + 1) * HALF)
        c_both[core, :, span] = own_ref[column * N : (column + 1) * N]
        c_both[1 - core, :, span] = came_ref[column * N : (column + 1) * N]
        hz_both[1 - core, :, span] = came_ref[
            3 * N + column * SHARE : 3 * N + (column + 1) * SHARE
        ]
    hw_both[core] = hw_ref[...]
    hw_both[1 - core] = came_ref[2 * N : 3 * N]
    hz_both[core] = hz_ref[...]

    inverse = split(inverse_ref[...])
    right = split(c_both[1])
    u_right = split(mul(inverse, split(c_both[1, mine]), NT))
    arrivals = []
    for half in range(2):
        span = slice(half * HALF, (half + 1) * HALF)
        diag_send[span] = hw_both[1, span] + mul((right[0][span], right[1][span]), u_right)
        arrivals.append(send(diag_send.at[span], diag_came.at[span], after))
    z2 = split(z2_ref[share])
    rhs_send[...] = hz_both[1] + mul(z2, right, NT)
    arrivals.append(send(rhs_send, rhs_came, after))
    left = split(c_both[0])
    u_left = split(mul(inverse, split(c_both[0, mine]), NT))
    lows = []
    for half in range(2):
        span = slice(half * HALF, (half + 1) * HALF)
        low_send[span] = -mul((right[0][span], right[1][span]), u_left)
        lows.append(send(low_send.at[span], low_out.at[span], after))

    for copy in copies[:3]:
        copy.wait()
    diag_ref[...] = d0[...] - hw_both[0] - mul(left, u_left)
    rhs_ref[...] = f0[...] - hz_both[0] - mul(z2, left, NT)

    later.wait_recv()

    @pl.when(core == 0)
    def _():
        y_send[...] = y_next[...]
        ys_ref[0] = y_ref[...]

    @pl.when(core == 1)
    def _():
        y_send[...] = y_ref[...]
        ys_ref[0] = y_next[...]

    swap_y = send(y_send, ys_ref.at[1], partner)
    known = mul(split(y_ref[...]), left) + mul(split(y_next[...]), right)
    x2_ref[0] = z2_ref[share] - mul(split(known), inverse)
    swap_x2 = send(x2_ref.at[0], x2_ref.at[1], partner)
    for copy in copies[3:]:
        copy.wait()
    swap_y.wait_recv()
    swap_x2.wait_recv()
    v, w = split(v_ref[...]), split(w_ref[...])
    for slot, place in ((1, rest), (0, share)):
        x_ref[slot] = (
            z_ref[place]
            - mul(split(ys_ref[slot]), w, NT)
            - mul(split(x2_ref[slot]), v, NT)
        )
        if slot == 1:
            swap_x = send(x_ref.at[1], x_both.at[core], partner)
    solution_ref[:, :N] = y_ref[...]
    solution_ref[:, 2 * N : 3 * N] = x2_ref[0]
    swap_x.wait_recv()

    @pl.when(core == 0)
    def _():
        solution_ref[:, N : 2 * N] = x_ref[0]
        solution_ref[:, 3 * N :] = x_both[1]

    @pl.when(core == 1)
    def _():
        solution_ref[:, N : 2 * N] = x_both[0]
        solution_ref[:, 3 * N :] = x_ref[0]

    for half in range(2):
        span = slice(half * HALF, (half + 1) * HALF)
        arrivals[half].wait_recv()
        diag_ref[span] = diag_ref[span] - diag_came[span]
    arrivals[2].wait_recv()
    rhs_ref[...] = rhs_ref[...] - rhs_came[...]
    for copy in lows:
        copy.wait_recv()
    for copy in sent:
        copy.wait_send()


def partners_body(
    diag, lower, right_side,
    d_ref, g_ref, f_ref, h_ref, d2_ref, f2_ref,
    send_sems, recv_sems,
):
    core = lax.axis_index("rhs")
    partner = {"rhs": 1 - core}
    barrier = pltpu.get_barrier_semaphore()
    pl.semaphore_signal(barrier, inc=1, device_id=partner, device_id_type=MESH)
    pl.semaphore_wait(barrier, 1)
    section = rows(3 * N, N)
    windows = (
        (diag.at[rows(3 * N, N + HALF, HALF)], d_ref),
        (lower.at[rows(3 * N, 2 * N)], g_ref),
        (right_side.at[:, section], f_ref),
        (diag.at[rows(2 * N, 2 * N + HALF, HALF)], d2_ref),
        (right_side.at[:, 2 * N : 3 * N], f2_ref),
        (lower.at[N : 2 * N], h_ref),
    )
    copies = [
        pltpu.make_async_remote_copy(
            src_ref=source,
            dst_ref=target,
            send_sem=send_sems.at[index],
            recv_sem=recv_sems.at[index],
            device_id=partner,
            device_id_type=MESH,
        )
        for index, (source, target) in enumerate(windows)
    ]
    for copy in copies:
        copy.start()
    for copy in copies:
        copy.wait()


def shape(*dims):
    return jax.ShapeDtypeStruct(dims, f32)


def call(body, in_specs, outs, out_specs, scratch, flops, args, limit, **params):
    size = sum(a.size for a in args) + sum(o.size for o in outs)
    return pl.pallas_call(
        body,
        out_shape=outs,
        in_specs=in_specs,
        out_specs=out_specs,
        scratch_shapes=scratch,
        compiler_params=pltpu.CompilerParams(vmem_limit_bytes=limit << 20, **params),
        cost_estimate=pl.CostEstimate(flops=flops, bytes_accessed=4 * size, transcendentals=0),
    )(*args)


def newton_scratch():
    return [pltpu.VMEM((HALF, HALF), f32), pltpu.VMEM((2, HALF, HALF), bf16)]


def copy_sems(count):
    return pltpu.SemaphoreType.DMA((count,))


def shards(diag, lower, right_side, coarse_sol):
    runs = lax.axis_size("tm")
    next_left, next_right = (
        lax.ppermute(
            lower[:N],
            ("tm", "rhs"),
            [(2 * ((i + 1) % runs) + source, 2 * i + 1) for i in range(runs)],
        )
        for source in (0, 1)
    )
    swap = lambda x: lax.ppermute(x, "rhs", [(0, 1), (1, 0)])
    d_other, g_other, f_other, d2_other, f2_other, h_other = (
        lambda d, g, f, h, d2, f2: (d, g, f, d2, f2, h)
    )(
        *call(
            partners_body,
            [ANY] * 3,
            [shape(HALF, HALF), shape(N, HALF), shape(SHARE, N), shape(N, HALF),
             shape(HALF, HALF), shape(SHARE, N)],
            [ANY] * 6,
            [copy_sems(6), copy_sems(6)],
            0,
            (diag, lower, right_side),
            8,
            collective_id=1,
            has_side_effects=True,
        )
    )
    inverse, v, z, send, keep, gz = call(
        level_one,
        [ANY] * 6,
        [shape(N, N), shape(N, N), shape(RHS, N), shape(2 * N, HALF), shape(N + HALF, HALF),
         shape(RHS, N)],
        [VMEM] * 6,
        [pltpu.VMEM((N, HALF), f32), pltpu.VMEM((HALF, HALF), f32), pltpu.VMEM((N, N), f32),
         pltpu.VMEM((N, N), f32), pltpu.VMEM((RHS, N), f32)] + newton_scratch() + [copy_sems(6)],
        2 * N**3 * 20,
        (diag, lower, right_side, d_other, g_other, f_other),
        28,
    )
    came = swap(send)
    w, pack, hw, hz = call(
        outward,
        [VMEM] * 3 + [ANY] * 4,
        [shape(N, N), shape(3 * N + RHS, HALF), shape(N, HALF), shape(SHARE, N)],
        [VMEM] * 4,
        [pltpu.VMEM((N, N), f32), pltpu.VMEM((N, N), f32), copy_sems(2)],
        2 * N**3 * 10,
        (inverse, v, z, lower, h_other, next_left, next_right),
        28,
    )
    pack_came = swap(pack)
    inverse2, z2 = call(
        level_two,
        [ANY] * 2 + [VMEM] * 5,
        [shape(N, N), shape(RHS, N)],
        [VMEM] * 2,
        [pltpu.VMEM((N, HALF), f32), pltpu.VMEM((RHS, N), f32)]
        + newton_scratch() + [copy_sems(2)],
        2 * N**3 * 20,
        (diag, right_side, d2_other, f2_other, keep, came, gz),
        28,
    )
    small = pltpu.VMEM((SHARE, N), f32)
    small_pair = pltpu.VMEM((2, SHARE, N), f32)
    half = pltpu.VMEM((N, HALF), f32)
    full = pltpu.VMEM((N, N), f32)
    return call(
        survivors,
        [VMEM] * 6 + [ANY] * 6,
        [shape(N, HALF), shape(N, HALF), shape(SHARE, N), shape(SHARE, 4 * N)],
        [VMEM, ANY, VMEM, VMEM],
        [pltpu.VMEM((2, N, N), f32), pltpu.VMEM((2, N, HALF), f32), small_pair,
         half, half, small, half, small,
         half, small, small, full, full, pltpu.VMEM((RHS, N), f32), small, small, small_pair,
         small_pair, small_pair, small_pair,
         copy_sems(6), copy_sems(9), copy_sems(9)],
        2 * N**3 * 9,
        (inverse2, z2, pack, pack_came, hw, hz, diag, right_side, coarse_sol, v, w, z),
        40,
        collective_id=2,
        has_side_effects=True,
    )


def solution(mesh):
    return jax.shard_map(
        shards,
        mesh=mesh,
        in_specs=(P("tm", "rhs"), P("tm", "rhs"), P("rhs", "tm"), P("rhs", "tm")),
        out_specs=(P("tm", "rhs"), P("tm", "rhs"), P("rhs", "tm"), P("rhs", "tm")),
        check_vma=False,
    )
```

```python
import functools

import jax
import jax.numpy as jnp
from jax import lax
from jax.experimental import pallas as pl
from jax.experimental.pallas import tpu as pltpu
from jax.sharding import PartitionSpec as P

f32, bf16 = jnp.float32, jnp.bfloat16
N = 512
HALF = 256
RHS = 128
SHARE = 64
LOWEST = 2.0
TOL = 4e-6
COARSE_TOL = 1.6e-3
NOISE = 2e-6
FIXED_STEPS = 4
MAX_STEPS = 40
VMEM = pl.BlockSpec(memory_space=pltpu.VMEM)
ANY = pl.BlockSpec(memory_space=pl.ANY)
HBM = pl.BlockSpec(memory_space=pltpu.HBM)
MESH = pl.DeviceIdType.MESH
NN = (((1,), (0,)), ((), ()))
NT = (((1,), (1,)), ((), ()))


def split(x):
    high = x.astype(bf16)
    return high, (x - high.astype(f32)).astype(bf16)


def mul(a, b, dims=NN):
    one = lambda p, q: lax.dot_general(p, q, dims, preferred_element_type=f32)
    return one(a[0], b[0]) + (one(a[0], b[1]) + one(a[1], b[0]))


def identity(n):
    return (
        lax.broadcasted_iota(jnp.int32, (n, n), 0) == lax.broadcasted_iota(jnp.int32, (n, n), 1)
    ).astype(f32)


def norm_steps(gap):
    gain = 2.0 / (2.0 - gap * gap)
    return gain, 0.5 * gain * gap * gap


def newton_start(block, x_ref, t_ref, d_ref):
    d_ref[0], d_ref[1] = split(block)
    top = jnp.maximum(jnp.max(jnp.sum(jnp.abs(block), axis=0, keepdims=True)), LOWEST)
    lead = 2.0 / (top + LOWEST)
    gain, gap = norm_steps((top - LOWEST) / (top + LOWEST))
    rest = 2.0 * identity(block.shape[0]) - lead * block
    x_ref[...] = (gain * lead) * rest
    t_ref[...] = (gain * lead) * mul((d_ref[0], d_ref[1]), split(rest))
    return gap


def newton_step(gap, x_ref, t_ref):
    gain, gap = norm_steps(gap)
    n = x_ref.shape[0]
    rest = split(2.0 * identity(n) - t_ref[...])
    both = mul(split(jnp.concatenate([t_ref[...], x_ref[...]], axis=0)), rest)
    t_ref[...] = gain * both[:n]
    x_ref[...] = gain * both[n:]
    return gap


def newton_finish(gap, x_ref, t_ref, d_ref, noise):
    def more(limit):
        return lambda state: jnp.logical_and(state[1] > limit, state[0] < MAX_STEPS)

    step = lambda state: (state[0] + 1, newton_step(state[1], x_ref, t_ref))
    _, gap = lax.while_loop(more(COARSE_TOL), step, (jnp.int32(0), gap))

    def correct(state):
        x = x_ref[...]
        x_parts = split(x)
        residual = split(identity(x.shape[0]) - mul((d_ref[0], d_ref[1]), x_parts))
        x_ref[...] = x + mul(x_parts, residual)
        return state[0] + 1, state[1] * state[1]

    lax.while_loop(more(TOL), correct, (jnp.int32(0), gap + noise))
    return x_ref[...]


def noise_of(block):
    return jnp.max(jnp.sum(jnp.abs(block), axis=0, keepdims=True)) * NOISE


def newton(block, x_ref, t_ref, d_ref):
    gap = newton_start(block, x_ref, t_ref, d_ref)
    return newton_finish(gap, x_ref, t_ref, d_ref, noise_of(block))


def places():
    core = lax.axis_index("rhs")
    return (
        core,
        pl.ds(pl.multiple_of(core * HALF, HALF), HALF),
        pl.ds(pl.multiple_of(HALF - core * HALF, HALF), HALF),
        pl.ds(pl.multiple_of(core * SHARE, SHARE), SHARE),
        pl.ds(pl.multiple_of(SHARE - core * SHARE, SHARE), SHARE),
    )


def invert(first, cross_block, last_block, out_ref, x_ref, t_ref, d_ref):
    _, mine, other, _, _ = places()
    cross = split(cross_block)
    lift = split(mul(cross, split(first)))
    out_ref[mine, mine] = first
    last = newton(last_block() - mul(lift, cross, NT), x_ref, t_ref, d_ref)
    low = -mul(split(last), lift)
    up = low.T
    out_ref[other, other] = last
    out_ref[other, mine] = low
    out_ref[mine, other] = up
    out_ref[mine, mine] = out_ref[mine, mine] - mul(split(up), lift)


def loads(sems, *pairs):
    copies = [
        pltpu.make_async_copy(source, target, sems.at[index])
        for index, (source, target) in enumerate(pairs)
    ]
    for copy in copies:
        copy.start()
    return copies


def rows(first, second, count=N):
    core = lax.axis_index("rhs")
    return pl.ds(pl.multiple_of(first + core * (second - first), HALF), count)


def remote(source, target, sems, index, device):
    copy = pltpu.make_async_remote_copy(
        src_ref=source,
        dst_ref=target,
        send_sem=sems[0].at[index],
        recv_sem=sems[1].at[index],
        device_id=device,
        device_id_type=MESH,
    )
    copy.start()
    return copy


def greet(*devices):
    barrier = pltpu.get_barrier_semaphore()
    for device in devices:
        pl.semaphore_signal(barrier, inc=1, device_id=device, device_id_type=MESH)
    return lambda: pl.semaphore_wait(barrier, len(devices))


def partners(
    diag, lower, right_side,
    d_other, g_other, f_other, h_other, d2_other, x_ref, t_ref, gap_ref,
    block_ref, d_ref, sems, send_sems, recv_sems,
):
    core = lax.axis_index("rhs")
    partner = {"rhs": 1 - core}
    arrived = greet(partner)
    mine = loads(sems, (diag.at[rows(N, 3 * N + HALF, HALF)], block_ref))
    arrived()
    pair = (send_sems, recv_sems)
    copies = [
        remote(source, target, pair, index, partner)
        for index, (source, target) in enumerate(
            (
                (diag.at[rows(3 * N, N + HALF, HALF)], d_other),
                (lower.at[rows(3 * N, 2 * N)], g_other),
                (right_side.at[:, rows(3 * N, N)], f_other),
                (diag.at[rows(2 * N, 2 * N + HALF, HALF)], d2_other),
                (lower.at[N : 2 * N], h_other),
            )
        )
    ]
    mine[0].wait()
    gap = newton_start(block_ref[...], x_ref, t_ref, d_ref)
    gap = lax.fori_loop(0, FIXED_STEPS, lambda _, gap: newton_step(gap, x_ref, t_ref), gap)
    gap_ref[...] = jnp.full(gap_ref.shape, gap, f32)
    for copy in copies:
        copy.wait()


def level_one(
    diag, lower, d_other, g_other, first_x, first_t, gap_in,
    inverse_ref, v_ref, send_ref, keep_ref,
    d_own, d_last, g_whole, g_ref, x_ref, t_ref, d_ref, sems,
):
    core, mine, other, share, rest = places()
    copies = loads(
        sems,
        (diag.at[rows(N, 3 * N)], d_own),
        (d_other, d_last),
        (lower.at[rows(2 * N, 3 * N)], g_whole.at[:, mine]),
        (g_other, g_whole.at[:, other]),
    )
    x_ref[...] = first_x[...]
    t_ref[...] = first_t[...]
    copies[0].wait()
    block = d_own[mine]
    d_ref[0], d_ref[1] = split(block)
    first = newton_finish(jnp.max(gap_in[...]), x_ref, t_ref, d_ref, noise_of(block))

    def last_block():
        copies[1].wait()
        return d_last[...]

    invert(first, d_own[other], last_block, inverse_ref, x_ref, t_ref, d_ref)
    for copy in copies[2:]:
        copy.wait()

    @pl.when(core == 0)
    def _():
        g_ref[...] = g_whole[...]

    @pl.when(core == 1)
    def _():
        g_ref[...] = g_whole[...].T

    g = split(g_ref[...])
    v = mul(split(inverse_ref[...]), g, NT)
    v_ref[...] = v
    g_whole[...] = mul(g, split(v))
    send_ref[:N] = g_whole[:, other]
    send_ref[N:] = g_whole[mine, mine]
    keep_ref[:N] = g_whole[:, mine]
    keep_ref[N:] = g_whole[other, other]


def outward(
    inverse_ref, v_ref, send_ref, lower, right_side, f_other, h_other, next_left, next_right,
    came_ref, w_ref, z_ref, pack_ref, hw_ref, small_ref,
    h_whole, h_ref, f_ref, sems, send_sems, recv_sems,
):
    core, mine, other, share, rest = places()
    partner = {"rhs": 1 - core}
    arrived = greet(partner)
    wanted = loads(
        sems, (right_side.at[:, rows(N, 3 * N)], f_ref.at[share]), (f_other, f_ref.at[rest])
    )
    arrived()
    swapped = remote(send_ref, came_ref, (send_sems, recv_sems), 0, partner)

    @pl.when(core == 0)
    def _():
        copies = [
            pltpu.make_async_copy(lower.at[N : 2 * N], h_whole.at[:, :HALF], sems.at[2]),
            pltpu.make_async_copy(h_other, h_whole.at[:, HALF:], sems.at[3]),
        ]
        for copy in copies:
            copy.start()
        for copy in copies:
            copy.wait()
        h_ref[...] = h_whole[...].T

    @pl.when(core == 1)
    def _():
        copies = [
            pltpu.make_async_copy(next_left, h_ref.at[:, :HALF], sems.at[2]),
            pltpu.make_async_copy(next_right, h_ref.at[:, HALF:], sems.at[3]),
        ]
        for copy in copies:
            copy.start()
        for copy in copies:
            copy.wait()

    h, v = split(h_ref[...]), split(v_ref[...])
    c = -mul(h, v)
    pack_ref[:N] = c[:, :HALF]
    pack_ref[N : 2 * N] = c[:, HALF:]
    inverse = split(inverse_ref[...])
    w = mul(inverse, h, NT)
    w_ref[...] = w
    w = split(w)
    h_whole[...] = mul(h, w)
    hw_ref[...] = h_whole[:, mine]
    pack_ref[2 * N : 3 * N] = h_whole[:, other]
    for copy in wanted:
        copy.wait()
    f = split(f_ref[...])
    z_ref[...] = mul(f, inverse)
    for index, term in enumerate((w, v)):
        first = 3 * N + index * RHS
        f_ref[...] = mul(f, term)
        small_ref[index] = f_ref[share]
        pack_ref[first : first + SHARE] = f_ref[rest, :HALF]
        pack_ref[first + SHARE : first + RHS] = f_ref[rest, HALF:]
    swapped.wait()


def level_two(
    diag, d_other, keep_ref, came_ref, inverse_ref,
    d_own, x_ref, t_ref, d_ref, sems,
):
    core, mine, other, share, rest = places()
    loads(sems, (diag.at[2 * N : 3 * N], d_own))[0].wait()
    d_own[...] = d_own[...] - (keep_ref[:N] + came_ref[:N])
    last_block = lambda: d_other[...] - (keep_ref[N:] + came_ref[N:])
    first = newton(d_own[mine], x_ref, t_ref, d_ref)
    invert(first, d_own[other], last_block, inverse_ref, x_ref, t_ref, d_ref)


def survivors(
    inverse_ref, own_ref, came_ref, hw_ref, small_ref,
    diag, right_side, coarse_sol, v_any, w_any, z_any,
    diag_ref, low_out, rhs_ref, solution_ref,
    c_both, hw_both, hz_both, low_send, diag_send, rhs_send, diag_came, cross_came, rhs_came,
    d0, f0, f2, y_ref, v_ref, w_ref, z_ref, y_next, y_send, ys_ref, x2_ref, x_ref, x_both,
    sems, send_sems, recv_sems,
):
    core, mine, other, share, rest = places()
    me = lax.axis_index("tm")
    runs = lax.axis_size("tm")
    after, before = {"tm": lax.rem(me + 1, runs)}, {"tm": lax.rem(me + runs - 1, runs)}
    partner = {"rhs": 1 - core}
    arrived = greet(after, before, partner)
    copies = loads(
        sems,
        (right_side.at[:, 2 * N : 3 * N], f2),
        (diag.at[:N], d0),
        (right_side.at[:, :N], f0),
        (coarse_sol, y_ref),
        (v_any, v_ref),
        (w_any, w_ref),
        (z_any, z_ref),
    )
    pair = (send_sems, recv_sems)
    inverse = split(inverse_ref[...])
    for column in range(2):
        span = slice(column * HALF, (column + 1) * HALF)
        c_both[core, :, span] = own_ref[column * N : (column + 1) * N]
        c_both[1 - core, :, span] = came_ref[column * N : (column + 1) * N]
        first = 3 * N + column * SHARE
        hz_both[1 - core, :, span] = came_ref[first : first + SHARE]
        hz_both[2, :, span] = came_ref[first + RHS : first + RHS + SHARE]
    hw_both[core] = hw_ref[...]
    hw_both[1 - core] = came_ref[2 * N : 3 * N]
    hz_both[core] = small_ref[0]
    right = split(c_both[1])
    u_right = split(mul(inverse, split(c_both[1, mine]), NT))
    arrived()
    later = remote(coarse_sol, y_next, pair, 0, before)

    def diag_block(place):
        c_rows = split(c_both[1, place])
        return hw_both[1, place] + mul(c_rows, u_right)

    corner = pl.ds(pl.multiple_of(core * HALF, HALF), HALF)

    @pl.when(core == 0)
    def _():
        diag_send[HALF:] = diag_block(slice(HALF, N))
        remote(diag_send.at[HALF:], diag_came.at[HALF:], pair, 1, after)

    diag_send[:HALF] = diag_block(corner)
    square = remote(diag_send.at[:HALF], diag_came.at[:HALF], pair, 2, after)
    left = split(c_both[0])
    u_left = split(mul(inverse, split(c_both[0, mine]), NT))
    lows = []
    for half in range(2):
        span = slice(half * HALF, (half + 1) * HALF)
        low_send[span] = -mul((right[0][span], right[1][span]), u_left)
        lows.append(remote(low_send.at[span], low_out.at[span], pair, 3 + half, after))
    copies[0].wait()
    z2 = mul(split(f2[...] - (small_ref[1] + hz_both[2])), inverse)
    z2_parts = split(z2)
    rhs_send[...] = hz_both[1] + mul(z2_parts, right, NT)
    rhs_sent = remote(rhs_send, rhs_came, pair, 5, after)

    for copy in copies[1:4]:
        copy.wait()
    diag_ref[...] = d0[...] - hw_both[0] - mul(left, u_left)
    rhs_ref[...] = f0[...] - hz_both[0] - mul(z2_parts, left, NT)

    later.wait_recv()

    @pl.when(core == 0)
    def _():
        y_send[...] = y_next[...]
        ys_ref[0] = y_ref[...]

    @pl.when(core == 1)
    def _():
        y_send[...] = y_ref[...]
        ys_ref[0] = y_next[...]

    swap_y = remote(y_send, ys_ref.at[1], pair, 6, partner)
    known = mul(split(y_ref[...]), left) + mul(split(y_next[...]), right)
    x2_ref[0] = z2 - mul(split(known), inverse)
    swap_x2 = remote(x2_ref.at[0], x2_ref.at[1], pair, 7, partner)
    for copy in copies[4:]:
        copy.wait()
    swap_y.wait_recv()
    swap_x2.wait_recv()
    v, w = split(v_ref[...]), split(w_ref[...])
    for slot, place in ((1, rest), (0, share)):
        x_ref[slot] = (
            z_ref[place]
            - mul(split(ys_ref[slot]), w, NT)
            - mul(split(x2_ref[slot]), v, NT)
        )
        if slot == 1:
            swap_x = remote(x_ref.at[1], x_both, pair, 8, partner)
    solution_ref[:, :N] = y_ref[...]
    solution_ref[:, 2 * N : 3 * N] = x2_ref[0]
    swap_x.wait_recv()

    @pl.when(core == 0)
    def _():
        solution_ref[:, N : 2 * N] = x_ref[0]
        solution_ref[:, 3 * N :] = x_both[...]

    @pl.when(core == 1)
    def _():
        solution_ref[:, N : 2 * N] = x_both[...]
        solution_ref[:, 3 * N :] = x_ref[0]

    def crossing(device):
        return pltpu.make_async_remote_copy(
            src_ref=diag_send.at[HALF:],
            dst_ref=diag_came.at[HALF:],
            send_sem=send_sems.at[1],
            recv_sem=recv_sems.at[1],
            device_id=device,
            device_id_type=MESH,
        )

    def handing():
        return pltpu.make_async_remote_copy(
            src_ref=diag_came.at[HALF:],
            dst_ref=cross_came,
            send_sem=send_sems.at[9],
            recv_sem=recv_sems.at[9],
            device_id=partner,
            device_id_type=MESH,
        )

    @pl.when(core == 0)
    def _():
        crossing(after).wait_recv()
        handing().start()
        diag_ref[HALF:] = diag_ref[HALF:] - diag_came[HALF:]

    square.wait_recv()
    diag_ref[corner] = diag_ref[corner] - diag_came[:HALF]

    @pl.when(core == 1)
    def _():
        handing().wait_recv()
        diag_ref[:HALF] = diag_ref[:HALF] - cross_came[...].T

    rhs_sent.wait_recv()
    rhs_ref[...] = rhs_ref[...] - rhs_came[...]
    for copy in lows:
        copy.wait_recv()
    for copy in (later, square, *lows, rhs_sent, swap_y, swap_x2, swap_x):
        copy.wait_send()

    @pl.when(core == 0)
    def _():
        crossing(after).wait_send()
        handing().wait_send()


def shape(*dims):
    return jax.ShapeDtypeStruct(dims, f32)


def call(body, in_specs, outs, out_specs, scratch, flops, args, limit, **params):
    size = sum(a.size for a in args) + sum(o.size for o in outs)
    return pl.pallas_call(
        body,
        out_shape=outs,
        in_specs=in_specs,
        out_specs=out_specs,
        scratch_shapes=scratch,
        compiler_params=pltpu.CompilerParams(vmem_limit_bytes=limit << 20, **params),
        cost_estimate=pl.CostEstimate(flops=flops, bytes_accessed=4 * size, transcendentals=0),
    )(*args)


def newton_scratch():
    return [pltpu.VMEM((HALF, HALF), f32)] * 2 + [pltpu.VMEM((2, HALF, HALF), bf16)]


def copy_sems(count):
    return pltpu.SemaphoreType.DMA((count,))


def shards(diag, lower, right_side, coarse_sol):
    runs = lax.axis_size("tm")
    sent_first = lower[:N]
    diag, lower, right_side, coarse_sol = (
        pltpu.with_memory_space_constraint(array, pltpu.HBM)
        for array in (diag, lower, right_side, coarse_sol)
    )
    next_left, next_right = (
        lax.ppermute(
            sent_first,
            ("tm", "rhs"),
            [(2 * ((i + 1) % runs) + source, 2 * i + 1) for i in range(runs)],
        )
        for source in (0, 1)
    )
    swap = lambda x: lax.ppermute(x, "rhs", [(0, 1), (1, 0)])
    full, half, quarter = (N, N), (N, HALF), (HALF, HALF)
    small, scratch = (SHARE, N), lambda *dims: pltpu.VMEM(dims, f32)
    d_other, g_other, f_other, h_other, d2_other, first_x, first_t, gap = call(
        partners,
        [HBM] * 3,
        [shape(*quarter), shape(*half), shape(*small), shape(*half), shape(*quarter),
         shape(*quarter), shape(*quarter), shape(8, 128)],
        [ANY] * 5 + [VMEM] * 3,
        [scratch(*quarter), pltpu.VMEM((2, HALF, HALF), bf16),
         copy_sems(1), copy_sems(5), copy_sems(5)],
        2 * HALF**3 * 30,
        (diag, lower, right_side),
        16,
        collective_id=1,
        has_side_effects=True,
    )
    inverse, v, send, keep = call(
        level_one,
        [HBM] * 2 + [ANY] * 2 + [VMEM] * 3,
        [shape(*full), shape(*full), shape(N + HALF, HALF), shape(N + HALF, HALF)],
        [VMEM] * 4,
        [scratch(*half), scratch(*quarter), scratch(*full), scratch(*full)]
        + newton_scratch() + [copy_sems(4)],
        2 * N**3 * 20,
        (diag, lower, d_other, g_other, first_x, first_t, gap),
        28,
    )
    came, w, z, pack, hw, tails = call(
        outward,
        [VMEM] * 2 + [ANY] + [HBM] * 2 + [ANY] * 4,
        [shape(N + HALF, HALF), shape(*full), shape(RHS, N), shape(3 * N + 2 * RHS, HALF),
         shape(*half), shape(2, *small)],
        [ANY] + [VMEM] * 5,
        [scratch(*full), scratch(*full), scratch(RHS, N), copy_sems(4), copy_sems(1), copy_sems(1)],
        2 * N**3 * 10,
        (inverse, v, send, lower, right_side, f_other, h_other, next_left, next_right),
        28,
        collective_id=3,
        has_side_effects=True,
    )
    pack_came = swap(pack)
    inverse2 = call(
        level_two,
        [HBM] + [VMEM] * 3,
        [shape(*full)],
        [VMEM],
        [scratch(*half)] + newton_scratch() + [copy_sems(1)],
        2 * N**3 * 20,
        (diag, d2_other, keep, came),
        28,
    )[0]
    return call(
        survivors,
        [VMEM] * 5 + [HBM] * 3 + [ANY] * 3,
        [shape(*half), shape(*half), shape(*small), shape(SHARE, 4 * N)],
        [VMEM, ANY, VMEM, VMEM],
        [scratch(2, *full), scratch(2, *half), scratch(3, *small),
         scratch(*half), scratch(*half), scratch(*small),
         scratch(*half), scratch(*quarter), scratch(*small),
         scratch(*half), scratch(*small), scratch(*small), scratch(*small),
         scratch(*full), scratch(*full), scratch(RHS, N),
         scratch(*small), scratch(*small), scratch(2, *small),
         scratch(2, *small), scratch(2, *small), scratch(*small),
         copy_sems(7), copy_sems(10), copy_sems(10)],
        2 * N**3 * 9,
        (inverse2, pack, pack_came, hw, tails, diag, right_side, coarse_sol, v, w, z),
        40,
        collective_id=2,
        has_side_effects=True,
    )


def solution(mesh):
    return jax.shard_map(
        shards,
        mesh=mesh,
        in_specs=(P("tm", "rhs"), P("tm", "rhs"), P("rhs", "tm"), P("rhs", "tm")),
        out_specs=(P("tm", "rhs"), P("tm", "rhs"), P("rhs", "tm"), P("rhs", "tm")),
        check_vma=False,
    )
```

```python
import functools

import jax
import jax.numpy as jnp
from jax import lax
from jax.experimental import pallas as pl
from jax.experimental.pallas import tpu as pltpu
from jax.sharding import PartitionSpec as P

f32, bf16 = jnp.float32, jnp.bfloat16
N = 512
HALF = 256
RHS = 128
SHARE = 64
QUARTER = 128
ROW = 4
DIRECT = 320
CHUNK = 96
LOWEST = 2.0
TOL = 4e-6
COARSE_TOL = 1.6e-3
NOISE = 2e-6
FIXED_STEPS = 4
MAX_STEPS = 40
VMEM = pl.BlockSpec(memory_space=pltpu.VMEM)
ANY = pl.BlockSpec(memory_space=pl.ANY)
HBM = pl.BlockSpec(memory_space=pltpu.HBM)
MESH = pl.DeviceIdType.MESH
NN = (((1,), (0,)), ((), ()))
NT = (((1,), (1,)), ((), ()))


def split(x):
    high = x.astype(bf16)
    return high, (x - high.astype(f32)).astype(bf16)


def mul(a, b, dims=NN):
    one = lambda p, q: lax.dot_general(p, q, dims, preferred_element_type=f32)
    return one(a[0], b[0]) + (one(a[0], b[1]) + one(a[1], b[0]))


def identity(n):
    return (
        lax.broadcasted_iota(jnp.int32, (n, n), 0) == lax.broadcasted_iota(jnp.int32, (n, n), 1)
    ).astype(f32)


def norm_steps(gap):
    gain = 2.0 / (2.0 - gap * gap)
    return gain, 0.5 * gain * gap * gap


def newton_start(block, x_ref, t_ref, d_ref):
    d_ref[0], d_ref[1] = split(block)
    top = jnp.maximum(jnp.max(jnp.sum(jnp.abs(block), axis=0, keepdims=True)), LOWEST)
    lead = 2.0 / (top + LOWEST)
    gain, gap = norm_steps((top - LOWEST) / (top + LOWEST))
    rest = 2.0 * identity(block.shape[0]) - lead * block
    x_ref[...] = (gain * lead) * rest
    t_ref[...] = (gain * lead) * mul((d_ref[0], d_ref[1]), split(rest))
    return gap


def newton_step(gap, x_ref, t_ref):
    gain, gap = norm_steps(gap)
    n = x_ref.shape[0]
    rest = split(2.0 * identity(n) - t_ref[...])
    both = mul(split(jnp.concatenate([t_ref[...], x_ref[...]], axis=0)), rest)
    t_ref[...] = gain * both[:n]
    x_ref[...] = gain * both[n:]
    return gap


def newton_finish(gap, x_ref, t_ref, d_ref, noise):
    def more(limit):
        return lambda state: jnp.logical_and(state[1] > limit, state[0] < MAX_STEPS)

    step = lambda state: (state[0] + 1, newton_step(state[1], x_ref, t_ref))
    _, gap = lax.while_loop(more(COARSE_TOL), step, (jnp.int32(0), gap))

    def correct(state):
        x = x_ref[...]
        x_parts = split(x)
        residual = split(identity(x.shape[0]) - mul((d_ref[0], d_ref[1]), x_parts))
        x_ref[...] = x + mul(x_parts, residual)
        return state[0] + 1, state[1] * state[1]

    lax.while_loop(more(TOL), correct, (jnp.int32(0), gap + noise))
    return x_ref[...]


def noise_of(block):
    return jnp.max(jnp.sum(jnp.abs(block), axis=0, keepdims=True)) * NOISE


def newton(block, x_ref, t_ref, d_ref):
    gap = newton_start(block, x_ref, t_ref, d_ref)
    return newton_finish(gap, x_ref, t_ref, d_ref, noise_of(block))


def places():
    core = lax.axis_index("rhs")
    return (
        core,
        pl.ds(pl.multiple_of(core * HALF, HALF), HALF),
        pl.ds(pl.multiple_of(HALF - core * HALF, HALF), HALF),
        pl.ds(pl.multiple_of(core * SHARE, SHARE), SHARE),
        pl.ds(pl.multiple_of(SHARE - core * SHARE, SHARE), SHARE),
    )


def invert(first, cross_block, last_block, out_ref, x_ref, t_ref, d_ref):
    _, mine, other, _, _ = places()
    cross = split(cross_block)
    lift = split(mul(cross, split(first)))
    out_ref[mine, mine] = first
    last = newton(last_block() - mul(lift, cross, NT), x_ref, t_ref, d_ref)
    low = -mul(split(last), lift)
    up = low.T
    out_ref[other, other] = last
    out_ref[other, mine] = low
    out_ref[mine, other] = up
    out_ref[mine, mine] = out_ref[mine, mine] - mul(split(up), lift)


def loads(sems, *pairs):
    copies = [
        pltpu.make_async_copy(source, target, sems.at[index])
        for index, (source, target) in enumerate(pairs)
    ]
    for copy in copies:
        copy.start()
    return copies


def rows(first, second, count=N):
    core = lax.axis_index("rhs")
    return pl.ds(pl.multiple_of(first + core * (second - first), HALF), count)


def remote(source, target, sems, index, device):
    copy = pltpu.make_async_remote_copy(
        src_ref=source,
        dst_ref=target,
        send_sem=sems[0].at[index],
        recv_sem=sems[1].at[index],
        device_id=device,
        device_id_type=MESH,
    )
    copy.start()
    return copy


def greet(*devices):
    barrier = pltpu.get_barrier_semaphore()
    for device in devices:
        pl.semaphore_signal(barrier, inc=1, device_id=device, device_id_type=MESH)
    return lambda: pl.semaphore_wait(barrier, len(devices))


def partners(
    diag, lower, right_side,
    d_own, d_other, g_ref, h_ref, f_ref, d2_own, x_ref, t_ref, gap_ref,
    d_ref, sems, send_sems, recv_sems,
):
    core, mine, other, share, rest = places()
    partner = {"rhs": 1 - core}
    arrived = greet(partner)
    section = rows(N, 3 * N)
    copies = loads(
        sems,
        (diag.at[section], d_own),
        (lower.at[rows(2 * N, 3 * N)], g_ref.at[:, mine]),
        (lower.at[N : 2 * N], h_ref.at[:, mine]),
        (right_side.at[:, section], f_ref.at[share]),
        (diag.at[2 * N : 3 * N], d2_own),
    )
    arrived()
    pair = (send_sems, recv_sems)
    swaps = [
        remote(source, target, pair, index, partner)
        for index, (source, target) in enumerate(
            (
                (diag.at[rows(3 * N, N + HALF, HALF)], d_other),
                (lower.at[rows(3 * N, 2 * N)], g_ref.at[:, mine]),
                (right_side.at[:, rows(3 * N, N)], f_ref.at[share]),
            )
        )
    ]

    def outer():
        return pltpu.make_async_remote_copy(
            src_ref=lower.at[N : 2 * N],
            dst_ref=h_ref.at[:, mine],
            send_sem=send_sems.at[3],
            recv_sem=recv_sems.at[3],
            device_id=partner,
            device_id_type=MESH,
        )

    @pl.when(core == 1)
    def _():
        outer().start()

    copies[0].wait()
    gap = newton_start(d_own[mine], x_ref, t_ref, d_ref)
    gap = lax.fori_loop(0, FIXED_STEPS, lambda _, gap: newton_step(gap, x_ref, t_ref), gap)
    gap_ref[...] = jnp.full(gap_ref.shape, gap, f32)
    for copy in copies[1:]:
        copy.wait()
    for copy in swaps:
        copy.wait()

    @pl.when(core == 0)
    def _():
        outer().wait_recv()

    @pl.when(core == 1)
    def _():
        outer().wait_send()


def level_one(
    d_own, d_other, g_whole, d2_own, first_x, first_t, gap_in,
    inverse_ref, v_ref, send_ref, keep_ref,
    gv_ref, g_ref, x_ref, t_ref, d_ref,
):
    core, mine, other, share, rest = places()
    x_ref[...] = first_x[...]
    t_ref[...] = first_t[...]
    block = d_own[mine]
    d_ref[0], d_ref[1] = split(block)
    first = newton_finish(jnp.max(gap_in[...]), x_ref, t_ref, d_ref, noise_of(block))
    invert(first, d_own[other], lambda: d_other[...], inverse_ref, x_ref, t_ref, d_ref)

    @pl.when(core == 0)
    def _():
        g_ref[...] = g_whole[...]

    @pl.when(core == 1)
    def _():
        g_ref[...] = g_whole[...].T

    g = split(g_ref[...])
    v = mul(split(inverse_ref[...]), g, NT)
    v_ref[...] = v
    gv_ref[...] = mul(g, split(v))
    send_ref[:N] = gv_ref[:, other]
    send_ref[N:] = gv_ref[mine, mine] - d2_own[mine]
    keep_ref[:N] = gv_ref[:, mine]
    keep_ref[N:] = gv_ref[other, other]


def outward(
    inverse_ref, v_ref, send_ref, h_own, f_own, next_left, next_right,
    came_ref, w_ref, z_ref, pack_ref, hw_ref, small_ref,
    h_whole, h_ref, f_ref, send_sems, recv_sems,
):
    core, mine, other, share, rest = places()
    partner = {"rhs": 1 - core}
    greet(partner)()
    swapped = remote(send_ref, came_ref, (send_sems, recv_sems), 0, partner)

    @pl.when(core == 0)
    def _():
        h_ref[...] = h_own[...].T

    @pl.when(core == 1)
    def _():
        h_ref[:, :HALF] = next_left[...]
        h_ref[:, HALF:] = next_right[...]

    h, v = split(h_ref[...]), split(v_ref[...])
    c = -mul(h, v)
    pack_ref[:N] = c[:, :HALF]
    pack_ref[N : 2 * N] = c[:, HALF:]
    inverse = split(inverse_ref[...])
    w = mul(inverse, h, NT)
    w_ref[...] = w
    w = split(w)
    h_whole[...] = mul(h, w)
    hw_ref[...] = h_whole[:, mine]
    pack_ref[2 * N : 3 * N] = h_whole[:, other]
    f = split(f_own[...])
    z_ref[...] = mul(f, inverse)
    for index, term in enumerate((w, v)):
        first = 3 * N + index * RHS
        f_ref[...] = mul(f, term)
        small_ref[index] = f_ref[share]
        pack_ref[first : first + SHARE] = f_ref[rest, :HALF]
        pack_ref[first + SHARE : first + RHS] = f_ref[rest, HALF:]
    swapped.wait()


def level_two(d2_own, keep_ref, came_ref, inverse_ref, d_own, x_ref, t_ref, d_ref):
    core, mine, other, share, rest = places()
    d_own[...] = d2_own[...] - (keep_ref[:N] + came_ref[:N])
    last_block = lambda: -(keep_ref[N:] + came_ref[N:])
    first = newton(d_own[mine], x_ref, t_ref, d_ref)
    invert(first, d_own[other], last_block, inverse_ref, x_ref, t_ref, d_ref)


def survivors(
    inverse_ref, own_ref, came_ref, hw_ref, small_ref,
    diag, right_side, coarse_sol, v_any, w_any, z_any,
    diag_ref, low_out, rhs_ref, solution_ref,
    c_both, hw_both, hz_both, low_send, hops, diag_send, rhs_send, diag_came, cross_came, rhs_came,
    d0, f0, f2, y_ref, v_ref, w_ref, z_ref, y_next, y_send, ys_ref, x2_ref, x_ref, x_both,
    sems, send_sems, recv_sems,
):
    core, mine, other, share, rest = places()
    me = lax.axis_index("tm")
    runs = lax.axis_size("tm")
    after, before = {"tm": lax.rem(me + 1, runs)}, {"tm": lax.rem(me + runs - 1, runs)}
    partner = {"rhs": 1 - core}
    place_x = lax.rem(me, ROW)
    first_x = me - place_x
    left_chip = {"tm": first_x + lax.rem(place_x + ROW - 1, ROW)}
    right_chip = {"tm": first_x + lax.rem(place_x + 1, ROW)}
    row_after = {"tm": lax.rem(me + ROW, runs)}
    row_before = {"tm": lax.rem(me + runs - ROW, runs)}
    arrived = greet(after, before, partner, left_chip, right_chip, row_after, row_before)
    copies = loads(
        sems,
        (right_side.at[:, 2 * N : 3 * N], f2),
        (diag.at[:N], d0),
        (right_side.at[:, :N], f0),
        (coarse_sol, y_ref),
        (v_any, v_ref),
        (w_any, w_ref),
        (z_any, z_ref),
    )
    pair = (send_sems, recv_sems)
    inverse = split(inverse_ref[...])
    for column in range(2):
        span = slice(column * HALF, (column + 1) * HALF)
        c_both[core, :, span] = own_ref[column * N : (column + 1) * N]
        c_both[1 - core, :, span] = came_ref[column * N : (column + 1) * N]
        first = 3 * N + column * SHARE
        hz_both[1 - core, :, span] = came_ref[first : first + SHARE]
        hz_both[2, :, span] = came_ref[first + RHS : first + RHS + SHARE]
    hw_both[core] = hw_ref[...]
    hw_both[1 - core] = came_ref[2 * N : 3 * N]
    hz_both[core] = small_ref[0]
    right = split(c_both[1])
    left = split(c_both[0])
    u_left = split(mul(inverse, split(c_both[0, mine]), NT))
    arrived()
    later = remote(coarse_sol, y_next, pair, 0, before)

    def low_rows(first, count):
        span = slice(first, first + count)
        low_send[span] = -mul((right[0][span], right[1][span]), u_left)

    low_rows(DIRECT, N - DIRECT)
    steps = []
    for chunk in range(2):
        span = pl.ds(DIRECT + chunk * CHUNK, CHUNK)
        steps.append(remote(low_send.at[span], hops.at[0, chunk], pair, 10 + chunk, left_chip))

    u_right = split(mul(inverse, split(c_both[1, mine]), NT))

    def diag_block(place):
        c_rows = split(c_both[1, place])
        return hw_both[1, place] + mul(c_rows, u_right)

    corner = mine

    @pl.when(core == 0)
    def _():
        diag_send[HALF:] = diag_block(slice(HALF, N))
        remote(diag_send.at[HALF:], diag_came.at[HALF:], pair, 1, after)

    diag_send[:HALF] = diag_block(corner)
    square = [
        remote(diag_send.at[span, width], diag_came.at[span, width], pair, index, after)
        for index, span, width in (
            (2, slice(QUARTER, HALF), slice(0, HALF)),
            (9, slice(0, QUARTER), slice(0, QUARTER)),
        )
    ]
    lows = []
    for half in range(2):
        span = pl.ds(half * (DIRECT // 2), DIRECT // 2)
        low_rows(half * (DIRECT // 2), DIRECT // 2)
        lows.append(remote(low_send.at[span], low_out.at[span], pair, 3 + half, after))
    copies[0].wait()
    z2 = mul(split(f2[...] - (small_ref[1] + hz_both[2])), inverse)
    z2_parts = split(z2)
    rhs_send[...] = hz_both[1] + mul(z2_parts, right, NT)
    rhs_sent = remote(rhs_send, rhs_came, pair, 5, after)

    for copy in copies[1:4]:
        copy.wait()
    diag_ref[...] = d0[...] - hw_both[0] - mul(left, u_left)
    rhs_ref[...] = f0[...] - hz_both[0] - mul(z2_parts, left, NT)

    def forward(hop):
        for chunk in range(2):
            steps[2 * hop + chunk].wait_recv()
            steps.append(
                remote(
                    hops.at[hop, chunk], hops.at[hop + 1, chunk], pair,
                    12 + 2 * hop + chunk, left_chip,
                )
            )

    forward(0)
    later.wait_recv()

    @pl.when(core == 0)
    def _():
        y_send[...] = y_next[...]
        ys_ref[0] = y_ref[...]

    @pl.when(core == 1)
    def _():
        y_send[...] = y_ref[...]
        ys_ref[0] = y_next[...]

    swap_y = remote(y_send, ys_ref.at[1], pair, 6, partner)
    known = mul(split(y_ref[...]), left) + mul(split(y_next[...]), right)
    x2_ref[0] = z2 - mul(split(known), inverse)
    swap_x2 = remote(x2_ref.at[0], x2_ref.at[1], pair, 7, partner)
    for copy in copies[4:]:
        copy.wait()
    forward(1)
    swap_y.wait_recv()
    swap_x2.wait_recv()
    v, w = split(v_ref[...]), split(w_ref[...])
    for slot, place in ((1, rest), (0, share)):
        x_ref[slot] = (
            z_ref[place]
            - mul(split(ys_ref[slot]), w, NT)
            - mul(split(x2_ref[slot]), v, NT)
        )
        if slot == 1:
            swap_x = remote(x_ref.at[1], x_both, pair, 8, partner)
    solution_ref[:, :N] = y_ref[...]
    solution_ref[:, 2 * N : 3 * N] = x2_ref[0]
    swap_x.wait_recv()

    @pl.when(core == 0)
    def _():
        solution_ref[:, N : 2 * N] = x_ref[0]
        solution_ref[:, 3 * N :] = x_both[...]

    @pl.when(core == 1)
    def _():
        solution_ref[:, N : 2 * N] = x_both[...]
        solution_ref[:, 3 * N :] = x_ref[0]

    def crossing(device):
        return pltpu.make_async_remote_copy(
            src_ref=diag_send.at[HALF:],
            dst_ref=diag_came.at[HALF:],
            send_sem=send_sems.at[1],
            recv_sem=recv_sems.at[1],
            device_id=device,
            device_id_type=MESH,
        )

    def handing():
        return pltpu.make_async_remote_copy(
            src_ref=diag_came.at[HALF:],
            dst_ref=cross_came,
            send_sem=send_sems.at[18],
            recv_sem=recv_sems.at[18],
            device_id=partner,
            device_id_type=MESH,
        )

    @pl.when(core == 0)
    def _():
        crossing(after).wait_recv()
        handing().start()
        diag_ref[HALF:] = diag_ref[HALF:] - diag_came[HALF:]

    def turn(chunk):
        return pltpu.make_async_remote_copy(
            src_ref=hops.at[2, chunk],
            dst_ref=hops.at[3, chunk],
            send_sem=send_sems.at[16 + chunk],
            recv_sem=recv_sems.at[16 + chunk],
            device_id=row_after,
            device_id_type=MESH,
        )

    for chunk in range(2):
        steps[4 + chunk].wait_recv()

        @pl.when(place_x == 0)
        def _():
            turn(chunk).start()

    for copy in square:
        copy.wait_recv()
    diag_came[:QUARTER, QUARTER:] = diag_came[QUARTER:HALF, :QUARTER].T
    diag_ref[corner] = diag_ref[corner] - diag_came[:HALF]

    @pl.when(core == 1)
    def _():
        handing().wait_recv()
        diag_ref[:HALF] = diag_ref[:HALF] - cross_came[...].T

    for chunk in range(2):
        span = pl.ds(DIRECT + chunk * CHUNK, CHUNK)

        @pl.when(place_x == 0)
        def _():
            turn(chunk).wait_recv()
            low_out[span] = hops[3, chunk]

        @pl.when(place_x != 0)
        def _():
            low_out[span] = hops[2, chunk]

    rhs_sent.wait_recv()
    rhs_ref[...] = rhs_ref[...] - rhs_came[...]
    for copy in lows:
        copy.wait_recv()
    for copy in (later, *square, *lows, rhs_sent, swap_y, swap_x2, swap_x, *steps):
        copy.wait_send()

    @pl.when(place_x == 0)
    def _():
        for chunk in range(2):
            turn(chunk).wait_send()

    @pl.when(core == 0)
    def _():
        crossing(after).wait_send()
        handing().wait_send()


def deliver(*refs):
    count = (len(refs) - 1) // 2
    for copy in loads(refs[-1], *zip(refs[:count], refs[count : 2 * count])):
        copy.wait()


def shape(*dims):
    return jax.ShapeDtypeStruct(dims, f32)


def call(body, in_specs, outs, out_specs, scratch, flops, args, limit, **params):
    size = sum(a.size for a in args) + sum(o.size for o in outs)
    return pl.pallas_call(
        body,
        out_shape=outs,
        in_specs=in_specs,
        out_specs=out_specs,
        scratch_shapes=scratch,
        compiler_params=pltpu.CompilerParams(vmem_limit_bytes=limit << 20, **params),
        cost_estimate=pl.CostEstimate(flops=flops, bytes_accessed=4 * size, transcendentals=0),
    )(*args)


def newton_scratch():
    return [pltpu.VMEM((HALF, HALF), f32)] * 2 + [pltpu.VMEM((2, HALF, HALF), bf16)]


def copy_sems(count):
    return pltpu.SemaphoreType.DMA((count,))


def shards(diag, lower, right_side, coarse_sol):
    runs = lax.axis_size("tm")
    sent_first = lower[:N]
    diag, lower, right_side, coarse_sol = (
        pltpu.with_memory_space_constraint(array, pltpu.HBM)
        for array in (diag, lower, right_side, coarse_sol)
    )
    next_left, next_right = (
        lax.ppermute(
            sent_first,
            ("tm", "rhs"),
            [(2 * ((i + 1) % runs) + source, 2 * i + 1) for i in range(runs)],
        )
        for source in (0, 1)
    )
    swap = lambda x: lax.ppermute(x, "rhs", [(0, 1), (1, 0)])
    full, half, quarter = (N, N), (N, HALF), (HALF, HALF)
    small, scratch = (SHARE, N), lambda *dims: pltpu.VMEM(dims, f32)
    d_own, d_other, g, h, f, d2_own, first_x, first_t, gap = call(
        partners,
        [HBM] * 3,
        [shape(*half), shape(*quarter), shape(*full), shape(*full), shape(RHS, N), shape(*half),
         shape(*quarter), shape(*quarter), shape(8, 128)],
        [VMEM] * 9,
        [pltpu.VMEM((2, HALF, HALF), bf16), copy_sems(5), copy_sems(4), copy_sems(4)],
        2 * HALF**3 * 30,
        (diag, lower, right_side),
        16,
        collective_id=1,
        has_side_effects=True,
    )
    inverse, v, send, keep = call(
        level_one,
        [VMEM] * 7,
        [shape(*full), shape(*full), shape(N + HALF, HALF), shape(N + HALF, HALF)],
        [VMEM] * 4,
        [scratch(*full), scratch(*full)] + newton_scratch(),
        2 * N**3 * 20,
        (d_own, d_other, g, d2_own, first_x, first_t, gap),
        28,
    )
    came, w, z, pack, hw, tails = call(
        outward,
        [VMEM] * 2 + [ANY] + [VMEM] * 4,
        [shape(N + HALF, HALF), shape(*full), shape(RHS, N), shape(3 * N + 2 * RHS, HALF),
         shape(*half), shape(2, *small)],
        [ANY] + [VMEM] * 5,
        [scratch(*full), scratch(*full), scratch(RHS, N), copy_sems(1), copy_sems(1)],
        2 * N**3 * 10,
        (inverse, v, send, h, f, next_left, next_right),
        28,
        collective_id=3,
        has_side_effects=True,
    )
    pack_came = swap(pack)
    inverse2 = call(
        level_two,
        [VMEM] * 3,
        [shape(*full)],
        [VMEM],
        [scratch(*half)] + newton_scratch(),
        2 * N**3 * 20,
        (d2_own, keep, came),
        28,
    )[0]
    finals = [shape(*half), shape(*half), shape(*small), shape(SHARE, 4 * N)]
    results = call(
        survivors,
        [VMEM] * 5 + [HBM] * 3 + [ANY] * 3,
        finals,
        [VMEM] * 4,
        [scratch(2, *full), scratch(2, *half), scratch(3, *small),
         scratch(*half), scratch(4, 2, CHUNK, HALF), scratch(*half), scratch(*small),
         scratch(*half), scratch(*quarter), scratch(*small),
         scratch(*half), scratch(*small), scratch(*small), scratch(*small),
         scratch(*full), scratch(*full), scratch(RHS, N),
         scratch(*small), scratch(*small), scratch(2, *small),
         scratch(2, *small), scratch(2, *small), scratch(*small),
         copy_sems(7), copy_sems(19), copy_sems(19)],
        2 * N**3 * 9,
        (inverse2, pack, pack_came, hw, tails, diag, right_side, coarse_sol, v, w, z),
        40,
        collective_id=2,
        has_side_effects=True,
    )
    return call(
        deliver, [ANY] * 4, finals, [HBM] * 4, [copy_sems(4)], 0, tuple(results), 8
    )


def solution(mesh):
    return jax.shard_map(
        shards,
        mesh=mesh,
        in_specs=(P("tm", "rhs"), P("tm", "rhs"), P("rhs", "tm"), P("rhs", "tm")),
        out_specs=(P("tm", "rhs"), P("tm", "rhs"), P("rhs", "tm"), P("rhs", "tm")),
        check_vma=False,
    )
```

```python
import functools

import jax
import jax.numpy as jnp
from jax import lax
from jax.experimental import pallas as pl
from jax.experimental.pallas import tpu as pltpu
from jax.sharding import PartitionSpec as P

f32, bf16 = jnp.float32, jnp.bfloat16
N = 512
HALF = 256
RHS = 128
SHARE = 64
QUARTER = 128
ROW = 4
DIRECT = 320
CHUNK = 96
LOWEST = 2.0
TOL = 4e-6
COARSE_TOL = 1.6e-3
NOISE = 2e-6
FIXED_STEPS = 4
MAX_STEPS = 40
VMEM = pl.BlockSpec(memory_space=pltpu.VMEM)
ANY = pl.BlockSpec(memory_space=pl.ANY)
HBM = pl.BlockSpec(memory_space=pltpu.HBM)
MESH = pl.DeviceIdType.MESH
NN = (((1,), (0,)), ((), ()))
NT = (((1,), (1,)), ((), ()))


def split(x):
    high = x.astype(bf16)
    return high, (x - high.astype(f32)).astype(bf16)


def mul(a, b, dims=NN):
    one = lambda p, q: lax.dot_general(p, q, dims, preferred_element_type=f32)
    return one(a[0], b[0]) + (one(a[0], b[1]) + one(a[1], b[0]))


def identity(n):
    return (
        lax.broadcasted_iota(jnp.int32, (n, n), 0) == lax.broadcasted_iota(jnp.int32, (n, n), 1)
    ).astype(f32)


def norm_steps(gap):
    gain = 2.0 / (2.0 - gap * gap)
    return gain, 0.5 * gain * gap * gap


def newton_start(block, x_ref, t_ref, d_ref):
    d_ref[0], d_ref[1] = split(block)
    top = jnp.maximum(jnp.max(jnp.sum(jnp.abs(block), axis=0, keepdims=True)), LOWEST)
    lead = 2.0 / (top + LOWEST)
    gain, gap = norm_steps((top - LOWEST) / (top + LOWEST))
    rest = 2.0 * identity(block.shape[0]) - lead * block
    x_ref[...] = (gain * lead) * rest
    t_ref[...] = (gain * lead) * mul((d_ref[0], d_ref[1]), split(rest))
    return gap


def newton_step(gap, x_ref, t_ref):
    gain, gap = norm_steps(gap)
    n = x_ref.shape[0]
    rest = split(2.0 * identity(n) - t_ref[...])
    both = mul(split(jnp.concatenate([t_ref[...], x_ref[...]], axis=0)), rest)
    t_ref[...] = gain * both[:n]
    x_ref[...] = gain * both[n:]
    return gap


def newton_finish(gap, x_ref, t_ref, d_ref, noise):
    def more(limit):
        return lambda state: jnp.logical_and(state[1] > limit, state[0] < MAX_STEPS)

    step = lambda state: (state[0] + 1, newton_step(state[1], x_ref, t_ref))
    _, gap = lax.while_loop(more(COARSE_TOL), step, (jnp.int32(0), gap))

    def correct(state):
        x = x_ref[...]
        x_parts = split(x)
        residual = split(identity(x.shape[0]) - mul((d_ref[0], d_ref[1]), x_parts))
        x_ref[...] = x + mul(x_parts, residual)
        return state[0] + 1, state[1] * state[1]

    lax.while_loop(more(TOL), correct, (jnp.int32(0), gap + noise))
    return x_ref[...]


def noise_of(block):
    return jnp.max(jnp.sum(jnp.abs(block), axis=0, keepdims=True)) * NOISE


def newton(block, x_ref, t_ref, d_ref):
    gap = newton_start(block, x_ref, t_ref, d_ref)
    return newton_finish(gap, x_ref, t_ref, d_ref, noise_of(block))


def places():
    core = lax.axis_index("rhs")
    return (
        core,
        pl.ds(pl.multiple_of(core * HALF, HALF), HALF),
        pl.ds(pl.multiple_of(HALF - core * HALF, HALF), HALF),
        pl.ds(pl.multiple_of(core * SHARE, SHARE), SHARE),
        pl.ds(pl.multiple_of(SHARE - core * SHARE, SHARE), SHARE),
    )


def invert(first, cross_block, last_block, out_ref, x_ref, t_ref, d_ref):
    _, mine, other, _, _ = places()
    cross = split(cross_block)
    lift = split(mul(cross, split(first)))
    out_ref[mine, mine] = first
    last = newton(last_block() - mul(lift, cross, NT), x_ref, t_ref, d_ref)
    low = -mul(split(last), lift)
    up = low.T
    out_ref[other, other] = last
    out_ref[other, mine] = low
    out_ref[mine, other] = up
    out_ref[mine, mine] = out_ref[mine, mine] - mul(split(up), lift)


def loads(sems, *pairs):
    copies = [
        pltpu.make_async_copy(source, target, sems.at[index])
        for index, (source, target) in enumerate(pairs)
    ]
    for copy in copies:
        copy.start()
    return copies


def rows(first, second, count=N):
    core = lax.axis_index("rhs")
    return pl.ds(pl.multiple_of(first + core * (second - first), HALF), count)


def remote(source, target, sems, index, device):
    copy = pltpu.make_async_remote_copy(
        src_ref=source,
        dst_ref=target,
        send_sem=sems[0].at[index],
        recv_sem=sems[1].at[index],
        device_id=device,
        device_id_type=MESH,
    )
    copy.start()
    return copy


def greet(*devices):
    barrier = pltpu.get_barrier_semaphore()
    for device in devices:
        pl.semaphore_signal(barrier, inc=1, device_id=device, device_id_type=MESH)
    return lambda: pl.semaphore_wait(barrier, len(devices))


def partners(
    diag, lower, right_side,
    d_own, d_other, g_ref, h_ref, f_ref, d2_own, x_ref, t_ref, gap_ref,
    d_ref, sems, send_sems, recv_sems,
):
    core, mine, other, share, rest = places()
    partner = {"rhs": 1 - core}
    arrived = greet(partner)
    section = rows(N, 3 * N)
    copies = loads(
        sems,
        (diag.at[section], d_own),
        (lower.at[rows(2 * N, 3 * N)], g_ref.at[:, mine]),
        (lower.at[N : 2 * N], h_ref.at[:, mine]),
        (right_side.at[:, section], f_ref.at[share]),
        (diag.at[2 * N : 3 * N], d2_own),
    )
    arrived()
    pair = (send_sems, recv_sems)
    swaps = [
        remote(source, target, pair, index, partner)
        for index, (source, target) in enumerate(
            (
                (diag.at[rows(3 * N, N + HALF, HALF)], d_other),
                (lower.at[rows(3 * N, 2 * N)], g_ref.at[:, mine]),
                (right_side.at[:, rows(3 * N, N)], f_ref.at[share]),
            )
        )
    ]

    def outer():
        return pltpu.make_async_remote_copy(
            src_ref=lower.at[N : 2 * N],
            dst_ref=h_ref.at[:, mine],
            send_sem=send_sems.at[3],
            recv_sem=recv_sems.at[3],
            device_id=partner,
            device_id_type=MESH,
        )

    @pl.when(core == 1)
    def _():
        outer().start()

    copies[0].wait()
    gap = newton_start(d_own[mine], x_ref, t_ref, d_ref)
    gap = lax.fori_loop(0, FIXED_STEPS, lambda _, gap: newton_step(gap, x_ref, t_ref), gap)
    gap_ref[...] = jnp.full(gap_ref.shape, gap, f32)
    for copy in copies[1:]:
        copy.wait()
    for copy in swaps:
        copy.wait()

    @pl.when(core == 0)
    def _():
        outer().wait_recv()

    @pl.when(core == 1)
    def _():
        outer().wait_send()


def level_one(
    d_own, d_other, g_whole, d2_own, first_x, first_t, gap_in,
    inverse_ref, v_ref, send_ref, keep_ref,
    gv_ref, g_ref, x_ref, t_ref, d_ref,
):
    core, mine, other, share, rest = places()
    x_ref[...] = first_x[...]
    t_ref[...] = first_t[...]
    block = d_own[mine]
    d_ref[0], d_ref[1] = split(block)
    first = newton_finish(jnp.max(gap_in[...]), x_ref, t_ref, d_ref, noise_of(block))
    invert(first, d_own[other], lambda: d_other[...], inverse_ref, x_ref, t_ref, d_ref)

    @pl.when(core == 0)
    def _():
        g_ref[...] = g_whole[...]

    @pl.when(core == 1)
    def _():
        g_ref[...] = g_whole[...].T

    g = split(g_ref[...])
    v = mul(split(inverse_ref[...]), g, NT)
    v_ref[...] = v
    gv_ref[...] = mul(g, split(v))
    send_ref[:N] = gv_ref[:, other]
    send_ref[N:] = gv_ref[mine, mine] - d2_own[mine]
    keep_ref[:N] = gv_ref[:, mine]
    keep_ref[N:] = gv_ref[other, other]


def outward(
    inverse_ref, v_ref, send_ref, h_ref, f_own,
    came_ref, ht_ref, z_ref, pack_ref, corner_ref, small_ref,
    c_ref, f_ref, send_sems, recv_sems,
):
    core, mine, other, share, rest = places()
    partner = {"rhs": 1 - core}
    greet(partner)()
    swapped = remote(send_ref, came_ref, (send_sems, recv_sems), 0, partner)
    v, inverse = split(v_ref[...]), split(inverse_ref[...])
    z = mul(split(f_own[...]), inverse)
    z_ref[...] = z

    def stack(place, first):
        small_ref[place] = f_ref[share]
        pack_ref[first : first + SHARE] = f_ref[rest, :HALF]
        pack_ref[first + SHARE : first + RHS] = f_ref[rest, HALF:]

    @pl.when(core == 0)
    def _():
        ht_ref[...] = h_ref[...].T
        c_ref[...] = -mul(split(ht_ref[...]), v)
        f_ref[...] = mul(split(z), split(h_ref[...]))

    @pl.when(core == 1)
    def _():
        c_ref[...] = -v_ref[...]
        corner_ref[...] = inverse_ref[:, mine]
        pack_ref[2 * N : 3 * N] = inverse_ref[:, other]
        f_ref[...] = z

    pack_ref[:N] = c_ref[:, :HALF]
    pack_ref[N : 2 * N] = c_ref[:, HALF:]
    stack(0, 3 * N)
    f_ref[...] = mul(split(f_own[...]), v)
    stack(1, 3 * N + RHS)
    swapped.wait()


def level_two(d2_own, keep_ref, came_ref, inverse_ref, d_own, x_ref, t_ref, d_ref):
    core, mine, other, share, rest = places()
    d_own[...] = d2_own[...] - (keep_ref[:N] + came_ref[:N])
    last_block = lambda: -(keep_ref[N:] + came_ref[N:])
    first = newton(d_own[mine], x_ref, t_ref, d_ref)
    invert(first, d_own[other], last_block, inverse_ref, x_ref, t_ref, d_ref)


def survivors(
    inverse_ref, own_ref, came_ref, hw_ref, small_ref, first_inverse, v_ref, z_ref, h_ref, ht_ref,
    diag, lower, right_side, coarse_sol,
    diag_ref, low_out, rhs_ref, solution_ref,
    c_both, hw_next, hz_both, low_send, low_came, hops, diag_send, rhs_send, diag_came, cross_came,
    corner_came, m_ref, n_ref, hw_own, hw_came, rhs_came,
    d0, f0, f2, y_ref, y_next, y_back, y_send, ys_ref, x2_ref, x_ref, x_both,
    sems, send_sems, recv_sems,
):
    core, mine, other, share, rest = places()
    me = lax.axis_index("tm")
    runs = lax.axis_size("tm")
    after, before = {"tm": lax.rem(me + 1, runs)}, {"tm": lax.rem(me + runs - 1, runs)}
    partner = {"rhs": 1 - core}
    place_x = lax.rem(me, ROW)
    first_x = me - place_x
    left_chip = {"tm": first_x + lax.rem(place_x + ROW - 1, ROW)}
    right_chip = {"tm": first_x + lax.rem(place_x + 1, ROW)}
    row_after = {"tm": lax.rem(me + ROW, runs)}
    row_before = {"tm": lax.rem(me + runs - ROW, runs)}
    arrived = greet(after, before, partner, left_chip, right_chip, row_after, row_before)
    copies = loads(
        sems,
        (right_side.at[:, 2 * N : 3 * N], f2),
        (lower.at[:N], n_ref.at[:, mine]),
        (coarse_sol, y_ref),
        (diag.at[:N], d0),
        (right_side.at[:, :N], f0),
    )
    pair = (send_sems, recv_sems)
    inverse = split(inverse_ref[...])
    for column in range(2):
        span = slice(column * HALF, (column + 1) * HALF)
        c_both[core, :, span] = own_ref[column * N : (column + 1) * N]
        c_both[1 - core, :, span] = came_ref[column * N : (column + 1) * N]
        first = 3 * N + column * SHARE
        hz_both[1 - core, :, span] = came_ref[first : first + SHARE]
        hz_both[2, :, span] = came_ref[first + RHS : first + RHS + SHARE]

    @pl.when(core == 0)
    def _():
        hw_next[...] = came_ref[2 * N : 3 * N]

    @pl.when(core == 1)
    def _():
        hw_next[...] = hw_ref[...]

    hz_both[core] = small_ref[0]
    right = split(c_both[1])
    left = split(c_both[0])
    u_left = split(mul(inverse, split(c_both[0, mine]), NT))
    arrived()

    def low_rows(first, count):
        span = slice(first, first + count)
        low_send[span] = -mul((right[0][span], right[1][span]), u_left)

    low_rows(DIRECT, N - DIRECT)
    steps = []
    for chunk in range(2):
        span = pl.ds(DIRECT + chunk * CHUNK, CHUNK)
        steps.append(remote(low_send.at[span], hops.at[0, chunk], pair, 10 + chunk, left_chip))

    u_right = split(mul(inverse, split(c_both[1, mine]), NT))

    def diag_block(place):
        c_rows = split(c_both[1, place])
        return hw_next[place] + mul(c_rows, u_right)

    corner = mine

    @pl.when(core == 0)
    def _():
        diag_send[HALF:] = diag_block(slice(HALF, N))
        remote(diag_send.at[HALF:], diag_came.at[HALF:], pair, 1, after)

    diag_send[:HALF] = diag_block(corner)
    square = [
        remote(diag_send.at[span, width], diag_came.at[span, width], pair, index, after)
        for index, span, width in (
            (2, slice(QUARTER, HALF), slice(0, HALF)),
            (9, slice(0, QUARTER), slice(0, QUARTER)),
        )
    ]
    lows = []
    for index, (first, count) in enumerate(((0, HALF), (HALF, DIRECT - HALF))):
        span = pl.ds(first, count)
        low_rows(first, count)
        lows.append(remote(low_send.at[span], low_came.at[span], pair, 3 + index, after))
    swap_n = remote(lower.at[:N], n_ref.at[:, mine], pair, 19, partner)
    copies[0].wait()
    z2 = mul(split(f2[...] - (small_ref[1] + hz_both[2])), inverse)
    z2_parts = split(z2)
    rhs_send[...] = hz_both[1] + mul(z2_parts, right, NT)
    rhs_sent = remote(rhs_send, rhs_came, pair, 5, after)

    copies[1].wait()
    copies[2].wait()
    swap_n.wait_recv()
    n = split(n_ref[...])
    y = split(y_ref[...])
    y_back[...] = mul(y, n)
    later = remote(y_back, y_next, pair, 0, before)

    def forward(hop):
        for chunk in range(2):
            steps[2 * hop + chunk].wait_recv()
            steps.append(
                remote(
                    hops.at[hop, chunk], hops.at[hop + 1, chunk], pair,
                    12 + 2 * hop + chunk, left_chip,
                )
            )

    forward(0)

    def half_of_own():
        return pltpu.make_async_remote_copy(
            src_ref=hw_own.at[:, HALF:],
            dst_ref=hw_came,
            send_sem=send_sems.at[20],
            recv_sem=recv_sems.at[20],
            device_id=partner,
            device_id_type=MESH,
        )

    @pl.when(core == 0)
    def _():
        w = split(mul(split(first_inverse[...]), split(h_ref[...])))
        hw_own[...] = mul(split(ht_ref[...]), w)
        half_of_own().start()
        hw_came[...] = hw_own[:, :HALF]

    forward(1)
    later.wait_recv()

    @pl.when(core == 0)
    def _():
        y_send[...] = y_next[...]
        ys_ref[0] = y_ref[...]

    @pl.when(core == 1)
    def _():
        y_send[...] = y_ref[...]
        ys_ref[0] = y_next[...]

    swap_y = remote(y_send, ys_ref.at[1], pair, 6, partner)
    known = mul(y, left) + mul(split(y_next[...]), right)
    x2_ref[0] = z2 - mul(split(known), inverse)
    swap_x2 = remote(x2_ref.at[0], x2_ref.at[1], pair, 7, partner)

    for copy in copies[3:]:
        copy.wait()

    @pl.when(core == 1)
    def _():
        half_of_own().wait_recv()

    diag_ref[...] = d0[...] - hw_came[...] - mul(left, u_left)
    rhs_ref[...] = f0[...] - hz_both[0] - mul(z2_parts, left, NT)

    def turn(chunk):
        return pltpu.make_async_remote_copy(
            src_ref=hops.at[2, chunk],
            dst_ref=hops.at[3, chunk],
            send_sem=send_sems.at[16 + chunk],
            recv_sem=recv_sems.at[16 + chunk],
            device_id=row_after,
            device_id_type=MESH,
        )

    for chunk in range(2):
        steps[4 + chunk].wait_recv()

        @pl.when(place_x == 0)
        def _():
            turn(chunk).start()

    def crossing(device):
        return pltpu.make_async_remote_copy(
            src_ref=diag_send.at[HALF:],
            dst_ref=diag_came.at[HALF:],
            send_sem=send_sems.at[1],
            recv_sem=recv_sems.at[1],
            device_id=device,
            device_id_type=MESH,
        )

    def handing():
        return pltpu.make_async_remote_copy(
            src_ref=diag_came.at[HALF:],
            dst_ref=cross_came,
            send_sem=send_sems.at[18],
            recv_sem=recv_sems.at[18],
            device_id=partner,
            device_id_type=MESH,
        )

    @pl.when(core == 0)
    def _():
        crossing(after).wait_recv()
        handing().start()

    for copy in square:
        copy.wait_recv()
    diag_came[:QUARTER, QUARTER:HALF] = diag_came[QUARTER:HALF, :QUARTER].T
    swap_corner = remote(diag_came.at[:HALF], corner_came, pair, 21, partner)

    swap_y.wait_recv()
    swap_x2.wait_recv()

    @pl.when(core == 0)
    def _():
        for slot in range(2):
            ys_ref[slot] = mul(split(ys_ref[slot]), split(h_ref[...]), NT)

    v, w = split(v_ref[...]), split(first_inverse[...])
    for slot, place in ((1, rest), (0, share)):
        x_ref[slot] = (
            z_ref[place] - mul(split(ys_ref[slot]), w) - mul(split(x2_ref[slot]), v, NT)
        )
        if slot == 1:
            swap_x = remote(x_ref.at[1], x_both, pair, 8, partner)
    solution_ref[:, :N] = y_ref[...]
    solution_ref[:, 2 * N : 3 * N] = x2_ref[0]

    m_ref[mine, mine] = diag_came[:HALF]
    swap_corner.wait_recv()
    m_ref[other, other] = corner_came[...]

    @pl.when(core == 0)
    def _():
        m_ref[HALF:, :HALF] = diag_came[HALF:]

    @pl.when(core == 1)
    def _():
        handing().wait_recv()
        m_ref[HALF:, :HALF] = cross_came[...]

    m_ref[:HALF, HALF:] = m_ref[HALF:, :HALF].T
    applied = split(mul(split(m_ref[...]), split(n_ref[mine]), NT))
    diag_ref[...] = diag_ref[...] - mul(n, applied)
    swap_x.wait_recv()

    @pl.when(core == 0)
    def _():
        solution_ref[:, N : 2 * N] = x_ref[0]
        solution_ref[:, 3 * N :] = x_both[...]

    @pl.when(core == 1)
    def _():
        solution_ref[:, N : 2 * N] = x_both[...]
        solution_ref[:, 3 * N :] = x_ref[0]

    lows[0].wait_recv()
    low_out[...] = mul(split(n_ref[:, :HALF]), split(low_came[:HALF]))
    rhs_sent.wait_recv()
    rhs_ref[...] = rhs_ref[...] - mul(split(rhs_came[...]), n, NT)
    lows[1].wait_recv()
    for chunk in range(2):
        span = pl.ds(DIRECT + chunk * CHUNK, CHUNK)

        @pl.when(place_x == 0)
        def _():
            turn(chunk).wait_recv()
            low_came[span] = hops[3, chunk]

        @pl.when(place_x != 0)
        def _():
            low_came[span] = hops[2, chunk]

    low_out[...] = low_out[...] + mul(split(n_ref[:, HALF:]), split(low_came[HALF:]))
    for copy in (
        later, *square, *lows, rhs_sent, swap_y, swap_x2, swap_x, swap_n, swap_corner, *steps
    ):
        copy.wait_send()

    @pl.when(place_x == 0)
    def _():
        for chunk in range(2):
            turn(chunk).wait_send()

    @pl.when(core == 0)
    def _():
        crossing(after).wait_send()
        handing().wait_send()
        half_of_own().wait_send()


def deliver(*refs):
    count = (len(refs) - 1) // 2
    for copy in loads(refs[-1], *zip(refs[:count], refs[count : 2 * count])):
        copy.wait()


def shape(*dims):
    return jax.ShapeDtypeStruct(dims, f32)


def call(body, in_specs, outs, out_specs, scratch, flops, args, limit, **params):
    size = sum(a.size for a in args) + sum(o.size for o in outs)
    return pl.pallas_call(
        body,
        out_shape=outs,
        in_specs=in_specs,
        out_specs=out_specs,
        scratch_shapes=scratch,
        compiler_params=pltpu.CompilerParams(vmem_limit_bytes=limit << 20, **params),
        cost_estimate=pl.CostEstimate(flops=flops, bytes_accessed=4 * size, transcendentals=0),
    )(*args)


def newton_scratch():
    return [pltpu.VMEM((HALF, HALF), f32)] * 2 + [pltpu.VMEM((2, HALF, HALF), bf16)]


def copy_sems(count):
    return pltpu.SemaphoreType.DMA((count,))


def shards(diag, lower, right_side, coarse_sol):
    diag, lower, right_side, coarse_sol = (
        pltpu.with_memory_space_constraint(array, pltpu.HBM)
        for array in (diag, lower, right_side, coarse_sol)
    )
    swap = lambda x: lax.ppermute(x, "rhs", [(0, 1), (1, 0)])
    full, half, quarter = (N, N), (N, HALF), (HALF, HALF)
    small, scratch = (SHARE, N), lambda *dims: pltpu.VMEM(dims, f32)
    d_own, d_other, g, h, f, d2_own, first_x, first_t, gap = call(
        partners,
        [HBM] * 3,
        [shape(*half), shape(*quarter), shape(*full), shape(*full), shape(RHS, N), shape(*half),
         shape(*quarter), shape(*quarter), shape(8, 128)],
        [VMEM] * 9,
        [pltpu.VMEM((2, HALF, HALF), bf16), copy_sems(5), copy_sems(4), copy_sems(4)],
        2 * HALF**3 * 30,
        (diag, lower, right_side),
        16,
        collective_id=1,
        has_side_effects=True,
    )
    inverse, v, send, keep = call(
        level_one,
        [VMEM] * 7,
        [shape(*full), shape(*full), shape(N + HALF, HALF), shape(N + HALF, HALF)],
        [VMEM] * 4,
        [scratch(*full), scratch(*full)] + newton_scratch(),
        2 * N**3 * 20,
        (d_own, d_other, g, d2_own, first_x, first_t, gap),
        28,
    )
    came, ht, z, pack, hw, tails = call(
        outward,
        [VMEM] * 2 + [ANY] + [VMEM] * 2,
        [shape(N + HALF, HALF), shape(*full), shape(RHS, N), shape(3 * N + 2 * RHS, HALF),
         shape(*half), shape(2, *small)],
        [ANY] + [VMEM] * 5,
        [scratch(*full), scratch(RHS, N), copy_sems(1), copy_sems(1)],
        2 * N**3 * 6,
        (inverse, v, send, h, f),
        28,
        collective_id=3,
        has_side_effects=True,
    )
    pack_came = swap(pack)
    inverse2 = call(
        level_two,
        [VMEM] * 3,
        [shape(*full)],
        [VMEM],
        [scratch(*half)] + newton_scratch(),
        2 * N**3 * 20,
        (d2_own, keep, came),
        28,
    )[0]
    finals = [shape(*half), shape(*half), shape(*small), shape(SHARE, 4 * N)]
    results = call(
        survivors,
        [VMEM] * 10 + [HBM] * 4,
        finals,
        [VMEM] * 4,
        [scratch(2, *full), scratch(*half), scratch(3, *small), scratch(*half), scratch(*half),
         scratch(4, 2, CHUNK, HALF), scratch(*half), scratch(*small), scratch(*half),
         scratch(*quarter),
         scratch(*quarter), scratch(*full), scratch(*full), scratch(*full), scratch(*half),
         scratch(*small),
         scratch(*half), scratch(*small), scratch(*small), scratch(*small), scratch(*small),
         scratch(*small), scratch(*small), scratch(2, *small), scratch(2, *small),
         scratch(2, *small), scratch(*small),
         copy_sems(5), copy_sems(22), copy_sems(22)],
        2 * N**3 * 9,
        (inverse2, pack, pack_came, hw, tails, inverse, v, z, h, ht,
         diag, lower, right_side, coarse_sol),
        40,
        collective_id=2,
        has_side_effects=True,
    )
    return call(
        deliver, [ANY] * 4, finals, [HBM] * 4, [copy_sems(4)], 0, tuple(results), 8
    )


def solution(mesh):
    return jax.shard_map(
        shards,
        mesh=mesh,
        in_specs=(P("tm", "rhs"), P("tm", "rhs"), P("rhs", "tm"), P("rhs", "tm")),
        out_specs=(P("tm", "rhs"), P("tm", "rhs"), P("rhs", "tm"), P("rhs", "tm")),
        check_vma=False,
    )
```

```python
import functools

import jax
import jax.numpy as jnp
from jax import lax
from jax.experimental import pallas as pl
from jax.experimental.pallas import tpu as pltpu
from jax.sharding import PartitionSpec as P

f32, bf16 = jnp.float32, jnp.bfloat16
N = 512
HALF = 256
RHS = 128
SHARE = 64
QUARTER = 128
ROW = 4
DIRECT = 320
CHUNKS = 3
CHUNK = 64
LOWEST = 2.0
TOL = 2e-5
COARSE_TOL = 4e-3
NOISE = 2e-6
FIXED_STEPS = 4
MAX_STEPS = 40
VMEM = pl.BlockSpec(memory_space=pltpu.VMEM)
ANY = pl.BlockSpec(memory_space=pl.ANY)
HBM = pl.BlockSpec(memory_space=pltpu.HBM)
MESH = pl.DeviceIdType.MESH
NN = (((1,), (0,)), ((), ()))
NT = (((1,), (1,)), ((), ()))


def split(x):
    high = x.astype(bf16)
    return high, (x - high.astype(f32)).astype(bf16)


def mul(a, b, dims=NN):
    one = lambda p, q: lax.dot_general(p, q, dims, preferred_element_type=f32)
    return one(a[0], b[0]) + (one(a[0], b[1]) + one(a[1], b[0]))


def identity(n):
    return (
        lax.broadcasted_iota(jnp.int32, (n, n), 0) == lax.broadcasted_iota(jnp.int32, (n, n), 1)
    ).astype(f32)


def norm_steps(gap):
    gain = 2.0 / (2.0 - gap * gap)
    return gain, 0.5 * gain * gap * gap


def newton_start(block, x_ref, t_ref, d_ref):
    d_ref[0], d_ref[1] = split(block)
    top = jnp.maximum(jnp.max(jnp.sum(jnp.abs(block), axis=0, keepdims=True)), LOWEST)
    lead = 2.0 / (top + LOWEST)
    gain, gap = norm_steps((top - LOWEST) / (top + LOWEST))
    rest = 2.0 * identity(block.shape[0]) - lead * block
    x_ref[...] = (gain * lead) * rest
    t_ref[...] = (gain * lead) * mul((d_ref[0], d_ref[1]), split(rest))
    return gap


def newton_step(gap, x_ref, t_ref):
    gain, gap = norm_steps(gap)
    n = x_ref.shape[0]
    rest = split(2.0 * identity(n) - t_ref[...])
    both = mul(split(jnp.concatenate([t_ref[...], x_ref[...]], axis=0)), rest)
    t_ref[...] = gain * both[:n]
    x_ref[...] = gain * both[n:]
    return gap


def newton_finish(gap, x_ref, t_ref, d_ref, noise):
    def more(limit):
        return lambda state: jnp.logical_and(state[1] > limit, state[0] < MAX_STEPS)

    step = lambda state: (state[0] + 1, newton_step(state[1], x_ref, t_ref))
    _, gap = lax.while_loop(more(COARSE_TOL), step, (jnp.int32(0), gap))

    def correct(state):
        x = x_ref[...]
        x_parts = split(x)
        residual = identity(x.shape[0]) - mul((d_ref[0], d_ref[1]), x_parts)
        x_ref[...] = x + jnp.dot(x_parts[0], residual.astype(bf16), preferred_element_type=f32)
        return state[0] + 1, state[1] * state[1]

    lax.while_loop(more(TOL), correct, (jnp.int32(0), gap + noise))
    return x_ref[...]


def noise_of(block):
    return jnp.max(jnp.sum(jnp.abs(block), axis=0, keepdims=True)) * NOISE


def newton(block, x_ref, t_ref, d_ref):
    gap = newton_start(block, x_ref, t_ref, d_ref)
    return newton_finish(gap, x_ref, t_ref, d_ref, noise_of(block))


def places():
    core = lax.axis_index("rhs")
    return (
        core,
        pl.ds(pl.multiple_of(core * HALF, HALF), HALF),
        pl.ds(pl.multiple_of(HALF - core * HALF, HALF), HALF),
        pl.ds(pl.multiple_of(core * SHARE, SHARE), SHARE),
        pl.ds(pl.multiple_of(SHARE - core * SHARE, SHARE), SHARE),
    )


def invert(first, cross_block, last_block, out_ref, x_ref, t_ref, d_ref):
    _, mine, other, _, _ = places()
    cross = split(cross_block)
    lift = split(mul(cross, split(first)))
    out_ref[mine, mine] = first
    last = newton(last_block() - mul(lift, cross, NT), x_ref, t_ref, d_ref)
    low = -mul(split(last), lift)
    up = low.T
    out_ref[other, other] = last
    out_ref[other, mine] = low
    out_ref[mine, other] = up
    out_ref[mine, mine] = out_ref[mine, mine] - mul(split(up), lift)


def loads(sems, *pairs):
    copies = [
        pltpu.make_async_copy(source, target, sems.at[index])
        for index, (source, target) in enumerate(pairs)
    ]
    for copy in copies:
        copy.start()
    return copies


def rows(first, second, count=N):
    core = lax.axis_index("rhs")
    return pl.ds(pl.multiple_of(first + core * (second - first), HALF), count)


def remote(source, target, sems, index, device):
    copy = pltpu.make_async_remote_copy(
        src_ref=source,
        dst_ref=target,
        send_sem=sems[0].at[index],
        recv_sem=sems[1].at[index],
        device_id=device,
        device_id_type=MESH,
    )
    copy.start()
    return copy


def greet(*devices):
    barrier = pltpu.get_barrier_semaphore()
    for device in devices:
        pl.semaphore_signal(barrier, inc=1, device_id=device, device_id_type=MESH)
    return lambda: pl.semaphore_wait(barrier, len(devices))


def partners(
    diag, lower, right_side,
    d_own, d_other, g_ref, h_ref, f_ref, d2_own, x_ref, t_ref, gap_ref,
    d_ref, sems, send_sems, recv_sems,
):
    core, mine, other, share, rest = places()
    partner = {"rhs": 1 - core}
    arrived = greet(partner)
    section = rows(N, 3 * N)
    copies = loads(
        sems,
        (diag.at[section], d_own),
        (lower.at[rows(2 * N, 3 * N)], g_ref.at[:, mine]),
        (lower.at[N : 2 * N], h_ref.at[:, mine]),
        (right_side.at[:, section], f_ref.at[share]),
        (diag.at[2 * N : 3 * N], d2_own),
    )
    arrived()
    pair = (send_sems, recv_sems)
    swaps = [
        remote(source, target, pair, index, partner)
        for index, (source, target) in enumerate(
            (
                (diag.at[rows(3 * N, N + HALF, HALF)], d_other),
                (lower.at[rows(3 * N, 2 * N)], g_ref.at[:, mine]),
                (right_side.at[:, rows(3 * N, N)], f_ref.at[share]),
            )
        )
    ]

    def outer():
        return pltpu.make_async_remote_copy(
            src_ref=lower.at[N : 2 * N],
            dst_ref=h_ref.at[:, mine],
            send_sem=send_sems.at[3],
            recv_sem=recv_sems.at[3],
            device_id=partner,
            device_id_type=MESH,
        )

    @pl.when(core == 1)
    def _():
        outer().start()

    copies[0].wait()
    gap = newton_start(d_own[mine], x_ref, t_ref, d_ref)
    gap = lax.fori_loop(0, FIXED_STEPS, lambda _, gap: newton_step(gap, x_ref, t_ref), gap)
    gap_ref[...] = jnp.full(gap_ref.shape, gap, f32)
    for copy in copies[1:]:
        copy.wait()
    for copy in swaps:
        copy.wait()

    @pl.when(core == 0)
    def _():
        outer().wait_recv()

    @pl.when(core == 1)
    def _():
        outer().wait_send()


def level_one(
    d_own, d_other, g_whole, d2_own, first_x, first_t, gap_in,
    inverse_ref, v_ref, send_ref, keep_ref,
    gv_ref, g_ref, x_ref, t_ref, d_ref,
):
    core, mine, other, share, rest = places()
    x_ref[...] = first_x[...]
    t_ref[...] = first_t[...]
    block = d_own[mine]
    d_ref[0], d_ref[1] = split(block)
    first = newton_finish(jnp.max(gap_in[...]), x_ref, t_ref, d_ref, noise_of(block))
    invert(first, d_own[other], lambda: d_other[...], inverse_ref, x_ref, t_ref, d_ref)

    @pl.when(core == 0)
    def _():
        g_ref[...] = g_whole[...]

    @pl.when(core == 1)
    def _():
        g_ref[...] = g_whole[...].T

    g = split(g_ref[...])
    v = mul(split(inverse_ref[...]), g, NT)
    v_ref[...] = v
    gv_ref[...] = mul(g, split(v))
    send_ref[:N] = gv_ref[:, other]
    send_ref[N:] = gv_ref[mine, mine] - d2_own[mine]
    keep_ref[:N] = gv_ref[:, mine]
    keep_ref[N:] = gv_ref[other, other]


def outward(
    inverse_ref, v_ref, send_ref, h_ref, f_own,
    came_ref, ht_ref, z_ref, pack_ref, corner_ref, small_ref,
    c_ref, f_ref, send_sems, recv_sems,
):
    core, mine, other, share, rest = places()
    partner = {"rhs": 1 - core}
    greet(partner)()
    swapped = remote(send_ref, came_ref, (send_sems, recv_sems), 0, partner)
    v, inverse = split(v_ref[...]), split(inverse_ref[...])
    z = mul(split(f_own[...]), inverse)
    z_ref[...] = z

    def stack(place, first):
        small_ref[place] = f_ref[share]
        pack_ref[first : first + SHARE] = f_ref[rest, :HALF]
        pack_ref[first + SHARE : first + RHS] = f_ref[rest, HALF:]

    @pl.when(core == 0)
    def _():
        ht_ref[...] = h_ref[...].T
        c_ref[...] = -mul(split(ht_ref[...]), v)
        f_ref[...] = mul(split(z), split(h_ref[...]))

    @pl.when(core == 1)
    def _():
        c_ref[...] = -v_ref[...]
        corner_ref[...] = inverse_ref[:, mine]
        pack_ref[2 * N : 3 * N] = inverse_ref[:, other]
        f_ref[...] = z

    pack_ref[:N] = c_ref[:, :HALF]
    pack_ref[N : 2 * N] = c_ref[:, HALF:]
    stack(0, 3 * N)
    f_ref[...] = mul(split(f_own[...]), v)
    stack(1, 3 * N + RHS)
    swapped.wait()


def level_two(d2_own, keep_ref, came_ref, inverse_ref, d_own, x_ref, t_ref, d_ref):
    core, mine, other, share, rest = places()
    d_own[...] = d2_own[...] - (keep_ref[:N] + came_ref[:N])
    last_block = lambda: -(keep_ref[N:] + came_ref[N:])
    first = newton(d_own[mine], x_ref, t_ref, d_ref)
    invert(first, d_own[other], last_block, inverse_ref, x_ref, t_ref, d_ref)


def survivors(
    inverse_ref, own_ref, came_ref, hw_ref, small_ref, first_inverse, v_ref, z_ref, h_ref, ht_ref,
    diag, lower, right_side, coarse_sol,
    diag_ref, low_out, rhs_ref, solution_ref,
    c_both, hw_next, hz_both, low_send, low_came, hops, diag_send, rhs_send, diag_came, cross_came,
    corner_came, m_ref, n_ref, hw_own, hw_came, rhs_came,
    d0, f0, f2, y_ref, y_next, y_back, y_send, ys_ref, x2_ref, x_ref, x_both,
    sems, send_sems, recv_sems,
):
    core, mine, other, share, rest = places()
    me = lax.axis_index("tm")
    runs = lax.axis_size("tm")
    after, before = {"tm": lax.rem(me + 1, runs)}, {"tm": lax.rem(me + runs - 1, runs)}
    partner = {"rhs": 1 - core}
    place_x = lax.rem(me, ROW)
    first_x = me - place_x
    left_chip = {"tm": first_x + lax.rem(place_x + ROW - 1, ROW)}
    right_chip = {"tm": first_x + lax.rem(place_x + 1, ROW)}
    row_after = {"tm": lax.rem(me + ROW, runs)}
    row_before = {"tm": lax.rem(me + runs - ROW, runs)}
    arrived = greet(after, before, partner, left_chip, right_chip, row_after, row_before)
    copies = loads(
        sems,
        (right_side.at[:, 2 * N : 3 * N], f2),
        (lower.at[:N], n_ref.at[:, mine]),
        (coarse_sol, y_ref),
        (diag.at[:N], d0),
        (right_side.at[:, :N], f0),
    )
    pair = (send_sems, recv_sems)
    inverse = split(inverse_ref[...])
    for column in range(2):
        span = slice(column * HALF, (column + 1) * HALF)
        c_both[core, :, span] = own_ref[column * N : (column + 1) * N]
        c_both[1 - core, :, span] = came_ref[column * N : (column + 1) * N]
        first = 3 * N + column * SHARE
        hz_both[1 - core, :, span] = came_ref[first : first + SHARE]
        hz_both[2, :, span] = came_ref[first + RHS : first + RHS + SHARE]

    @pl.when(core == 0)
    def _():
        hw_next[...] = came_ref[2 * N : 3 * N]

    @pl.when(core == 1)
    def _():
        hw_next[...] = hw_ref[...]

    hz_both[core] = small_ref[0]
    right = split(c_both[1])
    u_right = split(mul(inverse, split(c_both[1, mine]), NT))
    arrived()
    swap_n = remote(lower.at[:N], n_ref.at[:, mine], pair, 23, partner)

    def diag_block(place):
        c_rows = split(c_both[1, place])
        return hw_next[place] + mul(c_rows, u_right)

    def described(source, target, index, device):
        return pltpu.make_async_remote_copy(
            src_ref=source,
            dst_ref=target,
            send_sem=send_sems.at[index],
            recv_sem=recv_sems.at[index],
            device_id=device,
            device_id_type=MESH,
        )

    crossing = lambda: described(diag_send.at[HALF:], diag_came.at[HALF:], 1, after)
    handing = lambda: described(diag_came.at[HALF:], cross_came, 22, partner)
    half_of_own = lambda: described(hw_own.at[:, HALF:], hw_came, 24, partner)
    turn = lambda chunk: described(hops.at[2, chunk], hops.at[3, chunk], 19 + chunk, row_after)

    @pl.when(core == 0)
    def _():
        diag_send[HALF:] = diag_block(slice(HALF, N))
        crossing().start()

    diag_send[:HALF] = diag_block(mine)
    square = [
        remote(diag_send.at[span, width], diag_came.at[span, width], pair, index, after)
        for index, span, width in (
            (2, slice(QUARTER, HALF), slice(0, HALF)),
            (9, slice(0, QUARTER), slice(0, QUARTER)),
        )
    ]
    left = split(c_both[0])
    u_left = split(mul(inverse, split(c_both[0, mine]), NT))

    def low_rows(first, count):
        span = slice(first, first + count)
        low_send[span] = -mul((right[0][span], right[1][span]), u_left)

    low_rows(DIRECT, N - DIRECT)
    steps = {}
    for chunk in range(CHUNKS):
        span = pl.ds(DIRECT + chunk * CHUNK, CHUNK)
        steps[0, chunk] = remote(
            low_send.at[span], hops.at[0, chunk], pair, 10 + chunk, left_chip
        )
    lows = []
    for index, (first, count) in enumerate(((0, HALF), (HALF, DIRECT - HALF))):
        span = pl.ds(first, count)
        low_rows(first, count)
        lows.append(remote(low_send.at[span], low_came.at[span], pair, 3 + index, after))
    copies[0].wait()
    z2 = mul(split(f2[...] - (small_ref[1] + hz_both[2])), inverse)
    z2_parts = split(z2)
    rhs_send[...] = hz_both[1] + mul(z2_parts, right, NT)
    rhs_sent = remote(rhs_send, rhs_came, pair, 5, after)

    copies[1].wait()
    copies[2].wait()
    swap_n.wait_recv()
    n = split(n_ref[...])
    y = split(y_ref[...])
    y_back[...] = mul(y, n)
    later = remote(y_back, y_next, pair, 0, before)

    def forward(hop, chunk):
        steps[hop, chunk].wait_recv()
        steps[hop + 1, chunk] = remote(
            hops.at[hop, chunk], hops.at[hop + 1, chunk], pair,
            10 + CHUNKS * (hop + 1) + chunk, left_chip,
        )

    forward(0, 0)
    copies[3].wait()
    diag_ref[...] = d0[...] - mul(left, u_left)

    @pl.when(core == 0)
    def _():
        hw_own[...] = mul(split(first_inverse[...]), split(h_ref[...]))

    forward(0, 1)

    @pl.when(core == 0)
    def _():
        hw_own[...] = mul(split(ht_ref[...]), split(hw_own[...]))
        half_of_own().start()
        hw_came[...] = hw_own[:, :HALF]

    forward(0, 2)
    later.wait_recv()

    @pl.when(core == 0)
    def _():
        y_send[...] = y_next[...]
        ys_ref[0] = y_ref[...]

    @pl.when(core == 1)
    def _():
        y_send[...] = y_ref[...]
        ys_ref[0] = y_next[...]

    swap_y = remote(y_send, ys_ref.at[1], pair, 6, partner)
    known = mul(y, left) + mul(split(y_next[...]), right)
    x2_ref[0] = z2 - mul(split(known), inverse)
    swap_x2 = remote(x2_ref.at[0], x2_ref.at[1], pair, 7, partner)
    copies[4].wait()
    rhs_ref[...] = f0[...] - hz_both[0] - mul(z2_parts, left, NT)
    forward(1, 0)

    @pl.when(core == 1)
    def _():
        half_of_own().wait_recv()

    diag_ref[...] = diag_ref[...] - hw_came[...]
    swap_y.wait_recv()
    swap_x2.wait_recv()

    @pl.when(core == 0)
    def _():
        for slot in range(2):
            ys_ref[slot] = mul(split(ys_ref[slot]), split(h_ref[...]), NT)

    forward(1, 1)
    v, w = split(v_ref[...]), split(first_inverse[...])
    for slot, place in ((1, rest), (0, share)):
        x_ref[slot] = (
            z_ref[place] - mul(split(ys_ref[slot]), w) - mul(split(x2_ref[slot]), v, NT)
        )
        if slot == 1:
            swap_x = remote(x_ref.at[1], x_both, pair, 8, partner)
    solution_ref[:, :N] = y_ref[...]
    solution_ref[:, 2 * N : 3 * N] = x2_ref[0]
    forward(1, 2)

    @pl.when(core == 0)
    def _():
        crossing().wait_recv()
        handing().start()

    for copy in square:
        copy.wait_recv()
    diag_came[:QUARTER, QUARTER:HALF] = diag_came[QUARTER:HALF, :QUARTER].T
    swap_corner = remote(diag_came.at[:HALF], corner_came, pair, 25, partner)

    def last_hop(chunk):
        steps[2, chunk].wait_recv()

        @pl.when(place_x == 0)
        def _():
            turn(chunk).start()

    last_hop(0)
    swap_x.wait_recv()

    @pl.when(core == 0)
    def _():
        solution_ref[:, N : 2 * N] = x_ref[0]
        solution_ref[:, 3 * N :] = x_both[...]

    @pl.when(core == 1)
    def _():
        solution_ref[:, N : 2 * N] = x_both[...]
        solution_ref[:, 3 * N :] = x_ref[0]

    m_ref[mine, mine] = diag_came[:HALF]
    swap_corner.wait_recv()
    m_ref[other, other] = corner_came[...]

    @pl.when(core == 0)
    def _():
        m_ref[HALF:, :HALF] = diag_came[HALF:]

    @pl.when(core == 1)
    def _():
        handing().wait_recv()
        m_ref[HALF:, :HALF] = cross_came[...]

    m_ref[:HALF, HALF:] = m_ref[HALF:, :HALF].T
    applied = split(mul(split(m_ref[...]), split(n_ref[mine]), NT))
    diag_ref[...] = diag_ref[...] - mul(n, applied)
    last_hop(1)
    lows[0].wait_recv()
    low_out[...] = mul(split(n_ref[:, :HALF]), split(low_came[:HALF]))
    last_hop(2)
    rhs_sent.wait_recv()
    rhs_ref[...] = rhs_ref[...] - mul(split(rhs_came[...]), n, NT)
    lows[1].wait_recv()
    for chunk in range(CHUNKS):
        span = pl.ds(DIRECT + chunk * CHUNK, CHUNK)

        @pl.when(place_x == 0)
        def _():
            turn(chunk).wait_recv()
            low_came[span] = hops[3, chunk]

        @pl.when(place_x != 0)
        def _():
            low_came[span] = hops[2, chunk]

    low_out[...] = low_out[...] + mul(split(n_ref[:, HALF:]), split(low_came[HALF:]))
    for copy in (
        later, *square, *lows, rhs_sent, swap_y, swap_x2, swap_x, swap_n, swap_corner,
        *steps.values(),
    ):
        copy.wait_send()

    @pl.when(place_x == 0)
    def _():
        for chunk in range(CHUNKS):
            turn(chunk).wait_send()

    @pl.when(core == 0)
    def _():
        crossing().wait_send()
        handing().wait_send()
        half_of_own().wait_send()


def deliver(*refs):
    count = (len(refs) - 1) // 2
    for copy in loads(refs[-1], *zip(refs[:count], refs[count : 2 * count])):
        copy.wait()


def shape(*dims):
    return jax.ShapeDtypeStruct(dims, f32)


def call(body, in_specs, outs, out_specs, scratch, flops, args, limit, **params):
    size = sum(a.size for a in args) + sum(o.size for o in outs)
    return pl.pallas_call(
        body,
        out_shape=outs,
        in_specs=in_specs,
        out_specs=out_specs,
        scratch_shapes=scratch,
        compiler_params=pltpu.CompilerParams(vmem_limit_bytes=limit << 20, **params),
        cost_estimate=pl.CostEstimate(flops=flops, bytes_accessed=4 * size, transcendentals=0),
    )(*args)


def newton_scratch():
    return [pltpu.VMEM((HALF, HALF), f32)] * 2 + [pltpu.VMEM((2, HALF, HALF), bf16)]


def copy_sems(count):
    return pltpu.SemaphoreType.DMA((count,))


def shards(diag, lower, right_side, coarse_sol):
    diag, lower, right_side, coarse_sol = (
        pltpu.with_memory_space_constraint(array, pltpu.HBM)
        for array in (diag, lower, right_side, coarse_sol)
    )
    swap = lambda x: lax.ppermute(x, "rhs", [(0, 1), (1, 0)])
    full, half, quarter = (N, N), (N, HALF), (HALF, HALF)
    small, scratch = (SHARE, N), lambda *dims: pltpu.VMEM(dims, f32)
    d_own, d_other, g, h, f, d2_own, first_x, first_t, gap = call(
        partners,
        [HBM] * 3,
        [shape(*half), shape(*quarter), shape(*full), shape(*full), shape(RHS, N), shape(*half),
         shape(*quarter), shape(*quarter), shape(8, 128)],
        [VMEM] * 9,
        [pltpu.VMEM((2, HALF, HALF), bf16), copy_sems(5), copy_sems(4), copy_sems(4)],
        2 * HALF**3 * 30,
        (diag, lower, right_side),
        16,
        collective_id=1,
        has_side_effects=True,
    )
    inverse, v, send, keep = call(
        level_one,
        [VMEM] * 7,
        [shape(*full), shape(*full), shape(N + HALF, HALF), shape(N + HALF, HALF)],
        [VMEM] * 4,
        [scratch(*full), scratch(*full)] + newton_scratch(),
        2 * N**3 * 20,
        (d_own, d_other, g, d2_own, first_x, first_t, gap),
        28,
    )
    came, ht, z, pack, hw, tails = call(
        outward,
        [VMEM] * 2 + [ANY] + [VMEM] * 2,
        [shape(N + HALF, HALF), shape(*full), shape(RHS, N), shape(3 * N + 2 * RHS, HALF),
         shape(*half), shape(2, *small)],
        [ANY] + [VMEM] * 5,
        [scratch(*full), scratch(RHS, N), copy_sems(1), copy_sems(1)],
        2 * N**3 * 6,
        (inverse, v, send, h, f),
        28,
        collective_id=3,
        has_side_effects=True,
    )
    pack_came = swap(pack)
    inverse2 = call(
        level_two,
        [VMEM] * 3,
        [shape(*full)],
        [VMEM],
        [scratch(*half)] + newton_scratch(),
        2 * N**3 * 20,
        (d2_own, keep, came),
        28,
    )[0]
    finals = [shape(*half), shape(*half), shape(*small), shape(SHARE, 4 * N)]
    results = call(
        survivors,
        [VMEM] * 10 + [HBM] * 4,
        finals,
        [VMEM] * 4,
        [scratch(2, *full), scratch(*half), scratch(3, *small), scratch(*half), scratch(*half),
         scratch(4, CHUNKS, CHUNK, HALF), scratch(*half), scratch(*small), scratch(*half),
         scratch(*quarter),
         scratch(*quarter), scratch(*full), scratch(*full), scratch(*full), scratch(*half),
         scratch(*small),
         scratch(*half), scratch(*small), scratch(*small), scratch(*small), scratch(*small),
         scratch(*small), scratch(*small), scratch(2, *small), scratch(2, *small),
         scratch(2, *small), scratch(*small),
         copy_sems(5), copy_sems(26), copy_sems(26)],
        2 * N**3 * 9,
        (inverse2, pack, pack_came, hw, tails, inverse, v, z, h, ht,
         diag, lower, right_side, coarse_sol),
        40,
        collective_id=2,
        has_side_effects=True,
    )
    return call(
        deliver, [ANY] * 4, finals, [HBM] * 4, [copy_sems(4)], 0, tuple(results), 8
    )


def solution(mesh):
    return jax.shard_map(
        shards,
        mesh=mesh,
        in_specs=(P("tm", "rhs"), P("tm", "rhs"), P("rhs", "tm"), P("rhs", "tm")),
        out_specs=(P("tm", "rhs"), P("tm", "rhs"), P("rhs", "tm"), P("rhs", "tm")),
        check_vma=False,
    )
```

```python
import functools

import jax
import jax.numpy as jnp
from jax import lax
from jax.experimental import pallas as pl
from jax.experimental.pallas import tpu as pltpu
from jax.sharding import PartitionSpec as P

f32, bf16 = jnp.float32, jnp.bfloat16
N = 512
HALF = 256
RHS = 128
SHARE = 64
QUARTER = 128
ROW = 4
DIRECT = 352
CHUNKS = 2
CHUNK = 80
LOWEST = 2.0
TOL = 2e-5
COARSE_TOL = 4e-3
NOISE = 2e-6
FIXED_STEPS = 4
MAX_STEPS = 40
VMEM = pl.BlockSpec(memory_space=pltpu.VMEM)
ANY = pl.BlockSpec(memory_space=pl.ANY)
HBM = pl.BlockSpec(memory_space=pltpu.HBM)
MESH = pl.DeviceIdType.MESH
NN = (((1,), (0,)), ((), ()))
NT = (((1,), (1,)), ((), ()))


def split(x):
    high = x.astype(bf16)
    return high, (x - high.astype(f32)).astype(bf16)


def mul(a, b, dims=NN):
    one = lambda p, q: lax.dot_general(p, q, dims, preferred_element_type=f32)
    return one(a[0], b[0]) + (one(a[0], b[1]) + one(a[1], b[0]))


def identity(n):
    return (
        lax.broadcasted_iota(jnp.int32, (n, n), 0) == lax.broadcasted_iota(jnp.int32, (n, n), 1)
    ).astype(f32)


def norm_steps(gap):
    gain = 2.0 / (2.0 - gap * gap)
    return gain, 0.5 * gain * gap * gap


def keep_state(t, x, tx_ref, z_ref):
    n = t.shape[0]
    tx_ref[0, :n], tx_ref[1, :n] = split(t)
    tx_ref[0, n:], tx_ref[1, n:] = split(x)
    z_ref[0], z_ref[1] = split(2.0 * identity(n) - t)


def newton_start(block, tx_ref, z_ref, d_ref):
    d_ref[0], d_ref[1] = split(block)
    top = jnp.maximum(jnp.max(jnp.sum(jnp.abs(block), axis=0, keepdims=True)), LOWEST)
    lead = 2.0 / (top + LOWEST)
    gain, gap = norm_steps((top - LOWEST) / (top + LOWEST))
    rest = 2.0 * identity(block.shape[0]) - lead * block
    t = (gain * lead) * mul((d_ref[0], d_ref[1]), split(rest))
    keep_state(t, (gain * lead) * rest, tx_ref, z_ref)
    return gap


def newton_step(gap, tx_ref, z_ref):
    gain, gap = norm_steps(gap)
    n = z_ref.shape[1]
    both = gain * mul((tx_ref[0], tx_ref[1]), (z_ref[0], z_ref[1]))
    keep_state(both[:n], both[n:], tx_ref, z_ref)
    return gap


def newton_finish(gap, x_ref, tx_ref, z_ref, d_ref, noise):
    n = z_ref.shape[1]

    def more(limit):
        return lambda state: jnp.logical_and(state[1] > limit, state[0] < MAX_STEPS)

    step = lambda state: (state[0] + 1, newton_step(state[1], tx_ref, z_ref))
    _, gap = lax.while_loop(more(COARSE_TOL), step, (jnp.int32(0), gap))

    def correct(x, x_parts):
        residual = identity(n) - mul((d_ref[0], d_ref[1]), x_parts)
        x_ref[...] = x + jnp.dot(x_parts[0], residual.astype(bf16), preferred_element_type=f32)

    high, low = tx_ref[0, n:], tx_ref[1, n:]
    correct(high.astype(f32) + low.astype(f32), (high, low))

    def again(state):
        x = x_ref[...]
        correct(x, split(x))
        return state[0] + 1, state[1] * state[1]

    left = gap + noise
    lax.while_loop(more(TOL), again, (jnp.int32(0), left * left))
    return x_ref[...]


def noise_of(block):
    return jnp.max(jnp.sum(jnp.abs(block), axis=0, keepdims=True)) * NOISE


def newton(block, x_ref, tx_ref, z_ref, d_ref):
    gap = newton_start(block, tx_ref, z_ref, d_ref)
    return newton_finish(gap, x_ref, tx_ref, z_ref, d_ref, noise_of(block))


def places():
    core = lax.axis_index("rhs")
    return (
        core,
        pl.ds(pl.multiple_of(core * HALF, HALF), HALF),
        pl.ds(pl.multiple_of(HALF - core * HALF, HALF), HALF),
        pl.ds(pl.multiple_of(core * SHARE, SHARE), SHARE),
        pl.ds(pl.multiple_of(SHARE - core * SHARE, SHARE), SHARE),
    )


def invert(first, cross_block, last_block, out_ref, *state):
    _, mine, other, _, _ = places()
    cross = split(cross_block)
    lift = split(mul(cross, split(first)))
    out_ref[mine, mine] = first
    last = newton(last_block() - mul(lift, cross, NT), *state)
    low = -mul(split(last), lift)
    up = low.T
    out_ref[other, other] = last
    out_ref[other, mine] = low
    out_ref[mine, other] = up
    out_ref[mine, mine] = out_ref[mine, mine] - mul(split(up), lift)


def loads(sems, *pairs):
    copies = [
        pltpu.make_async_copy(source, target, sems.at[index])
        for index, (source, target) in enumerate(pairs)
    ]
    for copy in copies:
        copy.start()
    return copies


def rows(first, second, count=N):
    core = lax.axis_index("rhs")
    return pl.ds(pl.multiple_of(first + core * (second - first), HALF), count)


def remote(source, target, sems, index, device):
    copy = pltpu.make_async_remote_copy(
        src_ref=source,
        dst_ref=target,
        send_sem=sems[0].at[index],
        recv_sem=sems[1].at[index],
        device_id=device,
        device_id_type=MESH,
    )
    copy.start()
    return copy


def greet(*devices):
    barrier = pltpu.get_barrier_semaphore()
    for device in devices:
        pl.semaphore_signal(barrier, inc=1, device_id=device, device_id_type=MESH)
    return lambda: pl.semaphore_wait(barrier, len(devices))


def partners(
    diag, lower, right_side,
    d_own, d_other, g_ref, h_ref, f_ref, d2_own, tx_ref, z_ref, gap_ref,
    d_ref, sems, send_sems, recv_sems,
):
    core, mine, other, share, rest = places()
    partner = {"rhs": 1 - core}
    arrived = greet(partner)
    section = rows(N, 3 * N)
    copies = loads(
        sems,
        (diag.at[section], d_own),
        (lower.at[rows(2 * N, 3 * N)], g_ref.at[:, mine]),
        (lower.at[N : 2 * N], h_ref.at[:, mine]),
        (right_side.at[:, section], f_ref.at[share]),
        (diag.at[2 * N : 3 * N], d2_own),
    )
    arrived()
    pair = (send_sems, recv_sems)
    swaps = [
        remote(source, target, pair, index, partner)
        for index, (source, target) in enumerate(
            (
                (diag.at[rows(3 * N, N + HALF, HALF)], d_other),
                (lower.at[rows(3 * N, 2 * N)], g_ref.at[:, mine]),
                (right_side.at[:, rows(3 * N, N)], f_ref.at[share]),
            )
        )
    ]

    def outer():
        return pltpu.make_async_remote_copy(
            src_ref=lower.at[N : 2 * N],
            dst_ref=h_ref.at[:, mine],
            send_sem=send_sems.at[3],
            recv_sem=recv_sems.at[3],
            device_id=partner,
            device_id_type=MESH,
        )

    @pl.when(core == 1)
    def _():
        outer().start()

    copies[0].wait()
    gap = newton_start(d_own[mine], tx_ref, z_ref, d_ref)
    gap = lax.fori_loop(0, FIXED_STEPS, lambda _, gap: newton_step(gap, tx_ref, z_ref), gap)
    gap_ref[...] = jnp.full(gap_ref.shape, gap, f32)
    for copy in copies[1:]:
        copy.wait()
    for copy in swaps:
        copy.wait()

    @pl.when(core == 0)
    def _():
        outer().wait_recv()

    @pl.when(core == 1)
    def _():
        outer().wait_send()


def level_one(
    d_own, d_other, g_whole, d2_own, first_tx, first_z, gap_in,
    inverse_ref, v_ref, send_ref, keep_ref,
    gv_ref, g_ref, x_ref, tx_ref, z_ref, d_ref,
):
    core, mine, other, share, rest = places()
    tx_ref[...] = first_tx[...]
    z_ref[...] = first_z[...]
    block = d_own[mine]
    d_ref[0], d_ref[1] = split(block)
    state = (x_ref, tx_ref, z_ref, d_ref)
    first = newton_finish(jnp.max(gap_in[...]), *state, noise_of(block))
    invert(first, d_own[other], lambda: d_other[...], inverse_ref, *state)

    @pl.when(core == 0)
    def _():
        g_ref[...] = g_whole[...]

    @pl.when(core == 1)
    def _():
        g_ref[...] = g_whole[...].T

    g = split(g_ref[...])
    v = mul(split(inverse_ref[...]), g, NT)
    v_ref[...] = v
    gv_ref[...] = mul(g, split(v))
    send_ref[:N] = gv_ref[:, other]
    send_ref[N:] = gv_ref[mine, mine] - d2_own[mine]
    keep_ref[:N] = gv_ref[:, mine]
    keep_ref[N:] = gv_ref[other, other]


def outward(
    inverse_ref, v_ref, send_ref, h_ref, f_own,
    came_ref, ht_ref, z_ref, pack_ref, corner_ref, small_ref,
    c_ref, f_ref, send_sems, recv_sems,
):
    core, mine, other, share, rest = places()
    partner = {"rhs": 1 - core}
    greet(partner)()
    swapped = remote(send_ref, came_ref, (send_sems, recv_sems), 0, partner)
    v, inverse = split(v_ref[...]), split(inverse_ref[...])
    z = mul(split(f_own[...]), inverse)
    z_ref[...] = z

    def stack(place, first):
        small_ref[place] = f_ref[share]
        pack_ref[first : first + SHARE] = f_ref[rest, :HALF]
        pack_ref[first + SHARE : first + RHS] = f_ref[rest, HALF:]

    @pl.when(core == 0)
    def _():
        ht_ref[...] = h_ref[...].T
        c_ref[...] = -mul(split(ht_ref[...]), v)
        f_ref[...] = mul(split(z), split(h_ref[...]))

    @pl.when(core == 1)
    def _():
        c_ref[...] = -v_ref[...]
        corner_ref[...] = inverse_ref[:, mine]
        pack_ref[2 * N : 3 * N] = inverse_ref[:, other]
        f_ref[...] = z

    pack_ref[:N] = c_ref[:, :HALF]
    pack_ref[N : 2 * N] = c_ref[:, HALF:]
    stack(0, 3 * N)
    f_ref[...] = mul(split(f_own[...]), v)
    stack(1, 3 * N + RHS)
    swapped.wait()


def level_two(d2_own, keep_ref, came_ref, inverse_ref, d_own, *state):
    core, mine, other, share, rest = places()
    d_own[...] = d2_own[...] - (keep_ref[:N] + came_ref[:N])
    last_block = lambda: -(keep_ref[N:] + came_ref[N:])
    first = newton(d_own[mine], *state)
    invert(first, d_own[other], last_block, inverse_ref, *state)


def survivors(
    inverse_ref, own_ref, came_ref, hw_ref, small_ref, first_inverse, v_ref, z_ref, h_ref, ht_ref,
    diag, lower, right_side, coarse_sol,
    diag_ref, low_out, rhs_ref, solution_ref,
    c_both, hw_next, hz_both, low_send, low_came, hops, diag_send, rhs_send, diag_came, cross_came,
    corner_came, m_ref, n_ref, hw_own, hw_came, rhs_came,
    d0, f0, f2, y_ref, y_next, y_back, y_send, ys_ref, x2_ref, x_ref, x_both,
    sems, send_sems, recv_sems,
):
    core, mine, other, share, rest = places()
    me = lax.axis_index("tm")
    runs = lax.axis_size("tm")
    after, before = {"tm": lax.rem(me + 1, runs)}, {"tm": lax.rem(me + runs - 1, runs)}
    partner = {"rhs": 1 - core}
    place_x = lax.rem(me, ROW)
    first_x = me - place_x
    left_chip = {"tm": first_x + lax.rem(place_x + ROW - 1, ROW)}
    right_chip = {"tm": first_x + lax.rem(place_x + 1, ROW)}
    row_after = {"tm": lax.rem(me + ROW, runs)}
    row_before = {"tm": lax.rem(me + runs - ROW, runs)}
    arrived = greet(after, before, partner, left_chip, right_chip, row_after, row_before)
    copies = loads(
        sems,
        (right_side.at[:, 2 * N : 3 * N], f2),
        (lower.at[:N], n_ref.at[:, mine]),
        (coarse_sol, y_ref),
        (diag.at[:N], d0),
        (right_side.at[:, :N], f0),
    )
    pair = (send_sems, recv_sems)
    inverse = split(inverse_ref[...])
    for column in range(2):
        span = slice(column * HALF, (column + 1) * HALF)
        c_both[core, :, span] = own_ref[column * N : (column + 1) * N]
        c_both[1 - core, :, span] = came_ref[column * N : (column + 1) * N]
        first = 3 * N + column * SHARE
        hz_both[1 - core, :, span] = came_ref[first : first + SHARE]
        hz_both[2, :, span] = came_ref[first + RHS : first + RHS + SHARE]

    @pl.when(core == 0)
    def _():
        hw_next[...] = came_ref[2 * N : 3 * N]

    @pl.when(core == 1)
    def _():
        hw_next[...] = hw_ref[...]

    hz_both[core] = small_ref[0]
    right = split(c_both[1])
    u_left = split(mul(inverse, split(c_both[0, mine]), NT))
    arrived()

    def low_rows(first, count):
        span = slice(first, first + count)
        low_send[span] = -mul((right[0][span], right[1][span]), u_left)

    low_rows(DIRECT, N - DIRECT)
    steps = {}
    for chunk in range(CHUNKS):
        span = pl.ds(DIRECT + chunk * CHUNK, CHUNK)
        steps[0, chunk] = remote(
            low_send.at[span], hops.at[0, chunk], pair, 10 + chunk, left_chip
        )
    lows = []

    def straight(index, first, count):
        span = pl.ds(first, count)
        low_rows(first, count)
        lows.append(remote(low_send.at[span], low_came.at[span], pair, 3 + index, after))

    straight(0, 0, HALF)
    swap_n = remote(lower.at[:N], n_ref.at[:, mine], pair, 23, partner)
    u_right = split(mul(inverse, split(c_both[1, mine]), NT))

    def diag_block(place):
        c_rows = split(c_both[1, place])
        return hw_next[place] + mul(c_rows, u_right)

    def described(source, target, index, device):
        return pltpu.make_async_remote_copy(
            src_ref=source,
            dst_ref=target,
            send_sem=send_sems.at[index],
            recv_sem=recv_sems.at[index],
            device_id=device,
            device_id_type=MESH,
        )

    crossing = lambda: described(diag_send.at[HALF:], diag_came.at[HALF:], 1, after)
    handing = lambda: described(diag_came.at[HALF:], cross_came, 22, partner)
    half_of_own = lambda: described(hw_own.at[:, HALF:], hw_came, 24, partner)
    turn = lambda chunk: described(hops.at[2, chunk], hops.at[3, chunk], 19 + chunk, row_after)

    @pl.when(core == 0)
    def _():
        diag_send[HALF:] = diag_block(slice(HALF, N))
        crossing().start()

    diag_send[:HALF] = diag_block(mine)
    square = [
        remote(diag_send.at[span, width], diag_came.at[span, width], pair, index, after)
        for index, span, width in (
            (2, slice(QUARTER, HALF), slice(0, HALF)),
            (9, slice(0, QUARTER), slice(0, QUARTER)),
        )
    ]
    straight(1, HALF, DIRECT - HALF)
    copies[0].wait()
    z2 = mul(split(f2[...] - (small_ref[1] + hz_both[2])), inverse)
    z2_parts = split(z2)
    rhs_send[...] = hz_both[1] + mul(z2_parts, right, NT)
    rhs_sent = remote(rhs_send, rhs_came, pair, 5, after)

    copies[1].wait()
    copies[2].wait()
    swap_n.wait_recv()
    n = split(n_ref[...])
    y = split(y_ref[...])
    y_back[...] = mul(y, n)
    later = remote(y_back, y_next, pair, 0, before)

    def forward(hop, chunk):
        steps[hop, chunk].wait_recv()
        steps[hop + 1, chunk] = remote(
            hops.at[hop, chunk], hops.at[hop + 1, chunk], pair,
            10 + CHUNKS * (hop + 1) + chunk, left_chip,
        )

    forward(0, 0)
    copies[3].wait()
    left = split(c_both[0])
    diag_ref[...] = d0[...] - mul(left, u_left)

    @pl.when(core == 0)
    def _():
        hw_own[...] = mul(split(first_inverse[...]), split(h_ref[...]))

    forward(0, 1)

    @pl.when(core == 0)
    def _():
        hw_own[...] = mul(split(ht_ref[...]), split(hw_own[...]))
        half_of_own().start()
        hw_came[...] = hw_own[:, :HALF]

    later.wait_recv()

    @pl.when(core == 0)
    def _():
        y_send[...] = y_next[...]
        ys_ref[0] = y_ref[...]

    @pl.when(core == 1)
    def _():
        y_send[...] = y_ref[...]
        ys_ref[0] = y_next[...]

    swap_y = remote(y_send, ys_ref.at[1], pair, 6, partner)
    known = mul(y, left) + mul(split(y_next[...]), right)
    x2_ref[0] = z2 - mul(split(known), inverse)
    swap_x2 = remote(x2_ref.at[0], x2_ref.at[1], pair, 7, partner)
    copies[4].wait()
    rhs_ref[...] = f0[...] - hz_both[0] - mul(z2_parts, left, NT)
    forward(1, 0)

    @pl.when(core == 1)
    def _():
        half_of_own().wait_recv()

    diag_ref[...] = diag_ref[...] - hw_came[...]
    swap_y.wait_recv()
    swap_x2.wait_recv()

    @pl.when(core == 0)
    def _():
        for slot in range(2):
            ys_ref[slot] = mul(split(ys_ref[slot]), split(h_ref[...]), NT)

    forward(1, 1)
    v, w = split(v_ref[...]), split(first_inverse[...])
    for slot, place in ((1, rest), (0, share)):
        x_ref[slot] = (
            z_ref[place] - mul(split(ys_ref[slot]), w) - mul(split(x2_ref[slot]), v, NT)
        )
        if slot == 1:
            swap_x = remote(x_ref.at[1], x_both, pair, 8, partner)
    solution_ref[:, :N] = y_ref[...]
    solution_ref[:, 2 * N : 3 * N] = x2_ref[0]

    @pl.when(core == 0)
    def _():
        crossing().wait_recv()
        handing().start()

    for copy in square:
        copy.wait_recv()
    diag_came[:QUARTER, QUARTER:HALF] = diag_came[QUARTER:HALF, :QUARTER].T
    swap_corner = remote(diag_came.at[:HALF], corner_came, pair, 25, partner)

    def last_hop(chunk):
        steps[2, chunk].wait_recv()

        @pl.when(place_x == 0)
        def _():
            turn(chunk).start()

    last_hop(0)
    swap_x.wait_recv()

    @pl.when(core == 0)
    def _():
        solution_ref[:, N : 2 * N] = x_ref[0]
        solution_ref[:, 3 * N :] = x_both[...]

    @pl.when(core == 1)
    def _():
        solution_ref[:, N : 2 * N] = x_both[...]
        solution_ref[:, 3 * N :] = x_ref[0]

    m_ref[mine, mine] = diag_came[:HALF]
    swap_corner.wait_recv()
    m_ref[other, other] = corner_came[...]

    @pl.when(core == 0)
    def _():
        m_ref[HALF:, :HALF] = diag_came[HALF:]

    @pl.when(core == 1)
    def _():
        handing().wait_recv()
        m_ref[HALF:, :HALF] = cross_came[...]

    m_ref[:HALF, HALF:] = m_ref[HALF:, :HALF].T
    applied = split(mul(split(m_ref[...]), split(n_ref[mine]), NT))
    diag_ref[...] = diag_ref[...] - mul(n, applied)
    last_hop(1)
    lows[0].wait_recv()
    low_out[...] = mul(split(n_ref[:, :HALF]), split(low_came[:HALF]))
    rhs_sent.wait_recv()
    rhs_ref[...] = rhs_ref[...] - mul(split(rhs_came[...]), n, NT)
    lows[1].wait_recv()
    for chunk in range(CHUNKS):
        span = pl.ds(DIRECT + chunk * CHUNK, CHUNK)

        @pl.when(place_x == 0)
        def _():
            turn(chunk).wait_recv()
            low_came[span] = hops[3, chunk]

        @pl.when(place_x != 0)
        def _():
            low_came[span] = hops[2, chunk]

    low_out[...] = low_out[...] + mul(split(n_ref[:, HALF:]), split(low_came[HALF:]))
    for copy in (
        later, *square, *lows, rhs_sent, swap_y, swap_x2, swap_x, swap_n, swap_corner,
        *steps.values(),
    ):
        copy.wait_send()

    @pl.when(place_x == 0)
    def _():
        for chunk in range(CHUNKS):
            turn(chunk).wait_send()

    @pl.when(core == 0)
    def _():
        crossing().wait_send()
        handing().wait_send()
        half_of_own().wait_send()


def deliver(*refs):
    count = (len(refs) - 1) // 2
    for copy in loads(refs[-1], *zip(refs[:count], refs[count : 2 * count])):
        copy.wait()


def shape(*dims):
    return jax.ShapeDtypeStruct(dims, f32)


def call(body, in_specs, outs, out_specs, scratch, flops, args, limit, **params):
    size = sum(a.size for a in args) + sum(o.size for o in outs)
    return pl.pallas_call(
        body,
        out_shape=outs,
        in_specs=in_specs,
        out_specs=out_specs,
        scratch_shapes=scratch,
        compiler_params=pltpu.CompilerParams(vmem_limit_bytes=limit << 20, **params),
        cost_estimate=pl.CostEstimate(flops=flops, bytes_accessed=4 * size, transcendentals=0),
    )(*args)


def newton_scratch():
    pair = pltpu.VMEM((2, HALF, HALF), bf16)
    return [pltpu.VMEM((HALF, HALF), f32), pltpu.VMEM((2, N, HALF), bf16), pair, pair]


def copy_sems(count):
    return pltpu.SemaphoreType.DMA((count,))


def shards(diag, lower, right_side, coarse_sol):
    diag, lower, right_side, coarse_sol = (
        pltpu.with_memory_space_constraint(array, pltpu.HBM)
        for array in (diag, lower, right_side, coarse_sol)
    )
    swap = lambda x: lax.ppermute(x, "rhs", [(0, 1), (1, 0)])
    full, half, quarter = (N, N), (N, HALF), (HALF, HALF)
    small, scratch = (SHARE, N), lambda *dims: pltpu.VMEM(dims, f32)
    d_own, d_other, g, h, f, d2_own, first_tx, first_z, gap = call(
        partners,
        [HBM] * 3,
        [shape(*half), shape(*quarter), shape(*full), shape(*full), shape(RHS, N), shape(*half),
         jax.ShapeDtypeStruct((2, N, HALF), bf16), jax.ShapeDtypeStruct((2, HALF, HALF), bf16),
         shape(8, 128)],
        [VMEM] * 9,
        [pltpu.VMEM((2, HALF, HALF), bf16), copy_sems(5), copy_sems(4), copy_sems(4)],
        2 * HALF**3 * 30,
        (diag, lower, right_side),
        16,
        collective_id=1,
        has_side_effects=True,
    )
    inverse, v, send, keep = call(
        level_one,
        [VMEM] * 7,
        [shape(*full), shape(*full), shape(N + HALF, HALF), shape(N + HALF, HALF)],
        [VMEM] * 4,
        [scratch(*full), scratch(*full)] + newton_scratch(),
        2 * N**3 * 20,
        (d_own, d_other, g, d2_own, first_tx, first_z, gap),
        28,
    )
    came, ht, z, pack, hw, tails = call(
        outward,
        [VMEM] * 2 + [ANY] + [VMEM] * 2,
        [shape(N + HALF, HALF), shape(*full), shape(RHS, N), shape(3 * N + 2 * RHS, HALF),
         shape(*half), shape(2, *small)],
        [ANY] + [VMEM] * 5,
        [scratch(*full), scratch(RHS, N), copy_sems(1), copy_sems(1)],
        2 * N**3 * 6,
        (inverse, v, send, h, f),
        28,
        collective_id=3,
        has_side_effects=True,
    )
    pack_came = swap(pack)
    inverse2 = call(
        level_two,
        [VMEM] * 3,
        [shape(*full)],
        [VMEM],
        [scratch(*half)] + newton_scratch(),
        2 * N**3 * 20,
        (d2_own, keep, came),
        28,
    )[0]
    finals = [shape(*half), shape(*half), shape(*small), shape(SHARE, 4 * N)]
    results = call(
        survivors,
        [VMEM] * 10 + [HBM] * 4,
        finals,
        [VMEM] * 4,
        [scratch(2, *full), scratch(*half), scratch(3, *small), scratch(*half), scratch(*half),
         scratch(4, CHUNKS, CHUNK, HALF), scratch(*half), scratch(*small), scratch(*half),
         scratch(*quarter),
         scratch(*quarter), scratch(*full), scratch(*full), scratch(*full), scratch(*half),
         scratch(*small),
         scratch(*half), scratch(*small), scratch(*small), scratch(*small), scratch(*small),
         scratch(*small), scratch(*small), scratch(2, *small), scratch(2, *small),
         scratch(2, *small), scratch(*small),
         copy_sems(5), copy_sems(26), copy_sems(26)],
        2 * N**3 * 9,
        (inverse2, pack, pack_came, hw, tails, inverse, v, z, h, ht,
         diag, lower, right_side, coarse_sol),
        40,
        collective_id=2,
        has_side_effects=True,
    )
    return call(
        deliver, [ANY] * 4, finals, [HBM] * 4, [copy_sems(4)], 0, tuple(results), 8
    )


def solution(mesh):
    return jax.shard_map(
        shards,
        mesh=mesh,
        in_specs=(P("tm", "rhs"), P("tm", "rhs"), P("rhs", "tm"), P("rhs", "tm")),
        out_specs=(P("tm", "rhs"), P("tm", "rhs"), P("rhs", "tm"), P("rhs", "tm")),
        check_vma=False,
    )
```

```python
import functools

import jax
import jax.numpy as jnp
from jax import lax
from jax.experimental import pallas as pl
from jax.experimental.pallas import tpu as pltpu
from jax.sharding import PartitionSpec as P

f32, bf16 = jnp.float32, jnp.bfloat16
N = 512
HALF = 256
RHS = 128
SHARE = 64
QUARTER = 128
ROW = 4
DIRECT = 320
CHUNKS = 3
CHUNK = 64
LOWEST = 2.0
TOL = 2e-5
COARSE_TOL = 4e-3
NOISE = 2e-6
FIXED_STEPS = 4
MAX_STEPS = 40
VMEM = pl.BlockSpec(memory_space=pltpu.VMEM)
ANY = pl.BlockSpec(memory_space=pl.ANY)
HBM = pl.BlockSpec(memory_space=pltpu.HBM)
MESH = pl.DeviceIdType.MESH
NN = (((1,), (0,)), ((), ()))
NT = (((1,), (1,)), ((), ()))


def split(x):
    high = x.astype(bf16)
    return high, (x - high.astype(f32)).astype(bf16)


def mul(a, b, dims=NN):
    one = lambda p, q: lax.dot_general(p, q, dims, preferred_element_type=f32)
    return one(a[0], b[0]) + (one(a[0], b[1]) + one(a[1], b[0]))


def identity(n):
    return (
        lax.broadcasted_iota(jnp.int32, (n, n), 0) == lax.broadcasted_iota(jnp.int32, (n, n), 1)
    ).astype(f32)


def norm_steps(gap):
    gain = 2.0 / (2.0 - gap * gap)
    return gain, 0.5 * gain * gap * gap


def newton_start(block, x_ref, t_ref, d_ref):
    d_ref[0], d_ref[1] = split(block)
    top = jnp.maximum(jnp.max(jnp.sum(jnp.abs(block), axis=0, keepdims=True)), LOWEST)
    lead = 2.0 / (top + LOWEST)
    gain, gap = norm_steps((top - LOWEST) / (top + LOWEST))
    rest = 2.0 * identity(block.shape[0]) - lead * block
    x_ref[...] = (gain * lead) * rest
    t_ref[...] = (gain * lead) * mul((d_ref[0], d_ref[1]), split(rest))
    return gap


def newton_step(gap, x_ref, t_ref):
    gain, gap = norm_steps(gap)
    n = x_ref.shape[0]
    rest = split(2.0 * identity(n) - t_ref[...])
    both = mul(split(jnp.concatenate([t_ref[...], x_ref[...]], axis=0)), rest)
    t_ref[...] = gain * both[:n]
    x_ref[...] = gain * both[n:]
    return gap


def newton_finish(gap, x_ref, t_ref, d_ref, noise):
    def more(limit):
        return lambda state: jnp.logical_and(state[1] > limit, state[0] < MAX_STEPS)

    step = lambda state: (state[0] + 1, newton_step(state[1], x_ref, t_ref))
    _, gap = lax.while_loop(more(COARSE_TOL), step, (jnp.int32(0), gap))

    def correct(state):
        x = x_ref[...]
        x_parts = split(x)
        residual = identity(x.shape[0]) - mul((d_ref[0], d_ref[1]), x_parts)
        x_ref[...] = x + jnp.dot(x_parts[0], residual.astype(bf16), preferred_element_type=f32)
        return state[0] + 1, state[1] * state[1]

    lax.while_loop(more(TOL), correct, (jnp.int32(0), gap + noise))
    return x_ref[...]


def noise_of(block):
    return jnp.max(jnp.sum(jnp.abs(block), axis=0, keepdims=True)) * NOISE


def newton(block, x_ref, t_ref, d_ref):
    gap = newton_start(block, x_ref, t_ref, d_ref)
    return newton_finish(gap, x_ref, t_ref, d_ref, noise_of(block))


def places():
    core = lax.axis_index("rhs")
    return (
        core,
        pl.ds(pl.multiple_of(core * HALF, HALF), HALF),
        pl.ds(pl.multiple_of(HALF - core * HALF, HALF), HALF),
        pl.ds(pl.multiple_of(core * SHARE, SHARE), SHARE),
        pl.ds(pl.multiple_of(SHARE - core * SHARE, SHARE), SHARE),
    )


def invert(first, cross_block, last_block, out_ref, x_ref, t_ref, d_ref):
    _, mine, other, _, _ = places()
    cross = split(cross_block)
    lift = split(mul(cross, split(first)))
    out_ref[mine, mine] = first
    last = newton(last_block() - mul(lift, cross, NT), x_ref, t_ref, d_ref)
    low = -mul(split(last), lift)
    up = low.T
    out_ref[other, other] = last
    out_ref[other, mine] = low
    out_ref[mine, other] = up
    out_ref[mine, mine] = out_ref[mine, mine] - mul(split(up), lift)


def loads(sems, *pairs):
    copies = [
        pltpu.make_async_copy(source, target, sems.at[index])
        for index, (source, target) in enumerate(pairs)
    ]
    for copy in copies:
        copy.start()
    return copies


def rows(first, second, count=N):
    core = lax.axis_index("rhs")
    return pl.ds(pl.multiple_of(first + core * (second - first), HALF), count)


def remote(source, target, sems, index, device):
    copy = pltpu.make_async_remote_copy(
        src_ref=source,
        dst_ref=target,
        send_sem=sems[0].at[index],
        recv_sem=sems[1].at[index],
        device_id=device,
        device_id_type=MESH,
    )
    copy.start()
    return copy


def greet(*devices):
    barrier = pltpu.get_barrier_semaphore()
    for device in devices:
        pl.semaphore_signal(barrier, inc=1, device_id=device, device_id_type=MESH)
    return lambda: pl.semaphore_wait(barrier, len(devices))


def partners(
    diag, lower, right_side,
    d_own, d_other, g_ref, h_ref, f_ref, d2_own, x_ref, t_ref, gap_ref,
    d_ref, sems, send_sems, recv_sems,
):
    core, mine, other, share, rest = places()
    partner = {"rhs": 1 - core}
    arrived = greet(partner)
    section = rows(N, 3 * N)
    copies = loads(
        sems,
        (diag.at[section], d_own),
        (lower.at[rows(2 * N, 3 * N)], g_ref.at[:, mine]),
        (lower.at[N : 2 * N], h_ref.at[:, mine]),
        (right_side.at[:, section], f_ref.at[share]),
        (diag.at[2 * N : 3 * N], d2_own),
    )
    arrived()
    pair = (send_sems, recv_sems)
    swaps = [
        remote(source, target, pair, index, partner)
        for index, (source, target) in enumerate(
            (
                (diag.at[rows(3 * N, N + HALF, HALF)], d_other),
                (lower.at[rows(3 * N, 2 * N)], g_ref.at[:, mine]),
                (right_side.at[:, rows(3 * N, N)], f_ref.at[share]),
            )
        )
    ]

    def outer():
        return pltpu.make_async_remote_copy(
            src_ref=lower.at[N : 2 * N],
            dst_ref=h_ref.at[:, mine],
            send_sem=send_sems.at[3],
            recv_sem=recv_sems.at[3],
            device_id=partner,
            device_id_type=MESH,
        )

    @pl.when(core == 1)
    def _():
        outer().start()

    copies[0].wait()
    gap = newton_start(d_own[mine], x_ref, t_ref, d_ref)
    gap = lax.fori_loop(0, FIXED_STEPS, lambda _, gap: newton_step(gap, x_ref, t_ref), gap)
    gap_ref[...] = jnp.full(gap_ref.shape, gap, f32)
    for copy in copies[1:]:
        copy.wait()
    for copy in swaps:
        copy.wait()

    @pl.when(core == 0)
    def _():
        outer().wait_recv()

    @pl.when(core == 1)
    def _():
        outer().wait_send()


def level_one(
    d_own, d_other, g_whole, d2_own, first_x, first_t, gap_in,
    inverse_ref, v_ref, send_ref, keep_ref,
    gv_ref, g_ref, x_ref, t_ref, d_ref,
):
    core, mine, other, share, rest = places()
    x_ref[...] = first_x[...]
    t_ref[...] = first_t[...]
    block = d_own[mine]
    d_ref[0], d_ref[1] = split(block)
    first = newton_finish(jnp.max(gap_in[...]), x_ref, t_ref, d_ref, noise_of(block))
    invert(first, d_own[other], lambda: d_other[...], inverse_ref, x_ref, t_ref, d_ref)

    @pl.when(core == 0)
    def _():
        g_ref[...] = g_whole[...]

    @pl.when(core == 1)
    def _():
        g_ref[...] = g_whole[...].T

    g = split(g_ref[...])
    v = mul(split(inverse_ref[...]), g, NT)
    v_ref[...] = v
    gv_ref[...] = mul(g, split(v))
    send_ref[:N] = gv_ref[:, other]
    send_ref[N:] = gv_ref[mine, mine] - d2_own[mine]
    keep_ref[:N] = gv_ref[:, mine]
    keep_ref[N:] = gv_ref[other, other]


def outward(
    inverse_ref, v_ref, send_ref, h_ref, f_own,
    came_ref, ht_ref, z_ref, pack_ref, corner_ref, small_ref,
    c_ref, f_ref, send_sems, recv_sems,
):
    core, mine, other, share, rest = places()
    partner = {"rhs": 1 - core}
    greet(partner)()
    swapped = remote(send_ref, came_ref, (send_sems, recv_sems), 0, partner)
    v, inverse = split(v_ref[...]), split(inverse_ref[...])
    z = mul(split(f_own[...]), inverse)
    z_ref[...] = z

    def stack(place, first):
        small_ref[place] = f_ref[share]
        pack_ref[first : first + SHARE] = f_ref[rest, :HALF]
        pack_ref[first + SHARE : first + RHS] = f_ref[rest, HALF:]

    @pl.when(core == 0)
    def _():
        ht_ref[...] = h_ref[...].T
        c_ref[...] = -mul(split(ht_ref[...]), v)
        f_ref[...] = mul(split(z), split(h_ref[...]))

    @pl.when(core == 1)
    def _():
        c_ref[...] = -v_ref[...]
        corner_ref[...] = inverse_ref[:, mine]
        pack_ref[2 * N : 3 * N] = inverse_ref[:, other]
        f_ref[...] = z

    pack_ref[:N] = c_ref[:, :HALF]
    pack_ref[N : 2 * N] = c_ref[:, HALF:]
    stack(0, 3 * N)
    f_ref[...] = mul(split(f_own[...]), v)
    stack(1, 3 * N + RHS)
    swapped.wait()


def level_two(d2_own, keep_ref, came_ref, inverse_ref, d_own, x_ref, t_ref, d_ref):
    core, mine, other, share, rest = places()
    d_own[...] = d2_own[...] - (keep_ref[:N] + came_ref[:N])
    last_block = lambda: -(keep_ref[N:] + came_ref[N:])
    first = newton(d_own[mine], x_ref, t_ref, d_ref)
    invert(first, d_own[other], last_block, inverse_ref, x_ref, t_ref, d_ref)


def survivors(
    inverse_ref, own_ref, came_ref, hw_ref, small_ref, first_inverse, v_ref, z_ref, h_ref, ht_ref,
    diag, lower, right_side, coarse_sol,
    diag_ref, low_out, rhs_ref, solution_ref,
    c_both, hw_next, hz_both, low_send, low_came, hops, diag_send, rhs_send, diag_came, cross_came,
    corner_came, m_ref, n_ref, hw_own, hw_came, rhs_came,
    d0, f0, f2, y_ref, y_next, y_back, y_send, ys_ref, x2_ref, x_ref, x_both,
    sems, send_sems, recv_sems,
):
    core, mine, other, share, rest = places()
    me = lax.axis_index("tm")
    runs = lax.axis_size("tm")
    after, before = {"tm": lax.rem(me + 1, runs)}, {"tm": lax.rem(me + runs - 1, runs)}
    partner = {"rhs": 1 - core}
    place_x = lax.rem(me, ROW)
    first_x = me - place_x
    left_chip = {"tm": first_x + lax.rem(place_x + ROW - 1, ROW)}
    right_chip = {"tm": first_x + lax.rem(place_x + 1, ROW)}
    row_after = {"tm": lax.rem(me + ROW, runs)}
    row_before = {"tm": lax.rem(me + runs - ROW, runs)}
    arrived = greet(after, before, partner, left_chip, right_chip, row_after, row_before)
    copies = loads(
        sems,
        (right_side.at[:, 2 * N : 3 * N], f2),
        (lower.at[:N], n_ref.at[:, mine]),
        (coarse_sol, y_ref),
        (diag.at[:N], d0),
        (right_side.at[:, :N], f0),
    )
    pair = (send_sems, recv_sems)
    inverse = split(inverse_ref[...])
    for column in range(2):
        span = slice(column * HALF, (column + 1) * HALF)
        c_both[core, :, span] = own_ref[column * N : (column + 1) * N]
        c_both[1 - core, :, span] = came_ref[column * N : (column + 1) * N]
        first = 3 * N + column * SHARE
        hz_both[1 - core, :, span] = came_ref[first : first + SHARE]
        hz_both[2, :, span] = came_ref[first + RHS : first + RHS + SHARE]

    @pl.when(core == 0)
    def _():
        hw_next[...] = came_ref[2 * N : 3 * N]

    @pl.when(core == 1)
    def _():
        hw_next[...] = hw_ref[...]

    hz_both[core] = small_ref[0]
    right = split(c_both[1])
    u_left = split(mul(inverse, split(c_both[0, mine]), NT))
    arrived()

    def low_rows(first, count):
        span = slice(first, first + count)
        low_send[span] = -mul((right[0][span], right[1][span]), u_left)

    def described(source, target, index, device):
        return pltpu.make_async_remote_copy(
            src_ref=source,
            dst_ref=target,
            send_sem=send_sems.at[index],
            recv_sem=recv_sems.at[index],
            device_id=device,
            device_id_type=MESH,
        )

    low_rows(DIRECT, N - DIRECT)
    around = lambda chunk: low_send.at[pl.ds(DIRECT + chunk * CHUNK, CHUNK)]
    first_hop = lambda chunk, source: described(source, hops.at[0, chunk], 10 + chunk, left_chip)
    turn = lambda chunk: described(around(chunk), hops.at[3, chunk], 19 + chunk, row_after)

    @pl.when(place_x == ROW - 1)
    def _():
        for chunk in range(CHUNKS):
            turn(chunk).start()

    @pl.when(place_x != ROW - 1)
    def _():
        for chunk in range(CHUNKS):
            first_hop(chunk, around(chunk)).start()

    lows = []

    def straight(index, first, count):
        span = pl.ds(first, count)
        low_rows(first, count)
        lows.append(remote(low_send.at[span], low_came.at[span], pair, 3 + index, after))

    straight(0, 0, HALF)
    swap_n = remote(lower.at[:N], n_ref.at[:, mine], pair, 23, partner)
    u_right = split(mul(inverse, split(c_both[1, mine]), NT))

    def diag_block(place):
        c_rows = split(c_both[1, place])
        return hw_next[place] + mul(c_rows, u_right)

    crossing = lambda: described(diag_send.at[HALF:], diag_came.at[HALF:], 1, after)
    handing = lambda: described(diag_came.at[HALF:], cross_came, 22, partner)
    half_of_own = lambda: described(hw_own.at[:, HALF:], hw_came, 24, partner)

    @pl.when(core == 0)
    def _():
        diag_send[HALF:] = diag_block(slice(HALF, N))
        crossing().start()

    diag_send[:HALF] = diag_block(mine)
    square = [
        remote(diag_send.at[span, width], diag_came.at[span, width], pair, index, after)
        for index, span, width in (
            (2, slice(QUARTER, HALF), slice(0, HALF)),
            (9, slice(0, QUARTER), slice(0, QUARTER)),
        )
    ]
    straight(1, HALF, DIRECT - HALF)

    @pl.when(place_x == ROW - 1)
    def _():
        for chunk in range(CHUNKS):
            turn(chunk).wait_recv()
            first_hop(chunk, hops.at[3, chunk]).start()

    copies[0].wait()
    z2 = mul(split(f2[...] - (small_ref[1] + hz_both[2])), inverse)
    z2_parts = split(z2)
    rhs_send[...] = hz_both[1] + mul(z2_parts, right, NT)
    rhs_sent = remote(rhs_send, rhs_came, pair, 5, after)

    copies[1].wait()
    copies[2].wait()
    swap_n.wait_recv()
    n = split(n_ref[...])
    y = split(y_ref[...])
    y_back[...] = mul(y, n)
    later = remote(y_back, y_next, pair, 0, before)

    steps = {(0, chunk): first_hop(chunk, around(chunk)) for chunk in range(CHUNKS)}

    def forward(hop, chunk):
        steps[hop, chunk].wait_recv()
        steps[hop + 1, chunk] = remote(
            hops.at[hop, chunk], hops.at[hop + 1, chunk], pair,
            10 + CHUNKS * (hop + 1) + chunk, left_chip,
        )

    forward(0, 0)
    copies[3].wait()
    left = split(c_both[0])
    diag_ref[...] = d0[...] - mul(left, u_left)

    @pl.when(core == 0)
    def _():
        hw_own[...] = mul(split(first_inverse[...]), split(h_ref[...]))

    forward(0, 1)

    @pl.when(core == 0)
    def _():
        hw_own[...] = mul(split(ht_ref[...]), split(hw_own[...]))
        half_of_own().start()
        hw_came[...] = hw_own[:, :HALF]

    forward(0, 2)
    later.wait_recv()

    @pl.when(core == 0)
    def _():
        y_send[...] = y_next[...]
        ys_ref[0] = y_ref[...]

    @pl.when(core == 1)
    def _():
        y_send[...] = y_ref[...]
        ys_ref[0] = y_next[...]

    swap_y = remote(y_send, ys_ref.at[1], pair, 6, partner)
    known = mul(y, left) + mul(split(y_next[...]), right)
    x2_ref[0] = z2 - mul(split(known), inverse)
    swap_x2 = remote(x2_ref.at[0], x2_ref.at[1], pair, 7, partner)
    copies[4].wait()
    rhs_ref[...] = f0[...] - hz_both[0] - mul(z2_parts, left, NT)
    forward(1, 0)

    @pl.when(core == 1)
    def _():
        half_of_own().wait_recv()

    diag_ref[...] = diag_ref[...] - hw_came[...]
    swap_y.wait_recv()
    swap_x2.wait_recv()

    @pl.when(core == 0)
    def _():
        for slot in range(2):
            ys_ref[slot] = mul(split(ys_ref[slot]), split(h_ref[...]), NT)

    forward(1, 1)
    v, w = split(v_ref[...]), split(first_inverse[...])
    for slot, place in ((1, rest), (0, share)):
        x_ref[slot] = (
            z_ref[place] - mul(split(ys_ref[slot]), w) - mul(split(x2_ref[slot]), v, NT)
        )
        if slot == 1:
            swap_x = remote(x_ref.at[1], x_both, pair, 8, partner)
    solution_ref[:, :N] = y_ref[...]
    solution_ref[:, 2 * N : 3 * N] = x2_ref[0]
    forward(1, 2)

    @pl.when(core == 0)
    def _():
        crossing().wait_recv()
        handing().start()

    for copy in square:
        copy.wait_recv()
    diag_came[:QUARTER, QUARTER:HALF] = diag_came[QUARTER:HALF, :QUARTER].T
    swap_corner = remote(diag_came.at[:HALF], corner_came, pair, 25, partner)

    swap_x.wait_recv()

    @pl.when(core == 0)
    def _():
        solution_ref[:, N : 2 * N] = x_ref[0]
        solution_ref[:, 3 * N :] = x_both[...]

    @pl.when(core == 1)
    def _():
        solution_ref[:, N : 2 * N] = x_both[...]
        solution_ref[:, 3 * N :] = x_ref[0]

    m_ref[mine, mine] = diag_came[:HALF]
    swap_corner.wait_recv()
    m_ref[other, other] = corner_came[...]

    @pl.when(core == 0)
    def _():
        m_ref[HALF:, :HALF] = diag_came[HALF:]

    @pl.when(core == 1)
    def _():
        handing().wait_recv()
        m_ref[HALF:, :HALF] = cross_came[...]

    m_ref[:HALF, HALF:] = m_ref[HALF:, :HALF].T
    applied = split(mul(split(m_ref[...]), split(n_ref[mine]), NT))
    diag_ref[...] = diag_ref[...] - mul(n, applied)
    lows[0].wait_recv()
    low_out[...] = mul(split(n_ref[:, :HALF]), split(low_came[:HALF]))
    rhs_sent.wait_recv()
    rhs_ref[...] = rhs_ref[...] - mul(split(rhs_came[...]), n, NT)
    lows[1].wait_recv()
    for chunk in range(CHUNKS):
        steps[2, chunk].wait_recv()
        low_came[pl.ds(DIRECT + chunk * CHUNK, CHUNK)] = hops[2, chunk]

    low_out[...] = low_out[...] + mul(split(n_ref[:, HALF:]), split(low_came[HALF:]))
    for copy in (
        later, *square, *lows, rhs_sent, swap_y, swap_x2, swap_x, swap_n, swap_corner,
        *steps.values(),
    ):
        copy.wait_send()

    @pl.when(place_x == ROW - 1)
    def _():
        for chunk in range(CHUNKS):
            turn(chunk).wait_send()

    @pl.when(core == 0)
    def _():
        crossing().wait_send()
        handing().wait_send()
        half_of_own().wait_send()


def deliver(*refs):
    count = (len(refs) - 1) // 2
    for copy in loads(refs[-1], *zip(refs[:count], refs[count : 2 * count])):
        copy.wait()


def shape(*dims):
    return jax.ShapeDtypeStruct(dims, f32)


def call(body, in_specs, outs, out_specs, scratch, flops, args, limit, **params):
    size = sum(a.size for a in args) + sum(o.size for o in outs)
    return pl.pallas_call(
        body,
        out_shape=outs,
        in_specs=in_specs,
        out_specs=out_specs,
        scratch_shapes=scratch,
        compiler_params=pltpu.CompilerParams(vmem_limit_bytes=limit << 20, **params),
        cost_estimate=pl.CostEstimate(flops=flops, bytes_accessed=4 * size, transcendentals=0),
    )(*args)


def newton_scratch():
    return [pltpu.VMEM((HALF, HALF), f32)] * 2 + [pltpu.VMEM((2, HALF, HALF), bf16)]


def copy_sems(count):
    return pltpu.SemaphoreType.DMA((count,))


def shards(diag, lower, right_side, coarse_sol):
    diag, lower, right_side, coarse_sol = (
        pltpu.with_memory_space_constraint(array, pltpu.HBM)
        for array in (diag, lower, right_side, coarse_sol)
    )
    swap = lambda x: lax.ppermute(x, "rhs", [(0, 1), (1, 0)])
    full, half, quarter = (N, N), (N, HALF), (HALF, HALF)
    small, scratch = (SHARE, N), lambda *dims: pltpu.VMEM(dims, f32)
    d_own, d_other, g, h, f, d2_own, first_x, first_t, gap = call(
        partners,
        [HBM] * 3,
        [shape(*half), shape(*quarter), shape(*full), shape(*full), shape(RHS, N), shape(*half),
         shape(*quarter), shape(*quarter), shape(8, 128)],
        [VMEM] * 9,
        [pltpu.VMEM((2, HALF, HALF), bf16), copy_sems(5), copy_sems(4), copy_sems(4)],
        2 * HALF**3 * 30,
        (diag, lower, right_side),
        16,
        collective_id=1,
        has_side_effects=True,
    )
    inverse, v, send, keep = call(
        level_one,
        [VMEM] * 7,
        [shape(*full), shape(*full), shape(N + HALF, HALF), shape(N + HALF, HALF)],
        [VMEM] * 4,
        [scratch(*full), scratch(*full)] + newton_scratch(),
        2 * N**3 * 20,
        (d_own, d_other, g, d2_own, first_x, first_t, gap),
        28,
    )
    came, ht, z, pack, hw, tails = call(
        outward,
        [VMEM] * 2 + [ANY] + [VMEM] * 2,
        [shape(N + HALF, HALF), shape(*full), shape(RHS, N), shape(3 * N + 2 * RHS, HALF),
         shape(*half), shape(2, *small)],
        [ANY] + [VMEM] * 5,
        [scratch(*full), scratch(RHS, N), copy_sems(1), copy_sems(1)],
        2 * N**3 * 6,
        (inverse, v, send, h, f),
        28,
        collective_id=3,
        has_side_effects=True,
    )
    pack_came = swap(pack)
    inverse2 = call(
        level_two,
        [VMEM] * 3,
        [shape(*full)],
        [VMEM],
        [scratch(*half)] + newton_scratch(),
        2 * N**3 * 20,
        (d2_own, keep, came),
        28,
    )[0]
    finals = [shape(*half), shape(*half), shape(*small), shape(SHARE, 4 * N)]
    results = call(
        survivors,
        [VMEM] * 10 + [HBM] * 4,
        finals,
        [VMEM] * 4,
        [scratch(2, *full), scratch(*half), scratch(3, *small), scratch(*half), scratch(*half),
         scratch(4, CHUNKS, CHUNK, HALF), scratch(*half), scratch(*small), scratch(*half),
         scratch(*quarter),
         scratch(*quarter), scratch(*full), scratch(*full), scratch(*full), scratch(*half),
         scratch(*small),
         scratch(*half), scratch(*small), scratch(*small), scratch(*small), scratch(*small),
         scratch(*small), scratch(*small), scratch(2, *small), scratch(2, *small),
         scratch(2, *small), scratch(*small),
         copy_sems(5), copy_sems(26), copy_sems(26)],
        2 * N**3 * 9,
        (inverse2, pack, pack_came, hw, tails, inverse, v, z, h, ht,
         diag, lower, right_side, coarse_sol),
        40,
        collective_id=2,
        has_side_effects=True,
    )
    return call(
        deliver, [ANY] * 4, finals, [HBM] * 4, [copy_sems(4)], 0, tuple(results), 8
    )


def solution(mesh):
    return jax.shard_map(
        shards,
        mesh=mesh,
        in_specs=(P("tm", "rhs"), P("tm", "rhs"), P("rhs", "tm"), P("rhs", "tm")),
        out_specs=(P("tm", "rhs"), P("tm", "rhs"), P("rhs", "tm"), P("rhs", "tm")),
        check_vma=False,
    )
```

```python
import functools

import jax
import jax.numpy as jnp
from jax import lax
from jax.experimental import pallas as pl
from jax.experimental.pallas import tpu as pltpu
from jax.sharding import PartitionSpec as P

f32, bf16 = jnp.float32, jnp.bfloat16
N = 512
HALF = 256
RHS = 128
SHARE = 64
QUARTER = 128
ROW = 4
DIRECT = 320
CHUNKS = 3
CHUNK = 64
LOWEST = 2.0
TOL = 2e-5
COARSE_TOL = 4e-3
NOISE = 2e-6
FIXED_STEPS = 4
MAX_STEPS = 40
VMEM = pl.BlockSpec(memory_space=pltpu.VMEM)
ANY = pl.BlockSpec(memory_space=pl.ANY)
HBM = pl.BlockSpec(memory_space=pltpu.HBM)
MESH = pl.DeviceIdType.MESH
NN = (((1,), (0,)), ((), ()))
NT = (((1,), (1,)), ((), ()))


def split(x):
    high = x.astype(bf16)
    return high, (x - high.astype(f32)).astype(bf16)


def mul(a, b, dims=NN):
    one = lambda p, q: lax.dot_general(p, q, dims, preferred_element_type=f32)
    return one(a[0], b[0]) + (one(a[0], b[1]) + one(a[1], b[0]))


def identity(n):
    return (
        lax.broadcasted_iota(jnp.int32, (n, n), 0) == lax.broadcasted_iota(jnp.int32, (n, n), 1)
    ).astype(f32)


def norm_steps(gap):
    gain = 2.0 / (2.0 - gap * gap)
    return gain, 0.5 * gain * gap * gap


def newton_start(block, x_ref, t_ref, d_ref):
    d_ref[0], d_ref[1] = split(block)
    top = jnp.maximum(jnp.max(jnp.sum(jnp.abs(block), axis=0, keepdims=True)), LOWEST)
    lead = 2.0 / (top + LOWEST)
    gain, gap = norm_steps((top - LOWEST) / (top + LOWEST))
    rest = 2.0 * identity(block.shape[0]) - lead * block
    x_ref[...] = (gain * lead) * rest
    t_ref[...] = (gain * lead) * mul((d_ref[0], d_ref[1]), split(rest))
    return gap


def newton_step(gap, x_ref, t_ref):
    gain, gap = norm_steps(gap)
    n = x_ref.shape[0]
    rest = split(2.0 * identity(n) - t_ref[...])
    both = mul(split(jnp.concatenate([t_ref[...], x_ref[...]], axis=0)), rest)
    t_ref[...] = gain * both[:n]
    x_ref[...] = gain * both[n:]
    return gap


def newton_finish(gap, x_ref, t_ref, d_ref, noise):
    def more(limit):
        return lambda state: jnp.logical_and(state[1] > limit, state[0] < MAX_STEPS)

    step = lambda state: (state[0] + 1, newton_step(state[1], x_ref, t_ref))
    _, gap = lax.while_loop(more(COARSE_TOL), step, (jnp.int32(0), gap))

    def correct(state):
        x = x_ref[...]
        x_parts = split(x)
        residual = identity(x.shape[0]) - mul((d_ref[0], d_ref[1]), x_parts)
        x_ref[...] = x + jnp.dot(x_parts[0], residual.astype(bf16), preferred_element_type=f32)
        return state[0] + 1, state[1] * state[1]

    lax.while_loop(more(TOL), correct, (jnp.int32(0), gap + noise))
    return x_ref[...]


def noise_of(block):
    return jnp.max(jnp.sum(jnp.abs(block), axis=0, keepdims=True)) * NOISE


def newton(block, x_ref, t_ref, d_ref):
    gap = newton_start(block, x_ref, t_ref, d_ref)
    return newton_finish(gap, x_ref, t_ref, d_ref, noise_of(block))


def places():
    core = lax.axis_index("rhs")
    return (
        core,
        pl.ds(pl.multiple_of(core * HALF, HALF), HALF),
        pl.ds(pl.multiple_of(HALF - core * HALF, HALF), HALF),
        pl.ds(pl.multiple_of(core * SHARE, SHARE), SHARE),
        pl.ds(pl.multiple_of(SHARE - core * SHARE, SHARE), SHARE),
    )


def invert(first, cross_block, last_block, out_ref, x_ref, t_ref, d_ref):
    _, mine, other, _, _ = places()
    cross = split(cross_block)
    lift = split(mul(cross, split(first)))
    out_ref[mine, mine] = first
    last = newton(last_block() - mul(lift, cross, NT), x_ref, t_ref, d_ref)
    low = -mul(split(last), lift)
    up = low.T
    out_ref[other, other] = last
    out_ref[other, mine] = low
    out_ref[mine, other] = up
    out_ref[mine, mine] = out_ref[mine, mine] - mul(split(up), lift)


def loads(sems, *pairs):
    copies = [
        pltpu.make_async_copy(source, target, sems.at[index])
        for index, (source, target) in enumerate(pairs)
    ]
    for copy in copies:
        copy.start()
    return copies


def rows(first, second, count=N):
    core = lax.axis_index("rhs")
    return pl.ds(pl.multiple_of(first + core * (second - first), HALF), count)


def remote(source, target, sems, index, device):
    copy = pltpu.make_async_remote_copy(
        src_ref=source,
        dst_ref=target,
        send_sem=sems[0].at[index],
        recv_sem=sems[1].at[index],
        device_id=device,
        device_id_type=MESH,
    )
    copy.start()
    return copy


def greet(*devices):
    barrier = pltpu.get_barrier_semaphore()
    for device in devices:
        pl.semaphore_signal(barrier, inc=1, device_id=device, device_id_type=MESH)
    return lambda: pl.semaphore_wait(barrier, len(devices))


def partners(
    diag, lower, right_side,
    d_own, d_other, g_ref, h_ref, f_ref, d2_own, x_ref, t_ref, gap_ref,
    d_ref, sems, send_sems, recv_sems,
):
    core, mine, other, share, rest = places()
    partner = {"rhs": 1 - core}
    arrived = greet(partner)
    section = rows(N, 3 * N)
    copies = loads(
        sems,
        (diag.at[section], d_own),
        (lower.at[rows(2 * N, 3 * N)], g_ref.at[:, mine]),
        (lower.at[N : 2 * N], h_ref.at[:, mine]),
        (right_side.at[:, section], f_ref.at[share]),
        (diag.at[2 * N : 3 * N], d2_own),
    )
    arrived()
    pair = (send_sems, recv_sems)
    swaps = [
        remote(source, target, pair, index, partner)
        for index, (source, target) in enumerate(
            (
                (diag.at[rows(3 * N, N + HALF, HALF)], d_other),
                (lower.at[rows(3 * N, 2 * N)], g_ref.at[:, mine]),
                (right_side.at[:, rows(3 * N, N)], f_ref.at[share]),
            )
        )
    ]

    def outer():
        return pltpu.make_async_remote_copy(
            src_ref=lower.at[N : 2 * N],
            dst_ref=h_ref.at[:, mine],
            send_sem=send_sems.at[3],
            recv_sem=recv_sems.at[3],
            device_id=partner,
            device_id_type=MESH,
        )

    @pl.when(core == 1)
    def _():
        outer().start()

    copies[0].wait()
    gap = newton_start(d_own[mine], x_ref, t_ref, d_ref)
    gap = lax.fori_loop(0, FIXED_STEPS, lambda _, gap: newton_step(gap, x_ref, t_ref), gap)
    gap_ref[...] = jnp.full(gap_ref.shape, gap, f32)
    for copy in copies[1:]:
        copy.wait()
    for copy in swaps:
        copy.wait()

    @pl.when(core == 0)
    def _():
        outer().wait_recv()

    @pl.when(core == 1)
    def _():
        outer().wait_send()


def level_one(
    d_own, d_other, g_whole, d2_own, first_x, first_t, gap_in,
    inverse_ref, v_ref, send_ref, keep_ref,
    gv_ref, g_ref, x_ref, t_ref, d_ref,
):
    core, mine, other, share, rest = places()
    x_ref[...] = first_x[...]
    t_ref[...] = first_t[...]
    block = d_own[mine]
    d_ref[0], d_ref[1] = split(block)
    first = newton_finish(jnp.max(gap_in[...]), x_ref, t_ref, d_ref, noise_of(block))
    invert(first, d_own[other], lambda: d_other[...], inverse_ref, x_ref, t_ref, d_ref)

    @pl.when(core == 0)
    def _():
        g_ref[...] = g_whole[...]

    @pl.when(core == 1)
    def _():
        g_ref[...] = g_whole[...].T

    g = split(g_ref[...])
    v = mul(split(inverse_ref[...]), g, NT)
    v_ref[...] = v
    gv_ref[...] = mul(g, split(v))
    send_ref[:N] = gv_ref[:, other]
    send_ref[N:] = gv_ref[mine, mine] - d2_own[mine]
    keep_ref[:N] = gv_ref[:, mine]
    keep_ref[N:] = gv_ref[other, other]


def outward(
    inverse_ref, v_ref, send_ref, h_ref, f_own,
    came_ref, ht_ref, z_ref, pack_ref, corner_ref, small_ref,
    c_ref, f_ref, send_sems, recv_sems,
):
    core, mine, other, share, rest = places()
    partner = {"rhs": 1 - core}
    greet(partner)()
    swapped = remote(send_ref, came_ref, (send_sems, recv_sems), 0, partner)
    v, inverse = split(v_ref[...]), split(inverse_ref[...])
    z = mul(split(f_own[...]), inverse)
    z_ref[...] = z

    def stack(place, first):
        small_ref[place] = f_ref[share]
        pack_ref[first : first + SHARE] = f_ref[rest, :HALF]
        pack_ref[first + SHARE : first + RHS] = f_ref[rest, HALF:]

    @pl.when(core == 0)
    def _():
        ht_ref[...] = h_ref[...].T
        c_ref[...] = -mul(split(ht_ref[...]), v)
        f_ref[...] = mul(split(z), split(h_ref[...]))

    @pl.when(core == 1)
    def _():
        c_ref[...] = -v_ref[...]
        corner_ref[...] = inverse_ref[:, mine]
        pack_ref[2 * N : 3 * N] = inverse_ref[:, other]
        f_ref[...] = z

    pack_ref[:N] = c_ref[:, :HALF]
    pack_ref[N : 2 * N] = c_ref[:, HALF:]
    stack(0, 3 * N)
    f_ref[...] = mul(split(f_own[...]), v)
    stack(1, 3 * N + RHS)
    swapped.wait()


def level_two(d2_own, keep_ref, came_ref, inverse_ref, d_own, x_ref, t_ref, d_ref):
    core, mine, other, share, rest = places()
    d_own[...] = d2_own[...] - (keep_ref[:N] + came_ref[:N])
    last_block = lambda: -(keep_ref[N:] + came_ref[N:])
    first = newton(d_own[mine], x_ref, t_ref, d_ref)
    invert(first, d_own[other], last_block, inverse_ref, x_ref, t_ref, d_ref)


def survivors(
    inverse_ref, own_ref, came_ref, hw_ref, small_ref, first_inverse, v_ref, z_ref, h_ref, ht_ref,
    diag, lower, right_side, coarse_sol,
    diag_ref, low_out, rhs_ref, solution_ref,
    c_both, hw_next, hz_both, low_send, low_came, hops, diag_send, rhs_send, diag_came, cross_came,
    corner_came, m_ref, n_ref, hw_own, hw_came, rhs_came,
    d0, f0, f2, y_ref, y_next, y_back, y_send, ys_ref, x2_ref, x_ref, x_both,
    sems, send_sems, recv_sems,
):
    core, mine, other, share, rest = places()
    me = lax.axis_index("tm")
    runs = lax.axis_size("tm")
    after, before = {"tm": lax.rem(me + 1, runs)}, {"tm": lax.rem(me + runs - 1, runs)}
    partner = {"rhs": 1 - core}
    place_x = lax.rem(me, ROW)
    first_x = me - place_x
    left_chip = {"tm": first_x + lax.rem(place_x + ROW - 1, ROW)}
    right_chip = {"tm": first_x + lax.rem(place_x + 1, ROW)}
    row_after = {"tm": lax.rem(me + ROW, runs)}
    row_before = {"tm": lax.rem(me + runs - ROW, runs)}
    arrived = greet(after, before, partner, left_chip, right_chip, row_after, row_before)
    copies = loads(
        sems,
        (right_side.at[:, 2 * N : 3 * N], f2),
        (lower.at[:N], n_ref.at[:, mine]),
        (coarse_sol, y_ref),
        (diag.at[:N], d0),
        (right_side.at[:, :N], f0),
    )
    pair = (send_sems, recv_sems)
    inverse = split(inverse_ref[...])
    for column in range(2):
        span = slice(column * HALF, (column + 1) * HALF)
        c_both[core, :, span] = own_ref[column * N : (column + 1) * N]
        c_both[1 - core, :, span] = came_ref[column * N : (column + 1) * N]
        first = 3 * N + column * SHARE
        hz_both[1 - core, :, span] = came_ref[first : first + SHARE]
        hz_both[2, :, span] = came_ref[first + RHS : first + RHS + SHARE]

    @pl.when(core == 0)
    def _():
        hw_next[...] = came_ref[2 * N : 3 * N]

    @pl.when(core == 1)
    def _():
        hw_next[...] = hw_ref[...]

    hz_both[core] = small_ref[0]
    right = split(c_both[1])
    u_right = split(mul(inverse, split(c_both[1, mine]), NT))
    arrived()
    swap_n = remote(lower.at[:N], n_ref.at[:, mine], pair, 23, partner)

    def diag_block(place):
        c_rows = split(c_both[1, place])
        return hw_next[place] + mul(c_rows, u_right)

    def described(source, target, index, device):
        return pltpu.make_async_remote_copy(
            src_ref=source,
            dst_ref=target,
            send_sem=send_sems.at[index],
            recv_sem=recv_sems.at[index],
            device_id=device,
            device_id_type=MESH,
        )

    crossing = lambda: described(diag_send.at[HALF:], diag_came.at[HALF:], 1, after)
    handing = lambda: described(diag_came.at[HALF:], cross_came, 22, partner)
    half_of_own = lambda: described(hw_own.at[:, HALF:], hw_came, 24, partner)
    around = lambda chunk: low_send.at[pl.ds(DIRECT + chunk * CHUNK, CHUNK)]
    first_hop = lambda chunk, source: described(source, hops.at[0, chunk], 10 + chunk, left_chip)
    turn = lambda chunk: described(around(chunk), hops.at[3, chunk], 19 + chunk, row_after)

    @pl.when(core == 0)
    def _():
        diag_send[HALF:] = diag_block(slice(HALF, N))
        crossing().start()

    diag_send[:HALF] = diag_block(mine)
    square = [
        remote(diag_send.at[span, width], diag_came.at[span, width], pair, index, after)
        for index, span, width in (
            (2, slice(QUARTER, HALF), slice(0, HALF)),
            (9, slice(0, QUARTER), slice(0, QUARTER)),
        )
    ]
    left = split(c_both[0])
    u_left = split(mul(inverse, split(c_both[0, mine]), NT))

    def low_rows(first, count):
        span = slice(first, first + count)
        low_send[span] = -mul((right[0][span], right[1][span]), u_left)

    low_rows(DIRECT, N - DIRECT)

    @pl.when(place_x == ROW - 1)
    def _():
        for chunk in range(CHUNKS):
            turn(chunk).start()

    @pl.when(place_x != ROW - 1)
    def _():
        for chunk in range(CHUNKS):
            first_hop(chunk, around(chunk)).start()

    steps = {(0, chunk): first_hop(chunk, around(chunk)) for chunk in range(CHUNKS)}
    lows = []
    for index, (first, count) in enumerate(((0, HALF), (HALF, DIRECT - HALF))):
        span = pl.ds(first, count)
        low_rows(first, count)
        lows.append(remote(low_send.at[span], low_came.at[span], pair, 3 + index, after))
    copies[0].wait()
    z2 = mul(split(f2[...] - (small_ref[1] + hz_both[2])), inverse)
    z2_parts = split(z2)
    rhs_send[...] = hz_both[1] + mul(z2_parts, right, NT)
    rhs_sent = remote(rhs_send, rhs_came, pair, 5, after)

    copies[1].wait()
    copies[2].wait()
    swap_n.wait_recv()
    n = split(n_ref[...])
    y = split(y_ref[...])
    y_back[...] = mul(y, n)
    later = remote(y_back, y_next, pair, 0, before)

    @pl.when(place_x == ROW - 1)
    def _():
        for chunk in range(CHUNKS):
            turn(chunk).wait_recv()
            first_hop(chunk, hops.at[3, chunk]).start()

    def forward(hop, chunk):
        steps[hop, chunk].wait_recv()
        steps[hop + 1, chunk] = remote(
            hops.at[hop, chunk], hops.at[hop + 1, chunk], pair,
            10 + CHUNKS * (hop + 1) + chunk, left_chip,
        )

    forward(0, 0)
    copies[3].wait()
    diag_ref[...] = d0[...] - mul(left, u_left)

    @pl.when(core == 0)
    def _():
        hw_own[...] = mul(split(first_inverse[...]), split(h_ref[...]))

    forward(0, 1)

    @pl.when(core == 0)
    def _():
        hw_own[...] = mul(split(ht_ref[...]), split(hw_own[...]))
        half_of_own().start()
        hw_came[...] = hw_own[:, :HALF]

    forward(0, 2)
    later.wait_recv()

    @pl.when(core == 0)
    def _():
        y_send[...] = y_next[...]
        ys_ref[0] = y_ref[...]

    @pl.when(core == 1)
    def _():
        y_send[...] = y_ref[...]
        ys_ref[0] = y_next[...]

    swap_y = remote(y_send, ys_ref.at[1], pair, 6, partner)
    known = mul(y, left) + mul(split(y_next[...]), right)
    x2_ref[0] = z2 - mul(split(known), inverse)
    swap_x2 = remote(x2_ref.at[0], x2_ref.at[1], pair, 7, partner)
    copies[4].wait()
    rhs_ref[...] = f0[...] - hz_both[0] - mul(z2_parts, left, NT)
    forward(1, 0)

    @pl.when(core == 1)
    def _():
        half_of_own().wait_recv()

    diag_ref[...] = diag_ref[...] - hw_came[...]
    swap_y.wait_recv()
    swap_x2.wait_recv()

    @pl.when(core == 0)
    def _():
        for slot in range(2):
            ys_ref[slot] = mul(split(ys_ref[slot]), split(h_ref[...]), NT)

    forward(1, 1)
    v, w = split(v_ref[...]), split(first_inverse[...])
    for slot, place in ((1, rest), (0, share)):
        x_ref[slot] = (
            z_ref[place] - mul(split(ys_ref[slot]), w) - mul(split(x2_ref[slot]), v, NT)
        )
        if slot == 1:
            swap_x = remote(x_ref.at[1], x_both, pair, 8, partner)
    solution_ref[:, :N] = y_ref[...]
    solution_ref[:, 2 * N : 3 * N] = x2_ref[0]
    forward(1, 2)

    @pl.when(core == 0)
    def _():
        crossing().wait_recv()
        handing().start()

    for copy in square:
        copy.wait_recv()
    diag_came[:QUARTER, QUARTER:HALF] = diag_came[QUARTER:HALF, :QUARTER].T
    swap_corner = remote(diag_came.at[:HALF], corner_came, pair, 25, partner)

    swap_x.wait_recv()

    @pl.when(core == 0)
    def _():
        solution_ref[:, N : 2 * N] = x_ref[0]
        solution_ref[:, 3 * N :] = x_both[...]

    @pl.when(core == 1)
    def _():
        solution_ref[:, N : 2 * N] = x_both[...]
        solution_ref[:, 3 * N :] = x_ref[0]

    m_ref[mine, mine] = diag_came[:HALF]
    swap_corner.wait_recv()
    m_ref[other, other] = corner_came[...]

    @pl.when(core == 0)
    def _():
        m_ref[HALF:, :HALF] = diag_came[HALF:]

    @pl.when(core == 1)
    def _():
        handing().wait_recv()
        m_ref[HALF:, :HALF] = cross_came[...]

    m_ref[:HALF, HALF:] = m_ref[HALF:, :HALF].T
    applied = split(mul(split(m_ref[...]), split(n_ref[mine]), NT))
    diag_ref[...] = diag_ref[...] - mul(n, applied)
    lows[0].wait_recv()
    low_out[...] = mul(split(n_ref[:, :HALF]), split(low_came[:HALF]))
    rhs_sent.wait_recv()
    rhs_ref[...] = rhs_ref[...] - mul(split(rhs_came[...]), n, NT)
    lows[1].wait_recv()
    for chunk in range(CHUNKS):
        steps[2, chunk].wait_recv()
        low_came[pl.ds(DIRECT + chunk * CHUNK, CHUNK)] = hops[2, chunk]

    low_out[...] = low_out[...] + mul(split(n_ref[:, HALF:]), split(low_came[HALF:]))
    for copy in (
        later, *square, *lows, rhs_sent, swap_y, swap_x2, swap_x, swap_n, swap_corner,
        *steps.values(),
    ):
        copy.wait_send()

    @pl.when(place_x == ROW - 1)
    def _():
        for chunk in range(CHUNKS):
            turn(chunk).wait_send()

    @pl.when(core == 0)
    def _():
        crossing().wait_send()
        handing().wait_send()
        half_of_own().wait_send()


def deliver(*refs):
    count = (len(refs) - 1) // 2
    for copy in loads(refs[-1], *zip(refs[:count], refs[count : 2 * count])):
        copy.wait()


def shape(*dims):
    return jax.ShapeDtypeStruct(dims, f32)


def call(body, in_specs, outs, out_specs, scratch, flops, args, limit, **params):
    size = sum(a.size for a in args) + sum(o.size for o in outs)
    return pl.pallas_call(
        body,
        out_shape=outs,
        in_specs=in_specs,
        out_specs=out_specs,
        scratch_shapes=scratch,
        compiler_params=pltpu.CompilerParams(vmem_limit_bytes=limit << 20, **params),
        cost_estimate=pl.CostEstimate(flops=flops, bytes_accessed=4 * size, transcendentals=0),
    )(*args)


def newton_scratch():
    return [pltpu.VMEM((HALF, HALF), f32)] * 2 + [pltpu.VMEM((2, HALF, HALF), bf16)]


def copy_sems(count):
    return pltpu.SemaphoreType.DMA((count,))


def shards(diag, lower, right_side, coarse_sol):
    diag, lower, right_side, coarse_sol = (
        pltpu.with_memory_space_constraint(array, pltpu.HBM)
        for array in (diag, lower, right_side, coarse_sol)
    )
    swap = lambda x: lax.ppermute(x, "rhs", [(0, 1), (1, 0)])
    full, half, quarter = (N, N), (N, HALF), (HALF, HALF)
    small, scratch = (SHARE, N), lambda *dims: pltpu.VMEM(dims, f32)
    d_own, d_other, g, h, f, d2_own, first_x, first_t, gap = call(
        partners,
        [HBM] * 3,
        [shape(*half), shape(*quarter), shape(*full), shape(*full), shape(RHS, N), shape(*half),
         shape(*quarter), shape(*quarter), shape(8, 128)],
        [VMEM] * 9,
        [pltpu.VMEM((2, HALF, HALF), bf16), copy_sems(5), copy_sems(4), copy_sems(4)],
        2 * HALF**3 * 30,
        (diag, lower, right_side),
        16,
        collective_id=1,
        has_side_effects=True,
    )
    inverse, v, send, keep = call(
        level_one,
        [VMEM] * 7,
        [shape(*full), shape(*full), shape(N + HALF, HALF), shape(N + HALF, HALF)],
        [VMEM] * 4,
        [scratch(*full), scratch(*full)] + newton_scratch(),
        2 * N**3 * 20,
        (d_own, d_other, g, d2_own, first_x, first_t, gap),
        28,
    )
    came, ht, z, pack, hw, tails = call(
        outward,
        [VMEM] * 2 + [ANY] + [VMEM] * 2,
        [shape(N + HALF, HALF), shape(*full), shape(RHS, N), shape(3 * N + 2 * RHS, HALF),
         shape(*half), shape(2, *small)],
        [ANY] + [VMEM] * 5,
        [scratch(*full), scratch(RHS, N), copy_sems(1), copy_sems(1)],
        2 * N**3 * 6,
        (inverse, v, send, h, f),
        28,
        collective_id=3,
        has_side_effects=True,
    )
    pack_came = swap(pack)
    inverse2 = call(
        level_two,
        [VMEM] * 3,
        [shape(*full)],
        [VMEM],
        [scratch(*half)] + newton_scratch(),
        2 * N**3 * 20,
        (d2_own, keep, came),
        28,
    )[0]
    finals = [shape(*half), shape(*half), shape(*small), shape(SHARE, 4 * N)]
    results = call(
        survivors,
        [VMEM] * 10 + [HBM] * 4,
        finals,
        [VMEM] * 4,
        [scratch(2, *full), scratch(*half), scratch(3, *small), scratch(*half), scratch(*half),
         scratch(4, CHUNKS, CHUNK, HALF), scratch(*half), scratch(*small), scratch(*half),
         scratch(*quarter),
         scratch(*quarter), scratch(*full), scratch(*full), scratch(*full), scratch(*half),
         scratch(*small),
         scratch(*half), scratch(*small), scratch(*small), scratch(*small), scratch(*small),
         scratch(*small), scratch(*small), scratch(2, *small), scratch(2, *small),
         scratch(2, *small), scratch(*small),
         copy_sems(5), copy_sems(26), copy_sems(26)],
        2 * N**3 * 9,
        (inverse2, pack, pack_came, hw, tails, inverse, v, z, h, ht,
         diag, lower, right_side, coarse_sol),
        40,
        collective_id=2,
        has_side_effects=True,
    )
    return call(
        deliver, [ANY] * 4, finals, [HBM] * 4, [copy_sems(4)], 0, tuple(results), 8
    )


def solution(mesh):
    return jax.shard_map(
        shards,
        mesh=mesh,
        in_specs=(P("tm", "rhs"), P("tm", "rhs"), P("rhs", "tm"), P("rhs", "tm")),
        out_specs=(P("tm", "rhs"), P("tm", "rhs"), P("rhs", "tm"), P("rhs", "tm")),
        check_vma=False,
    )
```
